32 devices in a mesh: feat: 4 (over y, x), ex: 8 (over z, core).
Axes of the slice: x: 2, y: 2, z: 4, core: 2. Of those that a mesh axis runs over, the one named last changes fastest.
Arguments:
- x_values: bfloat16 [8192, 8192], P('ex', 'feat'), may hold values from -6 to 9, as said below
- tile_live: int32 [64, 64], P('ex', 'feat'), may hold values from 0 to 1
- labels: int32 [8192], P('ex'), may hold values from 0 to 127
- margins: bfloat16 [8192, 128], P('ex'), may hold values from -6 to 240, as said below
- coef: float32 [2, 4096, 128], P(None, ('feat', 'ex')), may hold values from -1.2 to 1.2
- order: int32 [3, 4], P(None, 'feat'), may hold values from 0 to 1
Outputs:
- margins_out: float32 [8192, 128], P('ex')
- coef_out: float32 [2, 4096, 128], P(None, ('feat', 'ex'))
The draws below stay inside these ranges and needn't reach their ends.
Inputs may be any that keep to these rules, and one draw needn't show every extreme that they name: `x_values`: feature values lie within this range. `margins`: start scores lie within this range.
All inputs are finite; a program needn't handle non-finite values.
Results may differ from the reference program's by a relative error of at most 0.0015.
Values may be sent and summed in bfloat16 or wider, within the bound.
No kernel may reach another device: no remote copies, remote signals or barrier semaphores. Data moves between devices by JAX's collectives and lax.ppermute only.
A program may use at most 64 MiB of HBM per device.

```python
import jax
import jax.numpy as jnp
from jax import lax

C = 128
BLOCK = 1024
BLOCKS = 2
STEPS = 3
EXAMPLES = 8192
FEATURES = 8192
N_FEAT = 4


def common_labels(key):
    return jax.random.randint(jax.random.fold_in(key, 11), (EXAMPLES,), 0, C).astype(jnp.int32)


def draw_labels(key, part):
    return common_labels(key)


def draw_x_values(key, part):
    labels = common_labels(key)
    inner = jax.random.fold_in(key, 12)
    base = jnp.clip(jax.random.normal(inner, (EXAMPLES, FEATURES), jnp.float32), -5.5, 5.5)
    feature_class = jnp.arange(FEATURES, dtype=jnp.int32) % C
    match = (labels[:, None] == feature_class[None, :]).astype(jnp.float32)
    return (base + 3.0 * match).astype(jnp.bfloat16)


def draw_tile_live(key, part):
    level = jax.random.randint(jax.random.fold_in(key, 21), (EXAMPLES // 128, 1), 2, 9)
    coin = jax.random.randint(jax.random.fold_in(key, 22), (EXAMPLES // 128, FEATURES // 128), 0, 8)
    return (coin < level).astype(jnp.int32)


def draw_margins(key, part):
    base = jnp.clip(jax.random.normal(jax.random.fold_in(key, 31), (EXAMPLES, C), jnp.float32), -5.5, 5.5)
    return base.astype(jnp.bfloat16)


def with_ends(result, key, smallest, high):
    longest = result.shape.index(max(result.shape))
    spots = []
    for shift in (0, 1):
        where = [jax.random.randint(jax.random.fold_in(key, axis), (), 0, length) for axis, length in enumerate(result.shape)]
        where[longest] = (where[longest] + shift) % result.shape[longest]
        spots.append(tuple(where))
    return result.at[spots[0]].set(smallest).at[spots[1]].set(high)


def block_levels(key, extent, split, least, top_value):
    loudness = 1.0
    for axis_at, shards_of in split:
        draws = jax.random.uniform(jax.random.fold_in(jax.random.fold_in(key, 6), axis_at), (shards_of,), jnp.float32, least / len(split), top_value / len(split))
        loudness = loudness * jnp.repeat(jnp.exp(draws), extent[axis_at] // shards_of).reshape((-1,) + (1,) * (len(extent) - 1 - axis_at))
    return loudness


def gaussian(key, extent, deviation, most, cuts=(), kind=jnp.bfloat16):
    drawn = deviation * jax.random.normal(key, extent, jnp.float32)
    if cuts:
        drawn = drawn * block_levels(key, extent, cuts, -0.22, 0.18)
    return jnp.clip(drawn, -most, most).astype(kind)


def setup_inputs(seed: int = 0) -> dict:
    seeds = jax.random.split(jax.random.key(seed), 7)
    x_values = draw_x_values(jax.random.fold_in(seeds[6], 71), 0)
    tile_live = draw_tile_live(jax.random.fold_in(seeds[6], 71), 0)
    labels = draw_labels(jax.random.fold_in(seeds[6], 71), 0)
    margins = draw_margins(jax.random.fold_in(seeds[6], 71), 0)
    coef = gaussian(seeds[4], (BLOCKS, N_FEAT * BLOCK, C), 0.2, 1.2, ((1, 32),), jnp.float32)
    order = with_ends(jax.random.randint(seeds[5], (STEPS, N_FEAT), 0, BLOCKS), jax.random.fold_in(seeds[5], 1), 0, BLOCKS - 1).astype(jnp.int32)
    return dict(x_values=x_values, tile_live=tile_live, labels=labels, margins=margins, coef=coef, order=order)


ridge = 0.002
lasso = 0.005


def soft_parts(score, onehot):
    row_max = jnp.max(score, axis=1, keepdims=True)
    expo = jnp.exp(score - row_max)
    prob = expo / jnp.sum(expo, axis=1, keepdims=True)
    residual = (prob - onehot).astype(jnp.bfloat16)
    spread = (1.0 - jnp.sum(prob * prob, axis=1)).astype(jnp.bfloat16)
    return residual, spread


def proximal(old_rows, grad_sum, curv_sum, count):
    curv = curv_sum / count + ridge
    shifted = old_rows - (grad_sum / count) / curv[:, None]
    limit = (lasso / curv)[:, None]
    return shifted - jnp.clip(shifted, -limit, limit)


def reference(x_values, tile_live, labels, margins, coef, order):
    count = x_values.shape[0]
    groups = order.shape[1]
    score = margins.astype(jnp.float32)
    classes = jnp.arange(C, dtype=jnp.int32)
    onehot = (labels[:, None] == classes[None, :]).astype(jnp.float32)
    tiles = BLOCK // 128
    for step in range(STEPS):
        residual, spread = soft_parts(score, onehot)
        total = jnp.zeros(score.shape, jnp.float32)
        for group in range(groups):
            chosen = order[step, group].astype(jnp.int32)
            col_start = (chosen * BLOCK + group * BLOCKS * BLOCK).astype(jnp.int32)
            block_x = lax.dynamic_slice_in_dim(x_values, col_start, BLOCK, 1)
            tile_start = (chosen * tiles + group * BLOCKS * tiles).astype(jnp.int32)
            live_tiles = lax.dynamic_slice_in_dim(tile_live, tile_start, tiles, 1).astype(jnp.bfloat16)
            block_x = (block_x.reshape(count // 128, 128, tiles, 128) * live_tiles[:, None, :, None]).reshape(count, BLOCK)
            squares = block_x * block_x
            grad_sum = lax.dot_general(block_x, residual, (((0,), (0,)), ((), ())), preferred_element_type=jnp.float32)
            curv_sum = jnp.dot(spread, squares, preferred_element_type=jnp.float32)
            row_start = jnp.int32(group * BLOCK)
            old_rows = lax.dynamic_slice(coef, (chosen, row_start, jnp.int32(0)), (1, BLOCK, C))[0]
            new_rows = proximal(old_rows, grad_sum, curv_sum, count)
            coef = lax.dynamic_update_slice(coef, new_rows[None], (chosen, row_start, jnp.int32(0)))
            step_delta = (new_rows - old_rows).astype(jnp.bfloat16)
            total = total + jnp.dot(block_x, step_delta, preferred_element_type=jnp.float32)
        score = score + total
    return score, coef
```

```python
import functools

import jax
import jax.numpy as jnp
from jax import lax
from jax.experimental import pallas as pl
from jax.experimental.pallas import tpu as pltpu
from jax.sharding import PartitionSpec as P

C = 128
BLOCK = 1024
STEPS = 3
HALF = BLOCK // 2
TILE = 128
NB = HALF // TILE
ROWS = C + 8

ridge = 0.002
lasso = 0.005

F32 = jnp.float32
BF16 = jnp.bfloat16


def vmem(n):
    return [pl.BlockSpec(memory_space=pltpu.VMEM)] * n


def smem(n):
    return [pl.BlockSpec(memory_space=pltpu.SMEM)] * n


def call(body, outs, in_specs, name, flops=0, nbytes=0, **kw):
    return pl.pallas_call(
        body,
        out_shape=outs,
        in_specs=in_specs,
        out_specs=jax.tree.map(lambda _: pl.BlockSpec(memory_space=pltpu.VMEM), outs),
        name=name,
        cost_estimate=pl.CostEstimate(flops=flops, bytes_accessed=nbytes, transcendentals=0),
        **kw,
    )


def sds(shape, dtype):
    return jax.ShapeDtypeStruct(shape, dtype)


def prep_body(info_ref, live_ref, x_ref, out_ref, buf, sems):
    chosen, core = info_ref[0], info_ref[1]
    rows = out_ref.shape[0]
    tiles = BLOCK // TILE

    def copy(r):
        return pltpu.make_async_copy(
            x_ref.at[pl.ds(r * TILE, TILE), pl.ds(pl.multiple_of(chosen * BLOCK, BLOCK), BLOCK)],
            buf.at[pl.ds(r * TILE, TILE)],
            sems.at[r],
        )

    for r in range(rows // TILE):
        copy(r).start()
    for r in range(rows // TILE):
        copy(r).wait()
        here = pl.ds(r * TILE, TILE)
        for k in range(tiles):
            col = 2 * (k % NB) + (core if k < NB else 1 - core)
            live = live_ref[r, chosen * tiles + col].astype(F32)
            tile = buf[here, pl.ds(pl.multiple_of(col * TILE, TILE), TILE)]
            out_ref[here, k * TILE : (k + 1) * TILE] = (tile.astype(F32) * live).astype(BF16)


def prep(x_values, tile_live, chosen, core):
    rows = x_values.shape[0]
    info = jnp.stack([chosen, core])
    return call(
        prep_body,
        sds((rows, BLOCK), BF16),
        smem(2) + [pl.BlockSpec(memory_space=pl.ANY)],
        "prep",
        nbytes=4 * rows * BLOCK,
        scratch_shapes=[
            pltpu.VMEM((rows, BLOCK), BF16),
            pltpu.SemaphoreType.DMA((rows // TILE,)),
        ],
    )(info, tile_live, x_values)


def prep_general(x_values, tile_live, chosen, core, own):
    rows = x_values.shape[0]
    tiles = BLOCK // TILE
    x = lax.dynamic_slice_in_dim(x_values, chosen * BLOCK, BLOCK, 1)
    live = lax.dynamic_slice_in_dim(tile_live, chosen * tiles, tiles, 1).astype(BF16)
    x = x.reshape(rows // TILE, TILE, tiles, TILE) * live[:, None, :, None]
    x = x.reshape(rows, HALF // own, 2, own)
    mine = lax.dynamic_index_in_dim(x, core, 2, keepdims=False)
    other = lax.dynamic_index_in_dim(x, 1 - core, 2, keepdims=False)
    return jnp.concatenate([mine.reshape(rows, HALF), other.reshape(rows, HALF)], axis=1)


def half_sums(res_t, spread_ref, x_ref, first, g_ref):
    rows = x_ref.shape[0]
    grad = jnp.dot(res_t, x_ref[:, first : first + HALF], preferred_element_type=F32)
    row = lax.broadcasted_iota(jnp.int32, (8, TILE), 0)
    for k in range(NB):
        lanes = slice(first + k * TILE, first + (k + 1) * TILE)
        acc = jnp.zeros((8, TILE), F32)
        for r in range(rows // TILE):
            here = slice(r * TILE, (r + 1) * TILE)
            x = x_ref[here, lanes].astype(F32)
            term = x * x * spread_ref[here, :]
            acc = acc + jnp.sum(term.reshape(TILE // 8, 8, TILE), axis=0)
        total = jnp.sum(acc, axis=0, keepdims=True)
        g_ref[k, 0:C, :] = grad[:, k * TILE : (k + 1) * TILE]
        g_ref[k, C:ROWS, :] = jnp.where(row == 0, total, 0.0)


def soft_tile(score, labels):
    top = jnp.max(score, axis=1, keepdims=True)
    expo = jnp.exp(score - top)
    prob = expo / jnp.sum(expo, axis=1, keepdims=True)
    label_col = jnp.broadcast_to(labels.astype(F32), (TILE, TILE)).T
    classes = lax.broadcasted_iota(jnp.int32, (TILE, C), 1).astype(F32)
    residual = prob - jnp.where(label_col == classes, 1.0, 0.0)
    spread = (1.0 - jnp.sum(prob * prob, axis=1, keepdims=True)).astype(BF16).astype(F32)
    return residual.T.astype(BF16), jnp.broadcast_to(spread, (TILE, TILE))


def first_body(margins_ref, lab_ref, x_ref, res_ref, spread_ref, g_ref):
    for r in range(margins_ref.shape[0] // TILE):
        here = slice(r * TILE, (r + 1) * TILE)
        res_t, spread = soft_tile(margins_ref[here, :].astype(F32), lab_ref[r : r + 1, :])
        res_ref[:, here] = res_t
        spread_ref[here, :] = spread
    half_sums(res_ref[...], spread_ref, x_ref, HALF, g_ref)


def next_body(score_ref, a_ref, ra_ref, b_ref, rb_ref, lab_ref, x_ref, new_ref, res_ref, spread_ref, g_ref):
    rows = score_ref.shape[0]
    for r in range(rows // TILE):
        here = slice(r * TILE, (r + 1) * TILE)
        if 2 * r * TILE < rows:
            part, got, at = a_ref, ra_ref, here
        else:
            part, got = b_ref, rb_ref
            at = slice(r * TILE - rows // 2, (r + 1) * TILE - rows // 2)
        change = part[at, :].astype(F32) + got[at, :].astype(F32)
        score = score_ref[here, :].astype(F32) + change
        new_ref[here, :] = score
        res_t, spread = soft_tile(score, lab_ref[r : r + 1, :])
        res_ref[:, here] = res_t
        spread_ref[here, :] = spread
    half_sums(res_ref[...], spread_ref, x_ref, HALF, g_ref)


def own_body(res_ref, spread_ref, x_ref, g_ref):
    half_sums(res_ref[...], spread_ref, x_ref, 0, g_ref)


def encode(k, grad, curv, out_ref):
    out_ref[k, 0:C, :] = grad.astype(BF16)
    high = curv.astype(BF16).astype(F32)
    low = curv - high
    row = lax.broadcasted_iota(jnp.int32, (8, TILE), 0)
    tail = jnp.where(row == 0, high, jnp.where(row == 1, low, 0.0))
    out_ref[k, C:ROWS, :] = tail.astype(BF16)


def pair_body(own_ref, got_ref, out_ref):
    for k in range(NB):
        total = own_ref[k] + got_ref[k]
        encode(k, total[0:C], total[C : C + 1], out_ref)


def decode_sum(k, mine_ref, got_ref):
    total = mine_ref[k].astype(F32) + got_ref[k].astype(F32)
    return total[0:C], total[C : C + 1] + total[C + 1 : C + 2]


def hop_body(mine_ref, got_ref, out_ref):
    for k in range(NB):
        encode(k, *decode_sum(k, mine_ref, got_ref), out_ref)


def prox_body(count, info_ref, mine_ref, got_ref, old_ref, new_ref, delta_ref):
    chosen, place = info_ref[0], info_ref[1]
    new_ref[1 - chosen] = old_ref[1 - chosen]
    for j in range(NB):
        k = jnp.bitwise_xor(place, j)
        grad, curv = decode_sum(k, mine_ref, got_ref)
        curv = curv / count + ridge
        old = old_ref[chosen, j]
        shifted = old - grad / count / curv
        limit = lasso / curv
        new = shifted - jnp.clip(shifted, -limit, limit)
        new_ref[chosen, j] = new
        delta_ref[k] = (new - old).astype(BF16)


def contrib_dot(x_ref, mine_ref, got_ref):
    delta = [mine_ref[k] for k in range(NB)] + [got_ref[k] for k in range(NB)]
    delta = jnp.concatenate(delta, axis=1)
    return lax.dot_general(
        x_ref[...], delta, (((1,), (1,)), ((), ())), preferred_element_type=F32
    )


def change_first_body(x_ref, mine_ref, got_ref, total_ref, a_ref, b_ref):
    part = contrib_dot(x_ref, mine_ref, got_ref)
    half = part.shape[0] // 2
    total_ref[...] = part
    a_ref[...] = part[:half].astype(BF16)
    b_ref[...] = part[half:].astype(BF16)


def change_next_body(x_ref, mine_ref, got_ref, before_ref, total_ref, a_ref, b_ref):
    part = contrib_dot(x_ref, mine_ref, got_ref)
    half = part.shape[0] // 2
    total_ref[...] = before_ref[...] + part
    a_ref[...] = part[:half].astype(BF16)
    b_ref[...] = part[half:].astype(BF16)


def change_last_body(x_ref, mine_ref, got_ref, before_ref, a_ref, b_ref):
    part = before_ref[...] + contrib_dot(x_ref, mine_ref, got_ref)
    half = part.shape[0] // 2
    a_ref[...] = part[:half]
    b_ref[...] = part[half:]


def flip(x, axis, bit):
    n = lax.axis_size(axis)
    return lax.ppermute(x, axis, [(i, i ^ bit) for i in range(n)])


def bits(n):
    return [1 << i for i in range(n.bit_length() - 1)]


def add_as(x, y, dtype):
    return (x.astype(F32) + y.astype(F32)).astype(dtype)


def spread_over_feat(a, b):
    order = bits(lax.axis_size("feat"))
    for n, (bit_a, bit_b) in enumerate(zip(order, reversed(order))):
        got_a, got_b = flip(a, "feat", bit_a), flip(b, "feat", bit_b)
        if n == len(order) - 1:
            return a, got_a, b, got_b
        a, b = add_as(a, got_a, a.dtype), add_as(b, got_b, b.dtype)


def local(x_values, tile_live, labels, margins, coef, order):
    rows = x_values.shape[0]
    n_ex = lax.axis_size("ex")
    count = float(rows * n_ex)
    own = coef.shape[1]
    me = lax.axis_index("ex")
    core, place = me % 2, me // 2
    aligned = own == TILE
    labels = labels.reshape(rows // TILE, TILE)
    z_bits = [2 * b for b in bits(n_ex // 2)]

    mine = jnp.swapaxes(coef, 1, 2)[:, None]
    if aligned:
        far = mine.astype(BF16)
        for bit in z_bits:
            far = jnp.concatenate([far, flip(far, "ex", bit)], axis=1)
        old = jnp.concatenate([mine, far[:, 1:].astype(F32)], axis=1)
    else:
        far = mine
        for bit in z_bits:
            far = jnp.concatenate([far, flip(far, "ex", bit)], axis=1)
        far = jnp.take(far, jnp.bitwise_xor(jnp.arange(n_ex // 2), place), axis=1)
        old = far.transpose(0, 2, 1, 3).reshape(2, C, NB, TILE).transpose(0, 2, 1, 3)

    g_shape = sds((NB, ROWS, TILE), F32)
    m_shape = sds((NB, ROWS, TILE), BF16)
    soft_shapes = (sds((C, rows), BF16), sds((rows, TILE), F32), g_shape)
    half_shape = (rows // 2, C)
    half_flops = 2 * rows * HALF * C
    score, total = margins, None
    for step in range(STEPS):
        chosen = order[step, 0]
        if aligned:
            x = prep(x_values, tile_live, chosen, core)
        else:
            x = prep_general(x_values, tile_live, chosen, core, own)
        if step == 0:
            res_t, spread, g_other = call(
                first_body, soft_shapes, vmem(3), "soft_first", half_flops, 1 << 20
            )(margins, labels, x)
        else:
            score, res_t, spread, g_other = call(
                next_body, (sds((rows, C), F32),) + soft_shapes, vmem(7), "soft_next", half_flops, 1 << 20
            )(score, a, got_a, b, got_b, labels, x)
        got = flip(g_other, "ex", 1)
        g_own = call(own_body, g_shape, vmem(3), "own", half_flops, 1 << 20)(res_t, spread, x)
        message = call(pair_body, m_shape, vmem(2), "pair")(g_own, got)
        for bit in z_bits[:-1]:
            got = flip(message, "ex", bit)
            message = call(hop_body, m_shape, vmem(2), "hop")(message, got)
        got = flip(message, "ex", z_bits[-1])
        info = jnp.stack([chosen, place if aligned else jnp.int32(0)])
        old, delta = call(
            functools.partial(prox_body, count),
            (sds(old.shape, F32), sds((NB, C, TILE), BF16)),
            smem(1) + vmem(3),
            "prox",
        )(info, message, got, old)
        got = flip(delta, "ex", 1)
        if step == 0:
            total, a, b = call(
                change_first_body,
                (sds((rows, C), F32), sds(half_shape, BF16), sds(half_shape, BF16)),
                vmem(3), "change_first", 2 * half_flops, 1 << 20,
            )(x, delta, got)
        elif step < STEPS - 1:
            total, a, b = call(
                change_next_body,
                (sds((rows, C), F32), sds(half_shape, BF16), sds(half_shape, BF16)),
                vmem(4), "change_next", 2 * half_flops, 1 << 20,
            )(x, delta, got, total)
        else:
            a, b = call(
                change_last_body,
                (sds(half_shape, F32), sds(half_shape, F32)),
                vmem(4), "change_last", 2 * half_flops, 1 << 20,
            )(x, delta, got, total)
        a, got_a, b, got_b = spread_over_feat(a, b)
    score = margins.astype(F32) + jnp.concatenate([a + got_a, b + got_b])
    if aligned:
        coef = old[:, 0]
    else:
        old = old.transpose(0, 2, 1, 3).reshape(2, C, HALF)
        coef = lax.dynamic_slice_in_dim(old, place * own, own, 2)
    return score, jnp.swapaxes(coef, 1, 2)


def solution(mesh):
    return jax.shard_map(
        local,
        mesh=mesh,
        in_specs=(
            P("ex", "feat"),
            P("ex", "feat"),
            P("ex"),
            P("ex", None),
            P(None, ("feat", "ex"), None),
            P(None, "feat"),
        ),
        out_specs=(P("ex", None), P(None, ("feat", "ex"), None)),
        check_vma=False,
    )
```

```python
import functools

import jax
import jax.numpy as jnp
from jax import lax
from jax.experimental import pallas as pl
from jax.experimental.pallas import tpu as pltpu
from jax.sharding import PartitionSpec as P

C = 128
BLOCK = 1024
STEPS = 3
HALF = BLOCK // 2
TILE = 128
NB = HALF // TILE
ROWS = C + 8

ridge = 0.002
lasso = 0.005

F32 = jnp.float32
BF16 = jnp.bfloat16


def vmem(n):
    return [pl.BlockSpec(memory_space=pltpu.VMEM)] * n


def smem(n):
    return [pl.BlockSpec(memory_space=pltpu.SMEM)] * n


def call(body, outs, in_specs, name, flops=0, nbytes=0, **kw):
    f = pl.pallas_call(
        body,
        out_shape=outs,
        in_specs=in_specs,
        out_specs=jax.tree.map(lambda _: pl.BlockSpec(memory_space=pltpu.VMEM), outs),
        name=name,
        cost_estimate=pl.CostEstimate(flops=flops, bytes_accessed=nbytes, transcendentals=0),
        compiler_params=pltpu.CompilerParams(vmem_limit_bytes=16 << 20),
        **kw,
    )

    def run(*args):
        return f(
            *(
                pltpu.with_memory_space_constraint(x, pltpu.VMEM)
                if spec.memory_space == pltpu.VMEM
                else x
                for spec, x in zip(in_specs, args, strict=True)
            )
        )

    return run


def sds(shape, dtype):
    return pltpu.VMEM(shape, dtype)


def prep_body(step, order_ref, live_ref, x_ref, out_ref, buf, sems):
    chosen, core = order_ref[step, 0], lax.axis_index("ex") % 2
    rows = out_ref.shape[0]
    tiles = BLOCK // TILE

    def copy(r):
        return pltpu.make_async_copy(
            x_ref.at[pl.ds(r * TILE, TILE), pl.ds(pl.multiple_of(chosen * BLOCK, BLOCK), BLOCK)],
            buf.at[pl.ds(r * TILE, TILE)],
            sems.at[r],
        )

    for r in range(rows // TILE):
        copy(r).start()
    for r in range(rows // TILE):
        copy(r).wait()
        here = pl.ds(r * TILE, TILE)
        for k in range(tiles):
            col = 2 * (k % NB) + (core if k < NB else 1 - core)
            live = live_ref[r, chosen * tiles + col].astype(F32)
            tile = buf[here, pl.ds(pl.multiple_of(col * TILE, TILE), TILE)]
            out_ref[here, k * TILE : (k + 1) * TILE] = (tile.astype(F32) * live).astype(BF16)


def prep(x_values, tile_live, order, step):
    rows = x_values.shape[0]
    return call(
        functools.partial(prep_body, step),
        sds((rows, BLOCK), BF16),
        smem(2) + [pl.BlockSpec(memory_space=pl.ANY)],
        "prep",
        nbytes=4 * rows * BLOCK,
        scratch_shapes=[
            pltpu.VMEM((rows, BLOCK), BF16),
            pltpu.SemaphoreType.DMA((rows // TILE,)),
        ],
    )(order, tile_live, x_values)


def prep_general(x_values, tile_live, chosen, core, own):
    rows = x_values.shape[0]
    tiles = BLOCK // TILE
    x = lax.dynamic_slice_in_dim(x_values, chosen * BLOCK, BLOCK, 1)
    live = lax.dynamic_slice_in_dim(tile_live, chosen * tiles, tiles, 1).astype(BF16)
    x = x.reshape(rows // TILE, TILE, tiles, TILE) * live[:, None, :, None]
    x = x.reshape(rows, HALF // own, 2, own)
    mine = lax.dynamic_index_in_dim(x, core, 2, keepdims=False)
    other = lax.dynamic_index_in_dim(x, 1 - core, 2, keepdims=False)
    return jnp.concatenate([mine.reshape(rows, HALF), other.reshape(rows, HALF)], axis=1)


def half_sums(res_t, spread_ref, x_ref, first, g_ref):
    rows = x_ref.shape[0]
    grad = jnp.dot(res_t, x_ref[:, first : first + HALF], preferred_element_type=F32)
    row = lax.broadcasted_iota(jnp.int32, (8, TILE), 0)
    for k in range(NB):
        lanes = slice(first + k * TILE, first + (k + 1) * TILE)
        acc = jnp.zeros((8, TILE), F32)
        for r in range(rows // TILE):
            here = slice(r * TILE, (r + 1) * TILE)
            x = x_ref[here, lanes].astype(F32)
            term = x * x * spread_ref[here, :]
            acc = acc + jnp.sum(term.reshape(TILE // 8, 8, TILE), axis=0)
        total = jnp.sum(acc, axis=0, keepdims=True)
        g_ref[k, 0:C, :] = grad[:, k * TILE : (k + 1) * TILE]
        g_ref[k, C:ROWS, :] = jnp.where(row == 0, total, 0.0)


def soft_tile(score, labels):
    top = jnp.max(score, axis=1, keepdims=True)
    expo = jnp.exp(score - top)
    prob = expo / jnp.sum(expo, axis=1, keepdims=True)
    label_col = jnp.broadcast_to(labels.astype(F32), (TILE, TILE)).T
    classes = lax.broadcasted_iota(jnp.int32, (TILE, C), 1).astype(F32)
    residual = prob - jnp.where(label_col == classes, 1.0, 0.0)
    spread = (1.0 - jnp.sum(prob * prob, axis=1, keepdims=True)).astype(BF16).astype(F32)
    return residual.T.astype(BF16), jnp.broadcast_to(spread, (TILE, TILE))


def first_body(margins_ref, lab_ref, x_ref, res_ref, spread_ref, g_ref):
    for r in range(margins_ref.shape[0] // TILE):
        here = slice(r * TILE, (r + 1) * TILE)
        res_t, spread = soft_tile(margins_ref[here, :].astype(F32), lab_ref[r : r + 1, :])
        res_ref[:, here] = res_t
        spread_ref[here, :] = spread
    half_sums(res_ref[...], spread_ref, x_ref, HALF, g_ref)


def next_body(score_ref, a_ref, ra_ref, b_ref, rb_ref, lab_ref, x_ref, new_ref, res_ref, spread_ref, g_ref):
    rows = score_ref.shape[0]
    for r in range(rows // TILE):
        here = slice(r * TILE, (r + 1) * TILE)
        if 2 * r * TILE < rows:
            part, got, at = a_ref, ra_ref, here
        else:
            part, got = b_ref, rb_ref
            at = slice(r * TILE - rows // 2, (r + 1) * TILE - rows // 2)
        change = part[at, :].astype(F32) + got[at, :].astype(F32)
        score = score_ref[here, :].astype(F32) + change
        new_ref[here, :] = score
        res_t, spread = soft_tile(score, lab_ref[r : r + 1, :])
        res_ref[:, here] = res_t
        spread_ref[here, :] = spread
    half_sums(res_ref[...], spread_ref, x_ref, HALF, g_ref)


def own_body(res_ref, spread_ref, x_ref, g_ref):
    half_sums(res_ref[...], spread_ref, x_ref, 0, g_ref)


def encode(k, grad, curv, out_ref):
    out_ref[k, 0:C, :] = grad.astype(BF16)
    high = curv.astype(BF16).astype(F32)
    low = curv - high
    row = lax.broadcasted_iota(jnp.int32, (8, TILE), 0)
    tail = jnp.where(row == 0, high, jnp.where(row == 1, low, 0.0))
    out_ref[k, C:ROWS, :] = tail.astype(BF16)


def pair_body(own_ref, got_ref, out_ref):
    for k in range(NB):
        total = own_ref[k] + got_ref[k]
        encode(k, total[0:C], total[C : C + 1], out_ref)


def decode_sum(k, mine_ref, got_ref):
    total = mine_ref[k].astype(F32) + got_ref[k].astype(F32)
    return total[0:C], total[C : C + 1] + total[C + 1 : C + 2]


def hop_body(mine_ref, got_ref, out_ref):
    for k in range(NB):
        encode(k, *decode_sum(k, mine_ref, got_ref), out_ref)


def prox_body(count, step, aligned, order_ref, mine_ref, got_ref, old_ref, new_ref, delta_ref):
    chosen = order_ref[step, 0]
    place = lax.axis_index("ex") // 2 if aligned else 0
    new_ref[1 - chosen] = old_ref[1 - chosen]
    for j in range(NB):
        k = jnp.bitwise_xor(place, j) if aligned else j
        grad, curv = decode_sum(k, mine_ref, got_ref)
        curv = curv / count + ridge
        old = old_ref[chosen, j]
        shifted = old - grad / count / curv
        limit = lasso / curv
        new = shifted - jnp.clip(shifted, -limit, limit)
        new_ref[chosen, j] = new
        delta_ref[k] = (new - old).astype(BF16)


def contrib_dot(x_ref, mine_ref, got_ref):
    delta = [mine_ref[k] for k in range(NB)] + [got_ref[k] for k in range(NB)]
    delta = jnp.concatenate(delta, axis=1)
    return lax.dot_general(
        x_ref[...], delta, (((1,), (1,)), ((), ())), preferred_element_type=F32
    )


def change_first_body(x_ref, mine_ref, got_ref, total_ref, a_ref, b_ref):
    part = contrib_dot(x_ref, mine_ref, got_ref)
    half = part.shape[0] // 2
    total_ref[...] = part
    a_ref[...] = part[:half].astype(BF16)
    b_ref[...] = part[half:].astype(BF16)


def change_next_body(x_ref, mine_ref, got_ref, before_ref, total_ref, a_ref, b_ref):
    part = contrib_dot(x_ref, mine_ref, got_ref)
    half = part.shape[0] // 2
    total_ref[...] = before_ref[...] + part
    a_ref[...] = part[:half].astype(BF16)
    b_ref[...] = part[half:].astype(BF16)


def change_last_body(x_ref, mine_ref, got_ref, before_ref, a_ref, b_ref):
    part = before_ref[...] + contrib_dot(x_ref, mine_ref, got_ref)
    half = part.shape[0] // 2
    a_ref[...] = part[:half]
    b_ref[...] = part[half:]


def flip(x, axis, bit):
    n = lax.axis_size(axis)
    return lax.ppermute(x, axis, [(i, i ^ bit) for i in range(n)])


def bits(n):
    return [1 << i for i in range(n.bit_length() - 1)]


def add_as(x, y, dtype):
    return (x.astype(F32) + y.astype(F32)).astype(dtype)


def spread_over_feat(a, b):
    order = bits(lax.axis_size("feat"))
    for n, (bit_a, bit_b) in enumerate(zip(order, reversed(order))):
        got_a, got_b = flip(a, "feat", bit_a), flip(b, "feat", bit_b)
        if n == len(order) - 1:
            return a, got_a, b, got_b
        a, b = add_as(a, got_a, a.dtype), add_as(b, got_b, b.dtype)


def local(x_values, tile_live, labels, margins, coef, order):
    rows = x_values.shape[0]
    n_ex = lax.axis_size("ex")
    count = float(rows * n_ex)
    own = coef.shape[1]
    me = lax.axis_index("ex")
    core, place = me % 2, me // 2
    aligned = own == TILE
    labels = labels.reshape(rows // TILE, TILE)
    z_bits = [2 * b for b in bits(n_ex // 2)]

    mine = jnp.swapaxes(coef, 1, 2)[:, None]
    if aligned:
        far = mine.astype(BF16)
        for bit in z_bits:
            far = jnp.concatenate([far, flip(far, "ex", bit)], axis=1)
        old = jnp.concatenate([mine, far[:, 1:].astype(F32)], axis=1)
    else:
        far = mine
        for bit in z_bits:
            far = jnp.concatenate([far, flip(far, "ex", bit)], axis=1)
        far = jnp.take(far, jnp.bitwise_xor(jnp.arange(n_ex // 2), place), axis=1)
        old = far.transpose(0, 2, 1, 3).reshape(2, C, NB, TILE).transpose(0, 2, 1, 3)

    g_shape = sds((NB, ROWS, TILE), F32)
    m_shape = sds((NB, ROWS, TILE), BF16)
    soft_shapes = (sds((C, rows), BF16), sds((rows, TILE), F32), g_shape)
    half_shape = (rows // 2, C)
    half_flops = 2 * rows * HALF * C
    score, total = margins, None
    for step in range(STEPS):
        chosen = order[step, 0]
        if aligned:
            x = prep(x_values, tile_live, order, step)
        else:
            x = prep_general(x_values, tile_live, chosen, core, own)
        if step == 0:
            res_t, spread, g_other = call(
                first_body, soft_shapes, vmem(3), "soft_first", half_flops, 1 << 20
            )(margins, labels, x)
        else:
            score, res_t, spread, g_other = call(
                next_body, (sds((rows, C), F32),) + soft_shapes, vmem(7), "soft_next", half_flops, 1 << 20
            )(score, a, got_a, b, got_b, labels, x)
        got = flip(g_other, "ex", 1)
        g_own = call(own_body, g_shape, vmem(3), "own", half_flops, 1 << 20)(res_t, spread, x)
        message = call(pair_body, m_shape, vmem(2), "pair")(g_own, got)
        for bit in z_bits[:-1]:
            got = flip(message, "ex", bit)
            message = call(hop_body, m_shape, vmem(2), "hop")(message, got)
        got = flip(message, "ex", z_bits[-1])
        old, delta = call(
            functools.partial(prox_body, count, step, aligned),
            (sds(old.shape, F32), sds((NB, C, TILE), BF16)),
            smem(1) + vmem(3),
            "prox",
        )(order, message, got, old)
        got = flip(delta, "ex", 1)
        if step == 0:
            total, a, b = call(
                change_first_body,
                (sds((rows, C), F32), sds(half_shape, BF16), sds(half_shape, BF16)),
                vmem(3), "change_first", 2 * half_flops, 1 << 20,
            )(x, delta, got)
        elif step < STEPS - 1:
            total, a, b = call(
                change_next_body,
                (sds((rows, C), F32), sds(half_shape, BF16), sds(half_shape, BF16)),
                vmem(4), "change_next", 2 * half_flops, 1 << 20,
            )(x, delta, got, total)
        else:
            a, b = call(
                change_last_body,
                (sds(half_shape, F32), sds(half_shape, F32)),
                vmem(4), "change_last", 2 * half_flops, 1 << 20,
            )(x, delta, got, total)
        a, got_a, b, got_b = spread_over_feat(a, b)
    score = margins.astype(F32) + jnp.concatenate([a + got_a, b + got_b])
    if aligned:
        coef = old[:, 0]
    else:
        old = old.transpose(0, 2, 1, 3).reshape(2, C, HALF)
        coef = lax.dynamic_slice_in_dim(old, place * own, own, 2)
    return score, jnp.swapaxes(coef, 1, 2)


def solution(mesh):
    return jax.shard_map(
        local,
        mesh=mesh,
        in_specs=(
            P("ex", "feat"),
            P("ex", "feat"),
            P("ex"),
            P("ex", None),
            P(None, ("feat", "ex"), None),
            P(None, "feat"),
        ),
        out_specs=(P("ex", None), P(None, ("feat", "ex"), None)),
        check_vma=False,
    )
```

```python
import functools

import jax
import jax.numpy as jnp
from jax import lax
from jax.experimental import pallas as pl
from jax.experimental.pallas import tpu as pltpu
from jax.sharding import PartitionSpec as P

C = 128
BLOCK = 1024
STEPS = 3
HALF = BLOCK // 2
TILE = 128
NB = HALF // TILE
PB = NB // 2
ROWS = C + 8

ridge = 0.002
lasso = 0.005

F32 = jnp.float32
BF16 = jnp.bfloat16


def vmem(n):
    return [pl.BlockSpec(memory_space=pltpu.VMEM)] * n


def smem(n):
    return [pl.BlockSpec(memory_space=pltpu.SMEM)] * n


def hbm(n):
    return [pl.BlockSpec(memory_space=pltpu.HBM)] * n


def call(body, outs, in_specs, name, flops=0, nbytes=0, **kw):
    f = pl.pallas_call(
        body,
        out_shape=outs,
        in_specs=in_specs,
        out_specs=jax.tree.map(lambda _: pl.BlockSpec(memory_space=pltpu.VMEM), outs),
        name=name,
        cost_estimate=pl.CostEstimate(flops=flops, bytes_accessed=nbytes, transcendentals=0),
        compiler_params=pltpu.CompilerParams(vmem_limit_bytes=16 << 20),
        **kw,
    )

    def run(*args):
        return f(
            *(
                x
                if spec.memory_space == pltpu.SMEM
                else pltpu.with_memory_space_constraint(x, spec.memory_space)
                for spec, x in zip(in_specs, args, strict=True)
            )
        )

    return run


def sds(shape, dtype):
    return pltpu.VMEM(shape, dtype)


def load_block(chosen, x_ref, buf, sems):
    copies = [
        pltpu.make_async_copy(
            x_ref.at[pl.ds(r * TILE, TILE), pl.ds(pl.multiple_of(chosen * BLOCK, BLOCK), BLOCK)],
            buf.at[pl.ds(r * TILE, TILE)],
            sems.at[r],
        )
        for r in range(buf.shape[0] // TILE)
    ]
    for copy in copies:
        copy.start()
    return copies


def mask_tile(r, chosen, core, live_ref, buf, out_ref):
    tiles = BLOCK // TILE
    here = pl.ds(r * TILE, TILE)
    for k in range(tiles):
        col = 2 * (k % NB) + (core if k < NB else 1 - core)
        live = live_ref[r, chosen * tiles + col].astype(F32)
        tile = buf[here, pl.ds(pl.multiple_of(col * TILE, TILE), TILE)]
        out_ref[here, k * TILE : (k + 1) * TILE] = (tile.astype(F32) * live).astype(BF16)


def prep_body(step, order_ref, live_ref, x_ref, out_ref, buf, sems):
    chosen, core = order_ref[0, step], lax.axis_index("ex") % 2
    copies = load_block(chosen, x_ref, buf, sems)
    for r, copy in enumerate(copies):
        copy.wait()
        mask_tile(r, chosen, core, live_ref, buf, out_ref)


def block_scratch(rows):
    return [pltpu.VMEM((rows, BLOCK), BF16), pltpu.SemaphoreType.DMA((rows // TILE,))]


def prep(order, tile_live, x_values, step):
    rows = x_values.shape[0]
    return call(
        functools.partial(prep_body, step),
        sds((rows, BLOCK), BF16),
        smem(2) + hbm(1),
        "prep",
        nbytes=4 * rows * BLOCK,
        scratch_shapes=block_scratch(rows),
    )(order, tile_live, x_values)


def prep_general(x_values, tile_live, chosen, core, own):
    rows = x_values.shape[0]
    tiles = BLOCK // TILE
    x = lax.dynamic_slice_in_dim(x_values, chosen * BLOCK, BLOCK, 1)
    live = lax.dynamic_slice_in_dim(tile_live, chosen * tiles, tiles, 1).astype(BF16)
    x = x.reshape(rows // TILE, TILE, tiles, TILE) * live[:, None, :, None]
    x = x.reshape(rows, HALF // own, 2, own)
    mine = lax.dynamic_index_in_dim(x, core, 2, keepdims=False)
    other = lax.dynamic_index_in_dim(x, 1 - core, 2, keepdims=False)
    return jnp.concatenate([mine.reshape(rows, HALF), other.reshape(rows, HALF)], axis=1)


def half_sums(res_t, spread_ref, x_ref, first, *g_refs):
    rows = x_ref.shape[0]
    row = lax.broadcasted_iota(jnp.int32, (8, TILE), 0)
    for n, g_ref in enumerate(g_refs):
        lane = first + n * PB * TILE
        grad = jnp.dot(res_t, x_ref[:, lane : lane + PB * TILE], preferred_element_type=F32)
        for k in range(PB):
            lanes = slice(lane + k * TILE, lane + (k + 1) * TILE)
            acc = jnp.zeros((8, TILE), F32)
            for r in range(rows // TILE):
                here = slice(r * TILE, (r + 1) * TILE)
                x = x_ref[here, lanes].astype(F32)
                term = x * x * spread_ref[here, :]
                acc = acc + jnp.sum(term.reshape(TILE // 8, 8, TILE), axis=0)
            total = jnp.sum(acc, axis=0, keepdims=True)
            g_ref[k, 0:C, :] = grad[:, k * TILE : (k + 1) * TILE]
            g_ref[k, C:ROWS, :] = jnp.where(row == 0, total, 0.0)


def soft_tile(score, labels):
    top = jnp.max(score, axis=1, keepdims=True)
    expo = jnp.exp(score - top)
    prob = expo / jnp.sum(expo, axis=1, keepdims=True)
    label_col = jnp.broadcast_to(labels.astype(F32), (TILE, TILE)).T
    classes = lax.broadcasted_iota(jnp.int32, (TILE, C), 1).astype(F32)
    residual = prob - jnp.where(label_col == classes, 1.0, 0.0)
    spread = (1.0 - jnp.sum(prob * prob, axis=1, keepdims=True)).astype(BF16).astype(F32)
    return residual.T.astype(BF16), jnp.broadcast_to(spread, (TILE, TILE))


def soft_rows(score, lab_ref, r, res_ref, spread_ref):
    here = slice(r * TILE, (r + 1) * TILE)
    res_t, spread = soft_tile(score, lab_ref[r : r + 1, :])
    res_ref[:, here] = res_t
    spread_ref[here, :] = spread


def first_body(order_ref, live_ref, margins_ref, lab_ref, x_ref, out_ref, res_ref, spread_ref, p_ref, q_ref, buf, sems):
    chosen, core = order_ref[0, 0], lax.axis_index("ex") % 2
    copies = load_block(chosen, x_ref, buf, sems)
    for r in range(len(copies)):
        score = margins_ref[r * TILE : (r + 1) * TILE, :].astype(F32)
        soft_rows(score, lab_ref, r, res_ref, spread_ref)
    for r, copy in enumerate(copies):
        copy.wait()
        mask_tile(r, chosen, core, live_ref, buf, out_ref)
    half_sums(res_ref[...], spread_ref, out_ref, HALF, p_ref, q_ref)


def first_general_body(margins_ref, lab_ref, x_ref, res_ref, spread_ref, p_ref, q_ref):
    for r in range(margins_ref.shape[0] // TILE):
        score = margins_ref[r * TILE : (r + 1) * TILE, :].astype(F32)
        soft_rows(score, lab_ref, r, res_ref, spread_ref)
    half_sums(res_ref[...], spread_ref, x_ref, HALF, p_ref, q_ref)


def next_body(score_ref, a_ref, ra_ref, b_ref, rb_ref, lab_ref, x_ref, new_ref, res_ref, spread_ref, p_ref, q_ref):
    rows = score_ref.shape[0]
    for r in range(rows // TILE):
        here = slice(r * TILE, (r + 1) * TILE)
        if 2 * r * TILE < rows:
            part, got, at = a_ref, ra_ref, here
        else:
            part, got = b_ref, rb_ref
            at = slice(r * TILE - rows // 2, (r + 1) * TILE - rows // 2)
        change = part[at, :].astype(F32) + got[at, :].astype(F32)
        score = score_ref[here, :].astype(F32) + change
        new_ref[here, :] = score
        soft_rows(score, lab_ref, r, res_ref, spread_ref)
    half_sums(res_ref[...], spread_ref, x_ref, HALF, p_ref, q_ref)


def own_body(res_ref, spread_ref, x_ref, p_ref, q_ref):
    half_sums(res_ref[...], spread_ref, x_ref, 0, p_ref, q_ref)


def encode(k, grad, curv, out_ref):
    out_ref[k, 0:C, :] = grad.astype(BF16)
    high = curv.astype(BF16).astype(F32)
    low = curv - high
    row = lax.broadcasted_iota(jnp.int32, (8, TILE), 0)
    tail = jnp.where(row == 0, high, jnp.where(row == 1, low, 0.0))
    out_ref[k, C:ROWS, :] = tail.astype(BF16)


def pair_body(own_ref, got_ref, out_ref):
    for k in range(PB):
        total = own_ref[k] + got_ref[k]
        encode(k, total[0:C], total[C : C + 1], out_ref)


def pair_with_body(slot, order_ref, own_ref, got_ref, coef_ref, out_ref):
    pair_body(own_ref, got_ref, out_ref)
    block = order_ref[0, 0] if slot == 0 else 1 - order_ref[0, 0]
    out_ref[PB, 0:C, :] = coef_ref[block].T.astype(BF16)
    out_ref[PB, C:ROWS, :] = jnp.zeros((ROWS - C, TILE), BF16)


def decode_sum(k, mine_ref, got_ref):
    total = mine_ref[k].astype(F32) + got_ref[k].astype(F32)
    return total[0:C], total[C : C + 1] + total[C + 1 : C + 2]


def hop_body(mine_ref, got_ref, out_ref):
    for k in range(PB):
        encode(k, *decode_sum(k, mine_ref, got_ref), out_ref)


def hop_with_body(mine_ref, got_ref, out_ref):
    hop_body(mine_ref, got_ref, out_ref)
    out_ref[PB] = mine_ref[PB]
    out_ref[PB + 1] = got_ref[PB]


def place_body(slot, order_ref, mine_ref, got_ref, coef_ref, out_ref):
    place = lax.axis_index("ex") // 2
    block = order_ref[0, 0] if slot == 0 else 1 - order_ref[0, 0]
    out_ref[place] = coef_ref[block].T
    out_ref[jnp.bitwise_xor(place, 2)] = mine_ref[PB + 1, 0:C, :].astype(F32)
    out_ref[jnp.bitwise_xor(place, 1)] = got_ref[PB, 0:C, :].astype(F32)
    out_ref[jnp.bitwise_xor(place, 3)] = got_ref[PB + 1, 0:C, :].astype(F32)


def step_coef(count, k, mine_ref, got_ref, old):
    grad, curv = decode_sum(k, mine_ref, got_ref)
    inverse = 1.0 / (curv / count + ridge)
    shifted = old - grad * (inverse / count)
    limit = lasso * inverse
    return shifted - jnp.clip(shifted, -limit, limit)


def prox_first_body(count, first, mine_ref, got_ref, old_ref, new_ref, delta_ref):
    for k in range(PB):
        old = old_ref[first + k]
        new = step_coef(count, k, mine_ref, got_ref, old)
        new_ref[k] = new
        delta_ref[k] = (new - old).astype(BF16)


def prox_body(count, step, first, order_ref, mine_ref, got_ref, old0_ref, old1_ref, new0_ref, new1_ref, delta_ref):
    same = order_ref[0, step] == order_ref[0, 0]
    for k in range(PB):
        old0, old1 = old0_ref[k], old1_ref[first + k]
        old = jnp.where(same, old0, old1)
        new = step_coef(count, k, mine_ref, got_ref, old)
        new0_ref[k] = jnp.where(same, new, old0)
        new1_ref[k] = jnp.where(same, old1, new)
        delta_ref[k] = (new - old).astype(BF16)


def coef_body(order_ref, p0_ref, p1_ref, q0_ref, q1_ref, out_ref):
    place = lax.axis_index("ex") // 2
    block = order_ref[0, 0]

    @pl.when(place < PB)
    def _():
        out_ref[block] = p0_ref[place].T
        out_ref[1 - block] = p1_ref[place].T

    @pl.when(place >= PB)
    def _():
        out_ref[block] = q0_ref[place - PB].T
        out_ref[1 - block] = q1_ref[place - PB].T


def contrib_dot(x_ref, p_ref, q_ref, rp_ref, rq_ref):
    delta = [ref[k] for ref in (p_ref, q_ref, rp_ref, rq_ref) for k in range(PB)]
    delta = jnp.concatenate(delta, axis=1)
    return lax.dot_general(
        x_ref[...], delta, (((1,), (1,)), ((), ())), preferred_element_type=F32
    )


def change_first_body(x_ref, p_ref, q_ref, rp_ref, rq_ref, total_ref, a_ref, b_ref):
    part = contrib_dot(x_ref, p_ref, q_ref, rp_ref, rq_ref)
    half = part.shape[0] // 2
    total_ref[...] = part
    a_ref[...] = part[:half].astype(BF16)
    b_ref[...] = part[half:].astype(BF16)


def change_next_body(x_ref, p_ref, q_ref, rp_ref, rq_ref, before_ref, total_ref, a_ref, b_ref):
    part = contrib_dot(x_ref, p_ref, q_ref, rp_ref, rq_ref)
    half = part.shape[0] // 2
    total_ref[...] = before_ref[...] + part
    a_ref[...] = part[:half].astype(BF16)
    b_ref[...] = part[half:].astype(BF16)


def change_last_body(x_ref, p_ref, q_ref, rp_ref, rq_ref, before_ref, a_ref, b_ref):
    part = before_ref[...] + contrib_dot(x_ref, p_ref, q_ref, rp_ref, rq_ref)
    half = part.shape[0] // 2
    a_ref[...] = part[:half]
    b_ref[...] = part[half:]


def flip(x, axis, bit):
    n = lax.axis_size(axis)
    return lax.ppermute(x, axis, [(i, i ^ bit) for i in range(n)])


def bits(n):
    return [1 << i for i in range(n.bit_length() - 1)]


def add_as(x, y, dtype):
    return (x.astype(F32) + y.astype(F32)).astype(dtype)


def spread_over_feat(a, b):
    order = bits(lax.axis_size("feat"))
    for n, (bit_a, bit_b) in enumerate(zip(order, reversed(order))):
        got_a, got_b = flip(a, "feat", bit_a), flip(b, "feat", bit_b)
        if n == len(order) - 1:
            return a, got_a, b, got_b
        a, b = add_as(a, got_a, a.dtype), add_as(b, got_b, b.dtype)


def gather_blocks(coef, order, z_bits):
    n_z = 1 << len(z_bits)
    far = jnp.swapaxes(coef, 1, 2)[:, None]
    for bit in z_bits:
        far = jnp.concatenate([far, flip(far, "ex", bit)], axis=1)
    place = lax.axis_index("ex") // 2
    far = jnp.take(far, jnp.bitwise_xor(jnp.arange(n_z), place), axis=1)
    old = far.transpose(0, 2, 1, 3).reshape(2, C, NB, TILE).transpose(0, 2, 1, 3)
    block = order[0, 0]
    return [lax.dynamic_index_in_dim(old, i, 0, keepdims=False) for i in (block, 1 - block)]


def own_blocks(olds, order, own):
    place = lax.axis_index("ex") // 2
    rows = []
    for p, q in olds:
        old = jnp.concatenate([p, q]).transpose(1, 0, 2).reshape(C, HALF)
        rows.append(lax.dynamic_slice_in_dim(old, place * own, own, 1))
    first = order[0, 0] == 0
    both = [jnp.where(first, rows[0], rows[1]), jnp.where(first, rows[1], rows[0])]
    return jnp.swapaxes(jnp.stack(both), 1, 2)


def local(x_values, tile_live, labels, margins, coef, order):
    rows = x_values.shape[0]
    n_ex = lax.axis_size("ex")
    count = float(rows * n_ex)
    own = coef.shape[1]
    core = lax.axis_index("ex") % 2
    aligned = own == TILE and n_ex == 2 * NB
    labels = labels.reshape(rows // TILE, TILE)
    order = order.reshape(1, STEPS)
    z_bits = [2 * b for b in bits(n_ex // 2)]
    if not aligned:
        olds = gather_blocks(coef, order, z_bits)

    g_shape = sds((PB, ROWS, TILE), F32)
    x_shape = sds((rows, BLOCK), BF16)
    soft_shapes = (sds((C, rows), BF16), sds((rows, TILE), F32), g_shape, g_shape)
    half_shape = (rows // 2, C)
    old_shape, delta_shape = sds((PB, C, TILE), F32), sds((PB, C, TILE), BF16)
    half_flops = 2 * rows * HALF * C

    def message(n):
        return sds((PB + n, ROWS, TILE), BF16)

    score, total = margins, None
    for step in range(STEPS):
        if not aligned:
            x = prep_general(x_values, tile_live, order[0, step], core, own)
        elif step > 0:
            x = prep(order, tile_live, x_values, step)
        if step > 0:
            score, res_t, spread, other_p, other_q = call(
                next_body, (sds((rows, C), F32),) + soft_shapes, vmem(7), "soft_next", half_flops, 1 << 20
            )(score, a, got_a, b, got_b, labels, x)
        elif aligned:
            x, res_t, spread, other_p, other_q = call(
                first_body, (x_shape,) + soft_shapes, smem(2) + vmem(2) + hbm(1), "soft_first",
                half_flops, 1 << 20, scratch_shapes=block_scratch(rows),
            )(order, tile_live, margins, labels, x_values)
        else:
            res_t, spread, other_p, other_q = call(
                first_general_body, soft_shapes, vmem(3), "soft_first", half_flops, 1 << 20
            )(margins, labels, x)
        got_p, got_q = flip(other_p, "ex", 1), flip(other_q, "ex", 1)
        own_p, own_q = call(
            own_body, (g_shape, g_shape), vmem(3), "own", half_flops, 1 << 20
        )(res_t, spread, x)
        carry = aligned and step < 2
        p = call(pair_body, message(0), vmem(2), "pair_p")(own_p, got_p)
        if carry:
            q = call(
                functools.partial(pair_with_body, step), message(1), smem(1) + vmem(3), "pair_q"
            )(order, own_q, got_q, coef)
        else:
            q = call(pair_body, message(0), vmem(2), "pair_q")(own_q, got_q)
        for n, (bit_p, bit_q) in enumerate(zip(z_bits, reversed(z_bits))):
            got_p, got_q = flip(p, "ex", bit_p), flip(q, "ex", bit_q)
            if n < len(z_bits) - 1:
                p = call(hop_body, message(0), vmem(2), "hop_p")(p, got_p)
                q = call(
                    hop_with_body if carry else hop_body, message(2 if carry else 0), vmem(2), "hop_q"
                )(q, got_q)
        if carry:
            far = call(
                functools.partial(place_body, step), sds((NB, C, TILE), F32), smem(1) + vmem(3), "place"
            )(order, q, got_q, coef)
        elif not aligned and step < 2:
            far = olds[step]
        if step == 0:
            new_p, delta_p = call(
                functools.partial(prox_first_body, count, 0), (old_shape, delta_shape), vmem(3), "prox_p"
            )(p, got_p, far)
            new_q, delta_q = call(
                functools.partial(prox_first_body, count, PB), (old_shape, delta_shape), vmem(3), "prox_q"
            )(q, got_q, far)
        else:
            p1, q1, at = (far, far, PB) if step == 1 else (other_block_p, other_block_q, 0)
            new_p, other_block_p, delta_p = call(
                functools.partial(prox_body, count, step, 0),
                (old_shape, old_shape, delta_shape), smem(1) + vmem(4), "prox_p",
            )(order, p, got_p, new_p, p1)
            new_q, other_block_q, delta_q = call(
                functools.partial(prox_body, count, step, at),
                (old_shape, old_shape, delta_shape), smem(1) + vmem(4), "prox_q",
            )(order, q, got_q, new_q, q1)
        deltas = (delta_p, delta_q, flip(delta_p, "ex", 1), flip(delta_q, "ex", 1))
        if step == 0:
            total, a, b = call(
                change_first_body,
                (sds((rows, C), F32), sds(half_shape, BF16), sds(half_shape, BF16)),
                vmem(5), "change_first", 2 * half_flops, 1 << 20,
            )(x, *deltas)
        elif step < STEPS - 1:
            total, a, b = call(
                change_next_body,
                (sds((rows, C), F32), sds(half_shape, BF16), sds(half_shape, BF16)),
                vmem(6), "change_next", 2 * half_flops, 1 << 20,
            )(x, *deltas, total)
        else:
            a, b = call(
                change_last_body,
                (sds(half_shape, F32), sds(half_shape, F32)),
                vmem(6), "change_last", 2 * half_flops, 1 << 20,
            )(x, *deltas, total)
        a, got_a, b, got_b = spread_over_feat(a, b)
    score = margins.astype(F32) + jnp.concatenate([a + got_a, b + got_b])
    if aligned:
        coef = call(coef_body, sds(coef.shape, F32), smem(1) + vmem(4), "coef_out")(
            order, new_p, other_block_p, new_q, other_block_q
        )
    else:
        coef = own_blocks([(new_p, new_q), (other_block_p, other_block_q)], order, own)
    return score, coef


def solution(mesh):
    return jax.shard_map(
        local,
        mesh=mesh,
        in_specs=(
            P("ex", "feat"),
            P("ex", "feat"),
            P("ex"),
            P("ex", None),
            P(None, ("feat", "ex"), None),
            P(None, "feat"),
        ),
        out_specs=(P("ex", None), P(None, ("feat", "ex"), None)),
        check_vma=False,
    )
```

```python
import functools

import jax
import jax.numpy as jnp
from jax import lax
from jax.experimental import pallas as pl
from jax.experimental.pallas import tpu as pltpu
from jax.sharding import PartitionSpec as P

C = 128
BLOCK = 1024
STEPS = 3
HALF = BLOCK // 2
TILE = 128
NB = HALF // TILE
ROWS = C + 8

ridge = 0.002
lasso = 0.005

F32 = jnp.float32
BF16 = jnp.bfloat16


def vmem(n):
    return [pl.BlockSpec(memory_space=pltpu.VMEM)] * n


def smem(n):
    return [pl.BlockSpec(memory_space=pltpu.SMEM)] * n


def hbm(n):
    return [pl.BlockSpec(memory_space=pltpu.HBM)] * n


def call(body, outs, in_specs, name, flops=0, nbytes=0, **kw):
    f = pl.pallas_call(
        body,
        out_shape=outs,
        in_specs=in_specs,
        out_specs=jax.tree.map(lambda _: pl.BlockSpec(memory_space=pltpu.VMEM), outs),
        name=name,
        cost_estimate=pl.CostEstimate(flops=flops, bytes_accessed=nbytes, transcendentals=0),
        compiler_params=pltpu.CompilerParams(vmem_limit_bytes=16 << 20),
        **kw,
    )

    def run(*args):
        return f(
            *(
                x
                if spec.memory_space == pltpu.SMEM
                else pltpu.with_memory_space_constraint(x, spec.memory_space)
                for spec, x in zip(in_specs, args, strict=True)
            )
        )

    return run


def sds(shape, dtype):
    return pltpu.VMEM(shape, dtype)


def load_block(chosen, x_ref, buf, sems):
    copies = [
        pltpu.make_async_copy(
            x_ref.at[pl.ds(r * TILE, TILE), pl.ds(pl.multiple_of(chosen * BLOCK, BLOCK), BLOCK)],
            buf.at[pl.ds(r * TILE, TILE)],
            sems.at[r],
        )
        for r in range(buf.shape[0] // TILE)
    ]
    for copy in copies:
        copy.start()
    return copies


def mask_tile(r, chosen, core, live_ref, buf, out_ref):
    tiles = BLOCK // TILE
    here = pl.ds(r * TILE, TILE)
    for k in range(tiles):
        col = 2 * (k % NB) + (core if k < NB else 1 - core)
        live = live_ref[r, chosen * tiles + col].astype(F32)
        tile = buf[here, pl.ds(pl.multiple_of(col * TILE, TILE), TILE)]
        out_ref[here, k * TILE : (k + 1) * TILE] = (tile.astype(F32) * live).astype(BF16)


def prep_body(step, order_ref, live_ref, x_ref, out_ref, buf, sems):
    chosen, core = order_ref[0, step], lax.axis_index("ex") % 2
    copies = load_block(chosen, x_ref, buf, sems)
    for r, copy in enumerate(copies):
        copy.wait()
        mask_tile(r, chosen, core, live_ref, buf, out_ref)


def block_scratch(rows):
    return [pltpu.VMEM((rows, BLOCK), BF16), pltpu.SemaphoreType.DMA((rows // TILE,))]


def prep(order, tile_live, x_values, step):
    rows = x_values.shape[0]
    return call(
        functools.partial(prep_body, step),
        sds((rows, BLOCK), BF16),
        smem(2) + hbm(1),
        "prep",
        nbytes=4 * rows * BLOCK,
        scratch_shapes=block_scratch(rows),
    )(order, tile_live, x_values)


def prep_general(x_values, tile_live, chosen, core, own):
    rows = x_values.shape[0]
    tiles = BLOCK // TILE
    x = lax.dynamic_slice_in_dim(x_values, chosen * BLOCK, BLOCK, 1)
    live = lax.dynamic_slice_in_dim(tile_live, chosen * tiles, tiles, 1).astype(BF16)
    x = x.reshape(rows // TILE, TILE, tiles, TILE) * live[:, None, :, None]
    x = x.reshape(rows, HALF // own, 2, own)
    mine = lax.dynamic_index_in_dim(x, core, 2, keepdims=False)
    other = lax.dynamic_index_in_dim(x, 1 - core, 2, keepdims=False)
    return jnp.concatenate([mine.reshape(rows, HALF), other.reshape(rows, HALF)], axis=1)


def half_sums(res_t, spread_ref, x_ref, first, g_ref):
    rows = x_ref.shape[0]
    grad = jnp.dot(res_t, x_ref[:, first : first + HALF], preferred_element_type=F32)
    row = lax.broadcasted_iota(jnp.int32, (8, TILE), 0)
    for k in range(NB):
        lanes = slice(first + k * TILE, first + (k + 1) * TILE)
        acc = jnp.zeros((8, TILE), F32)
        for r in range(rows // TILE):
            here = slice(r * TILE, (r + 1) * TILE)
            x = x_ref[here, lanes].astype(F32)
            term = x * x * spread_ref[here, :]
            acc = acc + jnp.sum(term.reshape(TILE // 8, 8, TILE), axis=0)
        total = jnp.sum(acc, axis=0, keepdims=True)
        g_ref[k, 0:C, :] = grad[:, k * TILE : (k + 1) * TILE]
        g_ref[k, C:ROWS, :] = jnp.where(row == 0, total, 0.0)


def soft_rows(score, labels, here, res_ref, spread_ref):
    top = jnp.max(score, axis=0, keepdims=True)
    expo = jnp.exp(score - top)
    prob = expo / jnp.sum(expo, axis=0, keepdims=True)
    classes = lax.broadcasted_iota(jnp.int32, (C, TILE), 0)
    residual = prob - jnp.where(labels == classes, 1.0, 0.0)
    spread = (1.0 - jnp.sum(prob * prob, axis=0, keepdims=True)).astype(BF16).astype(F32)
    res_ref[:, here] = residual.astype(BF16)
    spread_ref[here, :] = jnp.broadcast_to(spread, (TILE, TILE)).T


def tiles_of(rows):
    return [(r, slice(r * TILE, (r + 1) * TILE)) for r in range(rows // TILE)]


def first_body(
    order_hbm, live_hbm, margins_hbm, lab_hbm, coef_hbm, x_hbm,
    x_ref, score_ref, res_ref, spread_ref, g_ref, first_ref, other_ref, *rest,
):
    same_refs = rest[: STEPS - 1]
    order, live, margins, labels, coef, small, buf, sems = rest[STEPS - 1 :]
    loads = [
        pltpu.make_async_copy(src, dst, small.at[i])
        for i, (src, dst) in enumerate(
            ((order_hbm, order), (live_hbm, live), (margins_hbm, margins), (lab_hbm, labels), (coef_hbm, coef))
        )
    ]
    for load in loads:
        load.start()
    loads[0].wait()
    chosen, core = order[0, 0], lax.axis_index("ex") % 2
    copies = load_block(chosen, x_hbm, buf, sems)
    for load in loads[1:]:
        load.wait()
    for r, here in tiles_of(margins.shape[0]):
        score = margins[here, :].astype(F32).T
        score_ref[:, here] = score
        soft_rows(score, labels[r : r + 1, :], here, res_ref, spread_ref)
    first_ref[...] = coef[chosen].T
    other_ref[...] = coef[1 - chosen].T
    for step, same_ref in enumerate(same_refs):
        same_ref[...] = jnp.full((8, TILE), (order[0, step + 1] == chosen).astype(F32))
    for r, copy in enumerate(copies):
        copy.wait()
        mask_tile(r, chosen, core, live, buf, x_ref)
    half_sums(res_ref[...], spread_ref, x_ref, HALF, g_ref)


def first_general_body(margins_ref, lab_ref, x_ref, score_ref, res_ref, spread_ref, g_ref):
    for r, here in tiles_of(margins_ref.shape[0]):
        score = margins_ref[here, :].astype(F32).T
        score_ref[:, here] = score
        soft_rows(score, lab_ref[r : r + 1, :], here, res_ref, spread_ref)
    half_sums(res_ref[...], spread_ref, x_ref, HALF, g_ref)


def next_body(before_ref, part_ref, got_ref, lab_ref, x_ref, score_ref, res_ref, spread_ref, g_ref):
    for r, here in tiles_of(before_ref.shape[1]):
        change = part_ref[:, here].astype(F32) + got_ref[:, here].astype(F32)
        score = before_ref[:, here] + change
        score_ref[:, here] = score
        soft_rows(score, lab_ref[r : r + 1, :], here, res_ref, spread_ref)
    half_sums(res_ref[...], spread_ref, x_ref, HALF, g_ref)


def own_body(res_ref, spread_ref, x_ref, g_ref):
    half_sums(res_ref[...], spread_ref, x_ref, 0, g_ref)


def encode(k, grad, curv, out_ref):
    out_ref[k, 0:C, :] = grad.astype(BF16)
    high = curv.astype(BF16).astype(F32)
    low = curv - high
    row = lax.broadcasted_iota(jnp.int32, (8, TILE), 0)
    tail = jnp.where(row == 0, high, jnp.where(row == 1, low, 0.0))
    out_ref[k, C:ROWS, :] = tail.astype(BF16)


def pair_body(own_ref, got_ref, out_ref):
    for k in range(NB):
        total = own_ref[k] + got_ref[k]
        encode(k, total[0:C], total[C : C + 1], out_ref)


def pair_with_body(own_ref, got_ref, coef_ref, out_ref):
    pair_body(own_ref, got_ref, out_ref)
    out_ref[NB, 0:C, :] = coef_ref[...].astype(BF16)
    out_ref[NB, C:ROWS, :] = jnp.zeros((ROWS - C, TILE), BF16)


def decode_sum(k, mine_ref, got_ref):
    total = mine_ref[k].astype(F32) + got_ref[k].astype(F32)
    return total[0:C], total[C : C + 1] + total[C + 1 : C + 2]


def hop_body(mine_ref, got_ref, out_ref):
    for k in range(NB):
        encode(k, *decode_sum(k, mine_ref, got_ref), out_ref)


def hop_with_body(mine_ref, got_ref, out_ref):
    hop_body(mine_ref, got_ref, out_ref)
    out_ref[NB] = mine_ref[NB]
    out_ref[NB + 1] = got_ref[NB]


def place_body(mine_ref, got_ref, coef_ref, out_ref):
    me = lax.axis_index("ex")
    place, first = me // 2, 1 + me % 2
    out_ref[place] = coef_ref[...]
    out_ref[jnp.bitwise_xor(place, first)] = mine_ref[NB + 1, 0:C, :].astype(F32)
    out_ref[jnp.bitwise_xor(place, 3 - first)] = got_ref[NB, 0:C, :].astype(F32)
    out_ref[jnp.bitwise_xor(place, 3)] = got_ref[NB + 1, 0:C, :].astype(F32)


def step_coef(count, k, mine_ref, got_ref, old):
    grad, curv = decode_sum(k, mine_ref, got_ref)
    inverse = 1.0 / (curv / count + ridge)
    shifted = old - grad * (inverse / count)
    limit = lasso * inverse
    return shifted - jnp.clip(shifted, -limit, limit)


def prox_first_body(count, mine_ref, got_ref, old_ref, new_ref, delta_ref):
    for k in range(NB):
        old = old_ref[k]
        new = step_coef(count, k, mine_ref, got_ref, old)
        new_ref[k] = new
        delta_ref[:, k * TILE : (k + 1) * TILE] = (new - old).astype(BF16)


def prox_body(count, same_ref, mine_ref, got_ref, old0_ref, old1_ref, new0_ref, new1_ref, delta_ref):
    same = jnp.broadcast_to(same_ref[0:1, :], (C, TILE)) > 0.5
    for k in range(NB):
        old0, old1 = old0_ref[k], old1_ref[k]
        old = jnp.where(same, old0, old1)
        new = step_coef(count, k, mine_ref, got_ref, old)
        new0_ref[k] = jnp.where(same, new, old0)
        new1_ref[k] = jnp.where(same, old1, new)
        delta_ref[:, k * TILE : (k + 1) * TILE] = (new - old).astype(BF16)


def coef_body(order_ref, first_ref, other_ref, out_ref):
    place = lax.axis_index("ex") // 2
    block = order_ref[0, 0]
    out_ref[block] = first_ref[place].T
    out_ref[1 - block] = other_ref[place].T


def contrib(x_ref, first, delta_ref):
    return lax.dot_general(
        x_ref[:, first : first + HALF], delta_ref[...],
        (((1,), (1,)), ((), ())), preferred_element_type=F32,
    )


def mine_body(x_ref, delta_ref, part_ref):
    part_ref[...] = contrib(x_ref, 0, delta_ref)


def change_first_body(x_ref, part_ref, delta_ref, total_ref, out_ref):
    total_ref[...] = part_ref[...] + contrib(x_ref, HALF, delta_ref)
    for _, here in tiles_of(x_ref.shape[0]):
        out_ref[:, here] = total_ref[here, :].T.astype(BF16)


def change_next_body(x_ref, part_ref, delta_ref, before_ref, total_ref, out_ref):
    part = part_ref[...] + contrib(x_ref, HALF, delta_ref)
    total_ref[...] = before_ref[...] + part
    for _, here in tiles_of(x_ref.shape[0]):
        out_ref[:, here] = part[here, :].T.astype(BF16)


def change_last_body(x_ref, part_ref, delta_ref, before_ref, out_ref):
    out_ref[...] = before_ref[...] + (part_ref[...] + contrib(x_ref, HALF, delta_ref))


def bits(n):
    return [1 << i for i in range(n.bit_length() - 1)]


def swap(x, move):
    n_feat, n_ex = lax.axis_size("feat"), lax.axis_size("ex")
    pairs = []
    for f in range(n_feat):
        for e in range(n_ex):
            to_f, to_e = move(f, e)
            pairs.append((f * n_ex + e, to_f * n_ex + to_e))
    return lax.ppermute(x, ("feat", "ex"), pairs)


def swap_core(x):
    return swap(x, lambda f, e: (f, e ^ 1))


def by_core(order, e, n):
    return order[n] if e % 2 == 0 else order[len(order) - 1 - n]


def add_as(x, y, dtype):
    return (x.astype(F32) + y.astype(F32)).astype(dtype)


def sum_over_feat(x):
    order = bits(lax.axis_size("feat"))
    for n in range(len(order)):
        got = swap(x, lambda f, e, n=n: (f ^ by_core(order, e, n), e))
        if n == len(order) - 1:
            return x, got
        x = add_as(x, got, x.dtype)


def gather_blocks(coef, order, z_bits):
    n_z = 1 << len(z_bits)
    far = jnp.swapaxes(coef, 1, 2)[:, None]
    for bit in z_bits:
        far = jnp.concatenate([far, swap(far, lambda f, e, bit=bit: (f, e ^ bit))], axis=1)
    place = lax.axis_index("ex") // 2
    far = jnp.take(far, jnp.bitwise_xor(jnp.arange(n_z), place), axis=1)
    old = far.transpose(0, 2, 1, 3).reshape(2, C, NB, TILE).transpose(0, 2, 1, 3)
    block = order[0, 0]
    return [lax.dynamic_index_in_dim(old, i, 0, keepdims=False) for i in (block, 1 - block)]


def own_blocks(olds, order, own):
    place = lax.axis_index("ex") // 2
    rows = []
    for old in olds:
        old = old.transpose(1, 0, 2).reshape(C, HALF)
        rows.append(lax.dynamic_slice_in_dim(old, place * own, own, 1))
    first = order[0, 0] == 0
    both = [jnp.where(first, rows[0], rows[1]), jnp.where(first, rows[1], rows[0])]
    return jnp.swapaxes(jnp.stack(both), 1, 2)


def local(x_values, tile_live, labels, margins, coef, order):
    rows = x_values.shape[0]
    n_ex = lax.axis_size("ex")
    count = float(rows * n_ex)
    own = coef.shape[1]
    core = lax.axis_index("ex") % 2
    aligned = own == TILE and n_ex == 2 * NB
    labels = labels.reshape(rows // TILE, TILE)
    order = order.reshape(1, STEPS)
    z_bits = [2 * b for b in bits(n_ex // 2)]

    x_shape = sds((rows, BLOCK), BF16)
    soft_shapes = (
        sds((C, rows), F32), sds((C, rows), BF16), sds((rows, TILE), F32), sds((NB, ROWS, TILE), F32),
    )
    g_shape = soft_shapes[-1]
    old_shape, delta_shape = sds((NB, C, TILE), F32), sds((C, HALF), BF16)
    total_shape, change_shape = sds((rows, C), F32), sds((C, rows), BF16)
    own_shape, same_shape = sds((C, TILE), F32), sds((8, TILE), F32)
    flops, nbytes = 2 * rows * HALF * C, 1 << 20

    def message(n):
        return sds((NB + n, ROWS, TILE), BF16)

    if aligned:
        x, score, res_t, spread, g_other, *rest = call(
            first_body,
            (x_shape,) + soft_shapes + (own_shape,) * 2 + (same_shape,) * (STEPS - 1),
            hbm(6), "soft_first", flops, nbytes,
            scratch_shapes=[
                pltpu.SMEM(order.shape, jnp.int32),
                pltpu.SMEM(tile_live.shape, jnp.int32),
                pltpu.VMEM(margins.shape, BF16),
                pltpu.VMEM(labels.shape, jnp.int32),
                pltpu.VMEM(coef.shape, F32),
                pltpu.SemaphoreType.DMA((5,)),
            ] + block_scratch(rows),
        )(order, tile_live, margins, labels, coef, x_values)
        blocks, same = rest[:2], rest[2:]
    else:
        x = prep_general(x_values, tile_live, order[0, 0], core, own)
        score, res_t, spread, g_other = call(
            first_general_body, soft_shapes, vmem(3), "soft_first", flops, nbytes
        )(margins, labels, x)
        blocks = gather_blocks(coef, order, z_bits)
        same = [
            jnp.full((8, TILE), (order[0, step] == order[0, 0]).astype(F32)) for step in range(1, STEPS)
        ]

    for step in range(STEPS):
        if step > 0:
            if aligned:
                x = prep(order, tile_live, x_values, step)
            else:
                x = prep_general(x_values, tile_live, order[0, step], core, own)
            score, res_t, spread, g_other = call(
                next_body, soft_shapes, vmem(5), "soft_next", flops, nbytes
            )(score, change, got, labels, x)
        got = swap_core(g_other)
        g_own = call(own_body, g_shape, vmem(3), "own", flops, nbytes)(res_t, spread, x)
        carry = aligned and step < 2
        if carry:
            m = call(pair_with_body, message(1), vmem(3), "pair")(g_own, got, blocks[step])
        else:
            m = call(pair_body, message(0), vmem(2), "pair")(g_own, got)
        for n in range(len(z_bits)):
            got = swap(m, lambda f, e, n=n: (f, e ^ by_core(z_bits, e, n)))
            if n < len(z_bits) - 1:
                body, extra = (hop_with_body, 2) if carry else (hop_body, 0)
                m = call(body, message(extra), vmem(2), "hop")(m, got)
        if step < 2:
            far = blocks[step]
            if aligned:
                far = call(place_body, old_shape, vmem(3), "place")(m, got, far)
        if step == 0:
            first, delta = call(
                functools.partial(prox_first_body, count), (old_shape, delta_shape), vmem(3), "prox"
            )(m, got, far)
        else:
            first, other, delta = call(
                functools.partial(prox_body, count), (old_shape, old_shape, delta_shape), vmem(5), "prox"
            )(same[step - 1], m, got, first, far if step == 1 else other)
        got = swap_core(delta)
        part = call(mine_body, total_shape, vmem(2), "mine", flops, nbytes)(x, delta)
        if step == 0:
            total, change = call(
                change_first_body, (total_shape, change_shape), vmem(3), "change", flops, nbytes
            )(x, part, got)
        elif step < STEPS - 1:
            total, change = call(
                change_next_body, (total_shape, change_shape), vmem(4), "change", flops, nbytes
            )(x, part, got, total)
        else:
            change = call(change_last_body, total_shape, vmem(4), "change", flops, nbytes)(
                x, part, got, total
            )
        change, got = sum_over_feat(change)
    score = margins.astype(F32) + (change + got)
    if aligned:
        coef = call(coef_body, sds(coef.shape, F32), smem(1) + vmem(2), "coef_out")(order, first, other)
    else:
        coef = own_blocks((first, other), order, own)
    return score, coef


def solution(mesh):
    return jax.shard_map(
        local,
        mesh=mesh,
        in_specs=(
            P("ex", "feat"),
            P("ex", "feat"),
            P("ex"),
            P("ex", None),
            P(None, ("feat", "ex"), None),
            P(None, "feat"),
        ),
        out_specs=(P("ex", None), P(None, ("feat", "ex"), None)),
        check_vma=False,
    )
```

```python
import functools

import jax
import jax.numpy as jnp
from jax import lax
from jax.experimental import pallas as pl
from jax.experimental.pallas import tpu as pltpu
from jax.sharding import PartitionSpec as P

C = 128
BLOCK = 1024
STEPS = 3
HALF = BLOCK // 2
TILE = 128
NB = HALF // TILE
PB = NB // 2
ROWS = C + 8

ridge = 0.002
lasso = 0.005

F32 = jnp.float32
BF16 = jnp.bfloat16


def vmem(n):
    return [pl.BlockSpec(memory_space=pltpu.VMEM)] * n


def smem(n):
    return [pl.BlockSpec(memory_space=pltpu.SMEM)] * n


def hbm(n):
    return [pl.BlockSpec(memory_space=pltpu.HBM)] * n


def call(body, outs, in_specs, name, flops=0, nbytes=0, **kw):
    f = pl.pallas_call(
        body,
        out_shape=outs,
        in_specs=in_specs,
        out_specs=jax.tree.map(lambda _: pl.BlockSpec(memory_space=pltpu.VMEM), outs),
        name=name,
        cost_estimate=pl.CostEstimate(flops=flops, bytes_accessed=nbytes, transcendentals=0),
        compiler_params=pltpu.CompilerParams(vmem_limit_bytes=16 << 20),
        **kw,
    )

    def run(*args):
        return f(
            *(
                x
                if spec.memory_space == pltpu.SMEM
                else pltpu.with_memory_space_constraint(x, spec.memory_space)
                for spec, x in zip(in_specs, args, strict=True)
            )
        )

    return run


def sds(shape, dtype):
    return pltpu.VMEM(shape, dtype)


def load_block(chosen, x_ref, buf, sems):
    copies = [
        pltpu.make_async_copy(
            x_ref.at[pl.ds(r * TILE, TILE), pl.ds(pl.multiple_of(chosen * BLOCK, BLOCK), BLOCK)],
            buf.at[pl.ds(r * TILE, TILE)],
            sems.at[r],
        )
        for r in range(buf.shape[0] // TILE)
    ]
    for copy in copies:
        copy.start()
    return copies


def mask_tile(r, chosen, core, live_ref, buf, out_ref):
    tiles = BLOCK // TILE
    here = pl.ds(r * TILE, TILE)
    for k in range(tiles):
        col = 2 * (k % NB) + (core if k < NB else 1 - core)
        live = live_ref[r, chosen * tiles + col].astype(F32)
        tile = buf[here, pl.ds(pl.multiple_of(col * TILE, TILE), TILE)]
        out_ref[here, k * TILE : (k + 1) * TILE] = (tile.astype(F32) * live).astype(BF16)


def prep_body(step, order_ref, live_ref, x_ref, out_ref, buf, sems):
    chosen, core = order_ref[0, step], lax.axis_index("ex") % 2
    copies = load_block(chosen, x_ref, buf, sems)
    for r, copy in enumerate(copies):
        copy.wait()
        mask_tile(r, chosen, core, live_ref, buf, out_ref)


def block_scratch(rows):
    return [pltpu.VMEM((rows, BLOCK), BF16), pltpu.SemaphoreType.DMA((rows // TILE,))]


def prep(order, tile_live, x_values, step):
    rows = x_values.shape[0]
    return call(
        functools.partial(prep_body, step),
        sds((rows, BLOCK), BF16),
        smem(2) + hbm(1),
        "prep",
        nbytes=4 * rows * BLOCK,
        scratch_shapes=block_scratch(rows),
    )(order, tile_live, x_values)


def prep_general(x_values, tile_live, chosen, core, own):
    rows = x_values.shape[0]
    tiles = BLOCK // TILE
    x = lax.dynamic_slice_in_dim(x_values, chosen * BLOCK, BLOCK, 1)
    live = lax.dynamic_slice_in_dim(tile_live, chosen * tiles, tiles, 1).astype(BF16)
    x = x.reshape(rows // TILE, TILE, tiles, TILE) * live[:, None, :, None]
    x = x.reshape(rows, HALF // own, 2, own)
    mine = lax.dynamic_index_in_dim(x, core, 2, keepdims=False)
    other = lax.dynamic_index_in_dim(x, 1 - core, 2, keepdims=False)
    return jnp.concatenate([mine.reshape(rows, HALF), other.reshape(rows, HALF)], axis=1)


def half_sums(res_t, spread_ref, x_ref, first, g_ref):
    rows = x_ref.shape[0]
    grad = jnp.dot(res_t, x_ref[:, first : first + HALF], preferred_element_type=F32)
    row = lax.broadcasted_iota(jnp.int32, (8, TILE), 0)
    for k in range(NB):
        lanes = slice(first + k * TILE, first + (k + 1) * TILE)
        acc = jnp.zeros((8, TILE), F32)
        for r in range(rows // TILE):
            here = slice(r * TILE, (r + 1) * TILE)
            x = x_ref[here, lanes].astype(F32)
            term = x * x * spread_ref[here, :]
            acc = acc + jnp.sum(term.reshape(TILE // 8, 8, TILE), axis=0)
        total = jnp.sum(acc, axis=0, keepdims=True)
        g_ref[k, 0:C, :] = grad[:, k * TILE : (k + 1) * TILE]
        g_ref[k, C:ROWS, :] = jnp.where(row == 0, total, 0.0)


def soft_rows(score, labels, here, res_ref, spread_ref):
    top = jnp.max(score, axis=0, keepdims=True)
    expo = jnp.exp(score - top)
    prob = expo / jnp.sum(expo, axis=0, keepdims=True)
    classes = lax.broadcasted_iota(jnp.int32, (C, TILE), 0)
    residual = prob - jnp.where(labels == classes, 1.0, 0.0)
    spread = (1.0 - jnp.sum(prob * prob, axis=0, keepdims=True)).astype(BF16).astype(F32)
    res_ref[:, here] = residual.astype(BF16)
    spread_ref[here, :] = jnp.broadcast_to(spread, (TILE, TILE)).T


def tiles_of(rows):
    return [(r, slice(r * TILE, (r + 1) * TILE)) for r in range(rows // TILE)]


def first_body(
    order_hbm, live_hbm, margins_hbm, lab_hbm, coef_hbm, x_hbm,
    x_ref, score_ref, res_ref, spread_ref, g_ref, first_ref, other_ref, *rest,
):
    same_refs = rest[: STEPS - 1]
    order, live, margins, labels, coef, small, buf, sems = rest[STEPS - 1 :]
    loads = [
        pltpu.make_async_copy(src, dst, small.at[i])
        for i, (src, dst) in enumerate(
            ((order_hbm, order), (live_hbm, live), (margins_hbm, margins), (lab_hbm, labels), (coef_hbm, coef))
        )
    ]
    for load in loads:
        load.start()
    loads[0].wait()
    chosen, core = order[0, 0], lax.axis_index("ex") % 2
    copies = load_block(chosen, x_hbm, buf, sems)
    for load in loads[1:]:
        load.wait()
    for r, here in tiles_of(margins.shape[0]):
        score = margins[here, :].astype(F32).T
        score_ref[:, here] = score
        soft_rows(score, labels[r : r + 1, :], here, res_ref, spread_ref)
    first_ref[...] = coef[chosen].T
    other_ref[...] = coef[1 - chosen].T
    for step, same_ref in enumerate(same_refs):
        same_ref[...] = jnp.full((8, TILE), (order[0, step + 1] == chosen).astype(F32))
    for r, copy in enumerate(copies):
        copy.wait()
        mask_tile(r, chosen, core, live, buf, x_ref)
    half_sums(res_ref[...], spread_ref, x_ref, HALF, g_ref)


def first_general_body(margins_ref, lab_ref, x_ref, score_ref, res_ref, spread_ref, g_ref):
    for r, here in tiles_of(margins_ref.shape[0]):
        score = margins_ref[here, :].astype(F32).T
        score_ref[:, here] = score
        soft_rows(score, lab_ref[r : r + 1, :], here, res_ref, spread_ref)
    half_sums(res_ref[...], spread_ref, x_ref, HALF, g_ref)


def next_body(before_ref, a_ref, ra_ref, b_ref, rb_ref, lab_ref, x_ref, score_ref, res_ref, spread_ref, g_ref):
    rows = before_ref.shape[1]
    for r, here in tiles_of(rows):
        score = before_ref[:, here] + change_tile(here, rows, a_ref, ra_ref, b_ref, rb_ref)
        score_ref[:, here] = score
        soft_rows(score, lab_ref[r : r + 1, :], here, res_ref, spread_ref)
    half_sums(res_ref[...], spread_ref, x_ref, HALF, g_ref)


def last_body(before_ref, a_ref, ra_ref, b_ref, rb_ref, out_ref):
    rows = before_ref.shape[1]
    for _, here in tiles_of(rows):
        score = before_ref[:, here] + change_tile(here, rows, a_ref, ra_ref, b_ref, rb_ref)
        out_ref[here, :] = score.T


def change_tile(here, rows, a_ref, ra_ref, b_ref, rb_ref):
    if here.stop <= rows // 2:
        return a_ref[:, here].astype(F32) + ra_ref[:, here].astype(F32)
    at = slice(here.start - rows // 2, here.stop - rows // 2)
    return b_ref[:, at].astype(F32) + rb_ref[:, at].astype(F32)


def own_body(res_ref, spread_ref, x_ref, g_ref):
    half_sums(res_ref[...], spread_ref, x_ref, 0, g_ref)


def encode(k, grad, curv, out_ref):
    out_ref[k, 0:C, :] = grad.astype(BF16)
    high = curv.astype(BF16).astype(F32)
    low = curv - high
    row = lax.broadcasted_iota(jnp.int32, (8, TILE), 0)
    tail = jnp.where(row == 0, high, jnp.where(row == 1, low, 0.0))
    out_ref[k, C:ROWS, :] = tail.astype(BF16)


def pair_body(own_ref, got_ref, p_ref, q_ref):
    for k in range(NB):
        total = own_ref[k] + got_ref[k]
        encode(k % PB, total[0:C], total[C : C + 1], p_ref if k < PB else q_ref)


def pair_with_body(own_ref, got_ref, coef_ref, p_ref, q_ref):
    pair_body(own_ref, got_ref, p_ref, q_ref)
    p_ref[PB, 0:C, :] = coef_ref[...].astype(BF16)
    p_ref[PB, C:ROWS, :] = jnp.zeros((ROWS - C, TILE), BF16)


def decode_sum(k, mine_ref, got_ref):
    total = mine_ref[k].astype(F32) + got_ref[k].astype(F32)
    return total[0:C], total[C : C + 1] + total[C + 1 : C + 2]


def hop_body(mine_ref, got_ref, out_ref):
    for k in range(PB):
        encode(k, *decode_sum(k, mine_ref, got_ref), out_ref)


def hop_with_body(mine_ref, got_ref, out_ref):
    hop_body(mine_ref, got_ref, out_ref)
    out_ref[PB] = mine_ref[PB]
    out_ref[PB + 1] = got_ref[PB]


def place_body(mine_ref, got_ref, coef_ref, out_ref):
    place = lax.axis_index("ex") // 2
    out_ref[place] = coef_ref[...]
    out_ref[jnp.bitwise_xor(place, 1)] = mine_ref[PB + 1, 0:C, :].astype(F32)
    out_ref[jnp.bitwise_xor(place, 2)] = got_ref[PB, 0:C, :].astype(F32)
    out_ref[jnp.bitwise_xor(place, 3)] = got_ref[PB + 1, 0:C, :].astype(F32)


def step_coef(count, k, mine_ref, got_ref, old):
    grad, curv = decode_sum(k, mine_ref, got_ref)
    inverse = 1.0 / (curv / count + ridge)
    shifted = old - grad * (inverse / count)
    limit = lasso * inverse
    return shifted - jnp.clip(shifted, -limit, limit)


def prox_first_body(count, p_ref, gp_ref, q_ref, gq_ref, old_ref, new_ref, delta_ref):
    for k in range(NB):
        old = old_ref[k]
        chunk = (p_ref, gp_ref) if k < PB else (q_ref, gq_ref)
        new = step_coef(count, k % PB, *chunk, old)
        new_ref[k] = new
        delta_ref[:, k * TILE : (k + 1) * TILE] = (new - old).astype(BF16)


def prox_body(count, same_ref, p_ref, gp_ref, q_ref, gq_ref, old0_ref, old1_ref, new0_ref, new1_ref, delta_ref):
    same = jnp.broadcast_to(same_ref[0:1, :], (C, TILE)) > 0.5
    for k in range(NB):
        old0, old1 = old0_ref[k], old1_ref[k]
        old = jnp.where(same, old0, old1)
        chunk = (p_ref, gp_ref) if k < PB else (q_ref, gq_ref)
        new = step_coef(count, k % PB, *chunk, old)
        new0_ref[k] = jnp.where(same, new, old0)
        new1_ref[k] = jnp.where(same, old1, new)
        delta_ref[:, k * TILE : (k + 1) * TILE] = (new - old).astype(BF16)


def coef_body(order_ref, first_ref, other_ref, out_ref):
    place = lax.axis_index("ex") // 2
    block = order_ref[0, 0]
    out_ref[block] = first_ref[place].T
    out_ref[1 - block] = other_ref[place].T


def contrib(x_ref, first, delta_ref):
    return lax.dot_general(
        x_ref[:, first : first + HALF], delta_ref[...],
        (((1,), (1,)), ((), ())), preferred_element_type=F32,
    )


def mine_body(x_ref, delta_ref, part_ref):
    part_ref[...] = contrib(x_ref, 0, delta_ref)


def change_body(carried, x_ref, part_ref, delta_ref, *refs):
    errors, (a_ref, b_ref, ea_ref, eb_ref) = refs[:carried], refs[carried:]
    part = part_ref[...] + contrib(x_ref, HALF, delta_ref)
    rows = x_ref.shape[0]
    for _, here in tiles_of(rows):
        low = here.stop <= rows // 2
        at = here if low else slice(here.start - rows // 2, here.stop - rows // 2)
        full = part[here, :].T
        for e_ref in errors[0::2] if low else errors[1::2]:
            full = full + e_ref[:, at]
        sent = full.astype(BF16)
        (a_ref if low else b_ref)[:, at] = sent
        (ea_ref if low else eb_ref)[:, at] = full - sent.astype(F32)


def meet_body(share, mine_ref, got_ref, out_ref, error_ref):
    total = mine_ref[...].astype(F32) + got_ref[...].astype(F32)
    sent = total.astype(BF16)
    out_ref[...] = sent
    error_ref[...] = share * (total - sent.astype(F32))


def bits(n):
    return [1 << i for i in range(n.bit_length() - 1)]


def swap(x, move):
    n_feat, n_ex = lax.axis_size("feat"), lax.axis_size("ex")
    pairs = []
    for f in range(n_feat):
        for e in range(n_ex):
            to_f, to_e = move(f, e)
            pairs.append((f * n_ex + e, to_f * n_ex + to_e))
    return lax.ppermute(x, ("feat", "ex"), pairs)


def swap_core(x):
    return swap(x, lambda f, e: (f, e ^ 1))


def sum_over_feat(a, b):
    order = bits(lax.axis_size("feat"))
    errors, pair = [], 1
    for n in range(len(order)):
        got_a = swap(a, lambda f, e, n=n: (f ^ order[n], e))
        got_b = swap(b, lambda f, e, n=n: (f ^ order[-1 - n], e))
        if n == len(order) - 1:
            return (a, got_a, b, got_b), errors
        pair *= 2
        shapes = (sds(a.shape, BF16), sds(a.shape, F32))
        meet = functools.partial(meet_body, 1.0 / pair)
        a, ea = call(meet, shapes, vmem(2), "meet_a")(a, got_a)
        b, eb = call(meet, shapes, vmem(2), "meet_b")(b, got_b)
        errors += [ea, eb]


def gather_blocks(coef, order, z_bits):
    n_z = 1 << len(z_bits)
    far = jnp.swapaxes(coef, 1, 2)[:, None]
    for bit in z_bits:
        far = jnp.concatenate([far, swap(far, lambda f, e, bit=bit: (f, e ^ bit))], axis=1)
    place = lax.axis_index("ex") // 2
    far = jnp.take(far, jnp.bitwise_xor(jnp.arange(n_z), place), axis=1)
    old = far.transpose(0, 2, 1, 3).reshape(2, C, NB, TILE).transpose(0, 2, 1, 3)
    block = order[0, 0]
    return [lax.dynamic_index_in_dim(old, i, 0, keepdims=False) for i in (block, 1 - block)]


def own_blocks(olds, order, own):
    place = lax.axis_index("ex") // 2
    rows = []
    for old in olds:
        old = old.transpose(1, 0, 2).reshape(C, HALF)
        rows.append(lax.dynamic_slice_in_dim(old, place * own, own, 1))
    first = order[0, 0] == 0
    both = [jnp.where(first, rows[0], rows[1]), jnp.where(first, rows[1], rows[0])]
    return jnp.swapaxes(jnp.stack(both), 1, 2)


def local(x_values, tile_live, labels, margins, coef, order):
    rows = x_values.shape[0]
    n_ex = lax.axis_size("ex")
    count = float(rows * n_ex)
    own = coef.shape[1]
    core = lax.axis_index("ex") % 2
    aligned = own == TILE and n_ex == 2 * NB
    labels = labels.reshape(rows // TILE, TILE)
    order = order.reshape(1, STEPS)
    z_bits = [2 * b for b in bits(n_ex // 2)]

    x_shape = sds((rows, BLOCK), BF16)
    soft_shapes = (
        sds((C, rows), F32), sds((C, rows), BF16), sds((rows, TILE), F32), sds((NB, ROWS, TILE), F32),
    )
    g_shape = soft_shapes[-1]
    old_shape, delta_shape = sds((NB, C, TILE), F32), sds((C, HALF), BF16)
    part_shape, half = sds((rows, C), F32), (C, rows // 2)
    own_shape, same_shape = sds((C, TILE), F32), sds((8, TILE), F32)
    flops, nbytes = 2 * rows * HALF * C, 1 << 20

    def message(n):
        return sds((PB + n, ROWS, TILE), BF16)

    if aligned:
        x, score, res_t, spread, g_other, *rest = call(
            first_body,
            (x_shape,) + soft_shapes + (own_shape,) * 2 + (same_shape,) * (STEPS - 1),
            hbm(6), "soft_first", flops, nbytes,
            scratch_shapes=[
                pltpu.SMEM(order.shape, jnp.int32),
                pltpu.SMEM(tile_live.shape, jnp.int32),
                pltpu.VMEM(margins.shape, BF16),
                pltpu.VMEM(labels.shape, jnp.int32),
                pltpu.VMEM(coef.shape, F32),
                pltpu.SemaphoreType.DMA((5,)),
            ] + block_scratch(rows),
        )(order, tile_live, margins, labels, coef, x_values)
        blocks, same = rest[:2], rest[2:]
    else:
        x = prep_general(x_values, tile_live, order[0, 0], core, own)
        score, res_t, spread, g_other = call(
            first_general_body, soft_shapes, vmem(3), "soft_first", flops, nbytes
        )(margins, labels, x)
        blocks = gather_blocks(coef, order, z_bits)
        same = [
            jnp.full((8, TILE), (order[0, step] == order[0, 0]).astype(F32)) for step in range(1, STEPS)
        ]

    errors = []
    for step in range(STEPS):
        if step > 0:
            if aligned:
                x = prep(order, tile_live, x_values, step)
            else:
                x = prep_general(x_values, tile_live, order[0, step], core, own)
            score, res_t, spread, g_other = call(
                next_body, soft_shapes, vmem(7), "soft_next", flops, nbytes
            )(score, *halves, labels, x)
        got = swap_core(g_other)
        g_own = call(own_body, g_shape, vmem(3), "own", flops, nbytes)(res_t, spread, x)
        carry = aligned and step < 2
        if carry:
            p, q = call(pair_with_body, (message(1), message(0)), vmem(3), "pair")(g_own, got, blocks[step])
        else:
            p, q = call(pair_body, (message(0), message(0)), vmem(2), "pair")(g_own, got)
        for n, bit in enumerate(z_bits):
            got_p = swap(p, lambda f, e, bit=bit: (f, e ^ bit))
            got_q = swap(q, lambda f, e, bit=bit: (f, e ^ bit))
            if n < len(z_bits) - 1:
                body, extra = (hop_with_body, 2) if carry else (hop_body, 0)
                p = call(body, message(extra), vmem(2), "hop_p")(p, got_p)
                q = call(hop_body, message(0), vmem(2), "hop_q")(q, got_q)
        if step < 2:
            far = blocks[step]
            if aligned:
                far = call(place_body, old_shape, vmem(3), "place")(p, got_p, far)
        sums = (p, got_p, q, got_q)
        if step == 0:
            first, delta = call(
                functools.partial(prox_first_body, count), (old_shape, delta_shape), vmem(5), "prox"
            )(*sums, far)
        else:
            first, other, delta = call(
                functools.partial(prox_body, count), (old_shape, old_shape, delta_shape), vmem(7), "prox"
            )(same[step - 1], *sums, first, far if step == 1 else other)
        got = swap_core(delta)
        part = call(mine_body, part_shape, vmem(2), "mine", flops, nbytes)(x, delta)
        a, b, ea, eb = call(
            functools.partial(change_body, len(errors)),
            (sds(half, BF16), sds(half, BF16), sds(half, F32), sds(half, F32)),
            vmem(3 + len(errors)), "change", flops, nbytes,
        )(x, part, got, *errors)
        halves, errors = sum_over_feat(a, b)
        errors = [ea, eb] + errors
    score = call(last_body, jax.ShapeDtypeStruct((rows, C), F32), vmem(5), "last")(score, *halves)
    if aligned:
        coef = call(coef_body, sds(coef.shape, F32), smem(1) + vmem(2), "coef_out")(order, first, other)
    else:
        coef = own_blocks((first, other), order, own)
    return score, coef


def solution(mesh):
    return jax.shard_map(
        local,
        mesh=mesh,
        in_specs=(
            P("ex", "feat"),
            P("ex", "feat"),
            P("ex"),
            P("ex", None),
            P(None, ("feat", "ex"), None),
            P(None, "feat"),
        ),
        out_specs=(P("ex", None), P(None, ("feat", "ex"), None)),
        check_vma=False,
    )
```

```python
import functools

import jax
import jax.numpy as jnp
from jax import lax
from jax.experimental import pallas as pl
from jax.experimental.pallas import tpu as pltpu
from jax.sharding import PartitionSpec as P

C = 128
BLOCK = 1024
STEPS = 3
HALF = BLOCK // 2
TILE = 128
NB = HALF // TILE
PB = NB // 2
ROWS = C + 8

ridge = 0.002
lasso = 0.005

F32 = jnp.float32
BF16 = jnp.bfloat16


def vmem(n):
    return [pl.BlockSpec(memory_space=pltpu.VMEM)] * n


def smem(n):
    return [pl.BlockSpec(memory_space=pltpu.SMEM)] * n


def hbm(n):
    return [pl.BlockSpec(memory_space=pltpu.HBM)] * n


def call(body, outs, in_specs, name, flops=0, nbytes=0, **kw):
    f = pl.pallas_call(
        body,
        out_shape=outs,
        in_specs=in_specs,
        out_specs=jax.tree.map(lambda _: pl.BlockSpec(memory_space=pltpu.VMEM), outs),
        name=name,
        cost_estimate=pl.CostEstimate(flops=flops, bytes_accessed=nbytes, transcendentals=0),
        compiler_params=pltpu.CompilerParams(vmem_limit_bytes=16 << 20),
        **kw,
    )

    def run(*args):
        return f(
            *(
                x
                if spec.memory_space == pltpu.SMEM
                else pltpu.with_memory_space_constraint(x, spec.memory_space)
                for spec, x in zip(in_specs, args, strict=True)
            )
        )

    return run


def sds(shape, dtype):
    return pltpu.VMEM(shape, dtype)


def load_block(chosen, x_ref, buf, sems):
    copies = [
        pltpu.make_async_copy(
            x_ref.at[pl.ds(r * TILE, TILE), pl.ds(pl.multiple_of(chosen * BLOCK, BLOCK), BLOCK)],
            buf.at[pl.ds(r * TILE, TILE)],
            sems.at[r],
        )
        for r in range(buf.shape[0] // TILE)
    ]
    for copy in copies:
        copy.start()
    return copies


def mask_tile(r, chosen, core, live_ref, buf, out_ref):
    tiles = BLOCK // TILE
    here = pl.ds(r * TILE, TILE)
    for k in range(tiles):
        col = 2 * (k % NB) + (core if k < NB else 1 - core)
        live = live_ref[r, chosen * tiles + col].astype(F32)
        tile = buf[here, pl.ds(pl.multiple_of(col * TILE, TILE), TILE)]
        out_ref[here, k * TILE : (k + 1) * TILE] = (tile.astype(F32) * live).astype(BF16)


def prep_body(step, order_ref, live_ref, x_ref, out_ref, buf, sems):
    chosen, core = order_ref[0, step], lax.axis_index("ex") % 2
    copies = load_block(chosen, x_ref, buf, sems)
    for r, copy in enumerate(copies):
        copy.wait()
        mask_tile(r, chosen, core, live_ref, buf, out_ref)


def block_scratch(rows):
    return [pltpu.VMEM((rows, BLOCK), BF16), pltpu.SemaphoreType.DMA((rows // TILE,))]


def prep(order, tile_live, x_values, step):
    rows = x_values.shape[0]
    return call(
        functools.partial(prep_body, step),
        sds((rows, BLOCK), BF16),
        smem(2) + hbm(1),
        "prep",
        nbytes=4 * rows * BLOCK,
        scratch_shapes=block_scratch(rows),
    )(order, tile_live, x_values)


def prep_general(x_values, tile_live, chosen, core, own):
    rows = x_values.shape[0]
    tiles = BLOCK // TILE
    x = lax.dynamic_slice_in_dim(x_values, chosen * BLOCK, BLOCK, 1)
    live = lax.dynamic_slice_in_dim(tile_live, chosen * tiles, tiles, 1).astype(BF16)
    x = x.reshape(rows // TILE, TILE, tiles, TILE) * live[:, None, :, None]
    x = x.reshape(rows, HALF // own, 2, own)
    mine = lax.dynamic_index_in_dim(x, core, 2, keepdims=False)
    other = lax.dynamic_index_in_dim(x, 1 - core, 2, keepdims=False)
    return jnp.concatenate([mine.reshape(rows, HALF), other.reshape(rows, HALF)], axis=1)


def half_sums(res_t, spread_ref, x_ref, first, g_ref):
    rows = x_ref.shape[0]
    grad = jnp.dot(res_t, x_ref[:, first : first + HALF], preferred_element_type=F32)
    row = lax.broadcasted_iota(jnp.int32, (8, TILE), 0)
    for k in range(NB):
        lanes = slice(first + k * TILE, first + (k + 1) * TILE)
        acc = jnp.zeros((8, TILE), F32)
        for r in range(rows // TILE):
            here = slice(r * TILE, (r + 1) * TILE)
            x = x_ref[here, lanes].astype(F32)
            term = x * x * spread_ref[here, :]
            acc = acc + jnp.sum(term.reshape(TILE // 8, 8, TILE), axis=0)
        total = jnp.sum(acc, axis=0, keepdims=True)
        g_ref[k, 0:C, :] = grad[:, k * TILE : (k + 1) * TILE]
        g_ref[k, C:ROWS, :] = jnp.where(row == 0, total, 0.0)


def soft_rows(score, labels, here, res_ref, spread_ref):
    top = jnp.max(score, axis=0, keepdims=True)
    expo = jnp.exp(score - top)
    prob = expo / jnp.sum(expo, axis=0, keepdims=True)
    classes = lax.broadcasted_iota(jnp.int32, (C, TILE), 0)
    residual = prob - jnp.where(labels == classes, 1.0, 0.0)
    spread = (1.0 - jnp.sum(prob * prob, axis=0, keepdims=True)).astype(BF16).astype(F32)
    res_ref[:, here] = residual.astype(BF16)
    spread_ref[here, :] = jnp.broadcast_to(spread, (TILE, TILE)).T


def tiles_of(rows):
    return [(r, slice(r * TILE, (r + 1) * TILE)) for r in range(rows // TILE)]


def first_body(
    order_hbm, live_hbm, margins_hbm, lab_hbm, coef_hbm, x_hbm,
    x_ref, score_ref, res_ref, spread_ref, g_ref, first_ref, other_ref, first_send, other_send, *rest,
):
    same_refs = rest[: STEPS - 1]
    order, live, margins, labels, coef, small, buf, sems = rest[STEPS - 1 :]
    loads = [
        pltpu.make_async_copy(src, dst, small.at[i])
        for i, (src, dst) in enumerate(
            ((order_hbm, order), (live_hbm, live), (margins_hbm, margins), (lab_hbm, labels), (coef_hbm, coef))
        )
    ]
    for load in loads:
        load.start()
    loads[0].wait()
    chosen, core = order[0, 0], lax.axis_index("ex") % 2
    copies = load_block(chosen, x_hbm, buf, sems)
    for load in loads[1:]:
        load.wait()
    for r, here in tiles_of(margins.shape[0]):
        score = margins[here, :].astype(F32).T
        score_ref[:, here] = score
        soft_rows(score, labels[r : r + 1, :], here, res_ref, spread_ref)
    for block, keep, send in ((chosen, first_ref, first_send), (1 - chosen, other_ref, other_send)):
        rows = coef[block].T
        keep[...] = rows
        send[...] = rows.astype(BF16)
    for step, same_ref in enumerate(same_refs):
        same_ref[...] = jnp.full((8, TILE), (order[0, step + 1] == chosen).astype(F32))
    for r, copy in enumerate(copies):
        copy.wait()
        mask_tile(r, chosen, core, live, buf, x_ref)
    half_sums(res_ref[...], spread_ref, x_ref, HALF, g_ref)


def first_general_body(margins_ref, lab_ref, x_ref, score_ref, res_ref, spread_ref, g_ref):
    for r, here in tiles_of(margins_ref.shape[0]):
        score = margins_ref[here, :].astype(F32).T
        score_ref[:, here] = score
        soft_rows(score, lab_ref[r : r + 1, :], here, res_ref, spread_ref)
    half_sums(res_ref[...], spread_ref, x_ref, HALF, g_ref)


def next_body(before_ref, a_ref, ra_ref, b_ref, rb_ref, lab_ref, x_ref, score_ref, res_ref, spread_ref, g_ref):
    rows = before_ref.shape[1]
    for r, here in tiles_of(rows):
        score = before_ref[:, here] + change_tile(here, rows, a_ref, ra_ref, b_ref, rb_ref)
        score_ref[:, here] = score
        soft_rows(score, lab_ref[r : r + 1, :], here, res_ref, spread_ref)
    half_sums(res_ref[...], spread_ref, x_ref, HALF, g_ref)


def last_body(before_ref, a_ref, ra_ref, b_ref, rb_ref, out_ref):
    rows = before_ref.shape[1]
    for _, here in tiles_of(rows):
        score = before_ref[:, here] + change_tile(here, rows, a_ref, ra_ref, b_ref, rb_ref)
        out_ref[here, :] = score.T


def change_tile(here, rows, a_ref, ra_ref, b_ref, rb_ref):
    if here.stop <= rows // 2:
        return a_ref[:, here].astype(F32) + ra_ref[:, here].astype(F32)
    at = slice(here.start - rows // 2, here.stop - rows // 2)
    return b_ref[:, at].astype(F32) + rb_ref[:, at].astype(F32)


def own_body(res_ref, spread_ref, x_ref, g_ref):
    half_sums(res_ref[...], spread_ref, x_ref, 0, g_ref)


def encode(k, grad, curv, out_ref):
    out_ref[k, 0:C, :] = grad.astype(BF16)
    high = curv.astype(BF16).astype(F32)
    low = curv - high
    row = lax.broadcasted_iota(jnp.int32, (8, TILE), 0)
    tail = jnp.where(row == 0, high, jnp.where(row == 1, low, 0.0))
    out_ref[k, C:ROWS, :] = tail.astype(BF16)


def pair_body(own_ref, got_ref, p_ref, q_ref):
    for k in range(NB):
        total = own_ref[k] + got_ref[k]
        encode(k % PB, total[0:C], total[C : C + 1], p_ref if k < PB else q_ref)


def pair_with_body(own_ref, got_ref, mine_ref, far_ref, p_ref, q_ref):
    pair_body(own_ref, got_ref, p_ref, q_ref)
    for k, rows_ref in ((PB, mine_ref), (PB + 1, far_ref)):
        q_ref[k, 0:C, :] = rows_ref[...]
        q_ref[k, C:ROWS, :] = jnp.zeros((ROWS - C, TILE), BF16)


def decode_sum(k, mine_ref, got_ref):
    total = mine_ref[k].astype(F32) + got_ref[k].astype(F32)
    return total[0:C], total[C : C + 1] + total[C + 1 : C + 2]


def hop_body(mine_ref, got_ref, out_ref):
    for k in range(PB):
        encode(k, *decode_sum(k, mine_ref, got_ref), out_ref)


def place_body(got_ref, far_ref, coef_ref, out_ref):
    place = lax.axis_index("ex") // 2
    out_ref[place] = coef_ref[...]
    out_ref[jnp.bitwise_xor(place, 1)] = got_ref[PB, 0:C, :].astype(F32)
    out_ref[jnp.bitwise_xor(place, 2)] = far_ref[...].astype(F32)
    out_ref[jnp.bitwise_xor(place, 3)] = got_ref[PB + 1, 0:C, :].astype(F32)


def step_coef(count, k, mine_ref, got_ref, old):
    grad, curv = decode_sum(k, mine_ref, got_ref)
    inverse = 1.0 / (curv / count + ridge)
    shifted = old - grad * (inverse / count)
    limit = lasso * inverse
    return shifted - jnp.clip(shifted, -limit, limit)


def prox_first_body(count, p_ref, gp_ref, q_ref, gq_ref, old_ref, new_ref, delta_ref):
    for k in range(NB):
        old = old_ref[k]
        chunk = (p_ref, gp_ref) if k < PB else (q_ref, gq_ref)
        new = step_coef(count, k % PB, *chunk, old)
        new_ref[k] = new
        delta_ref[:, k * TILE : (k + 1) * TILE] = (new - old).astype(BF16)


def prox_body(count, same_ref, p_ref, gp_ref, q_ref, gq_ref, old0_ref, old1_ref, new0_ref, new1_ref, delta_ref):
    same = jnp.broadcast_to(same_ref[0:1, :], (C, TILE)) > 0.5
    for k in range(NB):
        old0, old1 = old0_ref[k], old1_ref[k]
        old = jnp.where(same, old0, old1)
        chunk = (p_ref, gp_ref) if k < PB else (q_ref, gq_ref)
        new = step_coef(count, k % PB, *chunk, old)
        new0_ref[k] = jnp.where(same, new, old0)
        new1_ref[k] = jnp.where(same, old1, new)
        delta_ref[:, k * TILE : (k + 1) * TILE] = (new - old).astype(BF16)


def coef_body(order_ref, first_ref, other_ref, out_ref):
    place = lax.axis_index("ex") // 2
    block = order_ref[0, 0]
    out_ref[block] = first_ref[place].T
    out_ref[1 - block] = other_ref[place].T


def contrib(x_ref, first, delta_ref):
    return lax.dot_general(
        x_ref[:, first : first + HALF], delta_ref[...],
        (((1,), (1,)), ((), ())), preferred_element_type=F32,
    )


def mine_body(x_ref, delta_ref, part_ref):
    part_ref[...] = contrib(x_ref, 0, delta_ref)


def change_body(carried, x_ref, part_ref, delta_ref, *refs):
    errors, (a_ref, b_ref, *keep) = refs[:carried], refs[carried:]
    part = part_ref[...] + contrib(x_ref, HALF, delta_ref)
    rows = x_ref.shape[0]
    for _, here in tiles_of(rows):
        low = here.stop <= rows // 2
        at = here if low else slice(here.start - rows // 2, here.stop - rows // 2)
        full = part[here, :].T
        for e_ref in errors[0::2] if low else errors[1::2]:
            full = full + e_ref[:, at]
        sent = full.astype(BF16)
        (a_ref if low else b_ref)[:, at] = sent
        if keep:
            keep[0 if low else 1][:, at] = full - sent.astype(F32)


def meet_body(share, mine_ref, got_ref, out_ref, *error_refs):
    total = mine_ref[...].astype(F32) + got_ref[...].astype(F32)
    sent = total.astype(BF16)
    out_ref[...] = sent
    for error_ref in error_refs:
        error_ref[...] = share * (total - sent.astype(F32))


def bits(n):
    return [1 << i for i in range(n.bit_length() - 1)]


def swap(x, move):
    n_feat, n_ex = lax.axis_size("feat"), lax.axis_size("ex")
    pairs = []
    for f in range(n_feat):
        for e in range(n_ex):
            to_f, to_e = move(f, e)
            pairs.append((f * n_ex + e, to_f * n_ex + to_e))
    return lax.ppermute(x, ("feat", "ex"), pairs)


def swap_core(x):
    return swap(x, lambda f, e: (f, e ^ 1))


def sum_over_feat(a, b, last):
    order = bits(lax.axis_size("feat"))
    errors, pair = [], 1
    for n in range(len(order)):
        got_a = swap(a, lambda f, e, n=n: (f ^ order[n], e))
        got_b = swap(b, lambda f, e, n=n: (f ^ order[-1 - n], e))
        if n == len(order) - 1:
            return (a, got_a, b, got_b), errors
        pair *= 2
        shapes = (sds(a.shape, BF16),) + (() if last else (sds(a.shape, F32),))
        meet = functools.partial(meet_body, 1.0 / pair)
        a, *ea = call(meet, shapes, vmem(2), "meet_a")(a, got_a)
        b, *eb = call(meet, shapes, vmem(2), "meet_b")(b, got_b)
        errors += ea + eb


def gather_blocks(coef, order, z_bits):
    n_z = 1 << len(z_bits)
    far = jnp.swapaxes(coef, 1, 2)[:, None]
    for bit in z_bits:
        far = jnp.concatenate([far, swap(far, lambda f, e, bit=bit: (f, e ^ bit))], axis=1)
    place = lax.axis_index("ex") // 2
    far = jnp.take(far, jnp.bitwise_xor(jnp.arange(n_z), place), axis=1)
    old = far.transpose(0, 2, 1, 3).reshape(2, C, NB, TILE).transpose(0, 2, 1, 3)
    block = order[0, 0]
    return [lax.dynamic_index_in_dim(old, i, 0, keepdims=False) for i in (block, 1 - block)]


def own_blocks(olds, order, own):
    place = lax.axis_index("ex") // 2
    rows = []
    for old in olds:
        old = old.transpose(1, 0, 2).reshape(C, HALF)
        rows.append(lax.dynamic_slice_in_dim(old, place * own, own, 1))
    first = order[0, 0] == 0
    both = [jnp.where(first, rows[0], rows[1]), jnp.where(first, rows[1], rows[0])]
    return jnp.swapaxes(jnp.stack(both), 1, 2)


def local(x_values, tile_live, labels, margins, coef, order):
    rows = x_values.shape[0]
    n_ex = lax.axis_size("ex")
    count = float(rows * n_ex)
    own = coef.shape[1]
    core = lax.axis_index("ex") % 2
    aligned = own == TILE and n_ex == 2 * NB
    labels = labels.reshape(rows // TILE, TILE)
    order = order.reshape(1, STEPS)
    z_bits = [2 * b for b in bits(n_ex // 2)]

    x_shape = sds((rows, BLOCK), BF16)
    soft_shapes = (
        sds((C, rows), F32), sds((C, rows), BF16), sds((rows, TILE), F32), sds((NB, ROWS, TILE), F32),
    )
    g_shape = soft_shapes[-1]
    old_shape, delta_shape = sds((NB, C, TILE), F32), sds((C, HALF), BF16)
    part_shape, half = sds((rows, C), F32), (C, rows // 2)
    own_shape, send_shape, same_shape = sds((C, TILE), F32), sds((C, TILE), BF16), sds((8, TILE), F32)
    flops, nbytes = 2 * rows * HALF * C, 1 << 20

    def message(n):
        return sds((PB + n, ROWS, TILE), BF16)

    if aligned:
        x, score, res_t, spread, g_other, *rest = call(
            first_body,
            (x_shape,) + soft_shapes + (own_shape,) * 2 + (send_shape,) * 2 + (same_shape,) * (STEPS - 1),
            hbm(6), "soft_first", flops, nbytes,
            scratch_shapes=[
                pltpu.SMEM(order.shape, jnp.int32),
                pltpu.SMEM(tile_live.shape, jnp.int32),
                pltpu.VMEM(margins.shape, BF16),
                pltpu.VMEM(labels.shape, jnp.int32),
                pltpu.VMEM(coef.shape, F32),
                pltpu.SemaphoreType.DMA((5,)),
            ] + block_scratch(rows),
        )(order, tile_live, margins, labels, coef, x_values)
        blocks, sends, same = rest[:2], rest[2:4], rest[4:]
        across = lambda rows: swap(rows, lambda f, e: (f, e ^ z_bits[-1]))
        fars = [across(sends[0]), None]
    else:
        x = prep_general(x_values, tile_live, order[0, 0], core, own)
        score, res_t, spread, g_other = call(
            first_general_body, soft_shapes, vmem(3), "soft_first", flops, nbytes
        )(margins, labels, x)
        blocks = gather_blocks(coef, order, z_bits)
        same = [
            jnp.full((8, TILE), (order[0, step] == order[0, 0]).astype(F32)) for step in range(1, STEPS)
        ]

    errors = []
    for step in range(STEPS):
        if step > 0:
            x = following
            score, res_t, spread, g_other = call(
                next_body, soft_shapes, vmem(7), "soft_next", flops, nbytes
            )(score, *halves, labels, x)
        got = swap_core(g_other)
        g_own = call(own_body, g_shape, vmem(3), "own", flops, nbytes)(res_t, spread, x)
        carry = aligned and step < 2
        if carry:
            p, q = call(pair_with_body, (message(0), message(2)), vmem(4), "pair")(
                g_own, got, sends[step], fars[step]
            )
        else:
            p, q = call(pair_body, (message(0), message(0)), vmem(2), "pair")(g_own, got)
        for n, bit in enumerate(z_bits):
            got_p = swap(p, lambda f, e, bit=bit: (f, e ^ bit))
            got_q = swap(q, lambda f, e, bit=bit: (f, e ^ bit))
            if n == 0 and carry:
                old = call(place_body, old_shape, vmem(3), "place")(got_q, fars[step], blocks[step])
            elif n == 0 and step < 2:
                old = blocks[step]
            if n < len(z_bits) - 1:
                p = call(hop_body, message(0), vmem(2), "hop_p")(p, got_p)
                q = call(hop_body, message(0), vmem(2), "hop_q")(q, got_q)
        sums = (p, got_p, q, got_q)
        if step < STEPS - 1 and aligned:
            following = prep(order, tile_live, x_values, step + 1)
            *sums, following = lax.optimization_barrier((*sums, following))
        elif step < STEPS - 1:
            following = prep_general(x_values, tile_live, order[0, step + 1], core, own)
        if step == 0:
            first, delta = call(
                functools.partial(prox_first_body, count), (old_shape, delta_shape), vmem(5), "prox"
            )(*sums, old)
        else:
            first, other, delta = call(
                functools.partial(prox_body, count), (old_shape, old_shape, delta_shape), vmem(7), "prox"
            )(same[step - 1], *sums, first, old if step == 1 else other)
        got = swap_core(delta)
        part = call(mine_body, part_shape, vmem(2), "mine", flops, nbytes)(x, delta)
        last = step == STEPS - 1
        shapes = (sds(half, BF16),) * 2 + (() if last else (sds(half, F32),) * 2)
        a, b, *kept = call(
            functools.partial(change_body, len(errors)), shapes, vmem(3 + len(errors)), "change", flops, nbytes,
        )(x, part, got, *errors)
        if step == 0 and aligned:
            a, b, send = lax.optimization_barrier((a, b, sends[1]))
            fars[1] = across(send)
        halves, errors = sum_over_feat(a, b, last)
        if step == 0 and aligned:
            *halves, fars[1] = lax.optimization_barrier((*halves, fars[1]))
        errors = kept + errors
    score = call(last_body, jax.ShapeDtypeStruct((rows, C), F32), vmem(5), "last")(score, *halves)
    if aligned:
        coef = call(coef_body, sds(coef.shape, F32), smem(1) + vmem(2), "coef_out")(order, first, other)
    else:
        coef = own_blocks((first, other), order, own)
    return score, coef


def solution(mesh):
    return jax.shard_map(
        local,
        mesh=mesh,
        in_specs=(
            P("ex", "feat"),
            P("ex", "feat"),
            P("ex"),
            P("ex", None),
            P(None, ("feat", "ex"), None),
            P(None, "feat"),
        ),
        out_specs=(P("ex", None), P(None, ("feat", "ex"), None)),
        check_vma=False,
    )
```

```python
import functools

import jax
import jax.numpy as jnp
from jax import lax
from jax.experimental import pallas as pl
from jax.experimental.pallas import tpu as pltpu
from jax.sharding import PartitionSpec as P

C = 128
BLOCK = 1024
STEPS = 3
HALF = BLOCK // 2
TILE = 128
NB = HALF // TILE
PB = NB // 2
ROWS = C + 8

ridge = 0.002
lasso = 0.005

F32 = jnp.float32
BF16 = jnp.bfloat16


def vmem(n):
    return [pl.BlockSpec(memory_space=pltpu.VMEM)] * n


def smem(n):
    return [pl.BlockSpec(memory_space=pltpu.SMEM)] * n


def hbm(n):
    return [pl.BlockSpec(memory_space=pltpu.HBM)] * n


def call(body, outs, in_specs, name, flops=0, nbytes=0, **kw):
    f = pl.pallas_call(
        body,
        out_shape=outs,
        in_specs=in_specs,
        out_specs=jax.tree.map(lambda _: pl.BlockSpec(memory_space=pltpu.VMEM), outs),
        name=name,
        cost_estimate=pl.CostEstimate(flops=flops, bytes_accessed=nbytes, transcendentals=0),
        compiler_params=pltpu.CompilerParams(vmem_limit_bytes=16 << 20),
        **kw,
    )

    def run(*args):
        return f(
            *(
                x
                if spec.memory_space == pltpu.SMEM
                else pltpu.with_memory_space_constraint(x, spec.memory_space)
                for spec, x in zip(in_specs, args, strict=True)
            )
        )

    return run


def sds(shape, dtype):
    return pltpu.VMEM(shape, dtype)


def load_block(chosen, x_ref, buf, sems):
    copies = [
        pltpu.make_async_copy(
            x_ref.at[pl.ds(r * TILE, TILE), pl.ds(pl.multiple_of(chosen * BLOCK, BLOCK), BLOCK)],
            buf.at[pl.ds(r * TILE, TILE)],
            sems.at[r],
        )
        for r in range(buf.shape[0] // TILE)
    ]
    for copy in copies:
        copy.start()
    return copies


def mask_tile(r, chosen, core, live_ref, buf, out_ref):
    tiles = BLOCK // TILE
    here = pl.ds(r * TILE, TILE)
    for k in range(tiles):
        col = 2 * (k % NB) + (core if k < NB else 1 - core)
        live = live_ref[r, chosen * tiles + col].astype(F32)
        tile = buf[here, pl.ds(pl.multiple_of(col * TILE, TILE), TILE)]
        out_ref[here, k * TILE : (k + 1) * TILE] = (tile.astype(F32) * live).astype(BF16)


def prep_body(step, order_ref, live_ref, x_ref, out_ref, buf, sems):
    chosen, core = order_ref[0, step], lax.axis_index("ex") % 2
    copies = load_block(chosen, x_ref, buf, sems)
    for r, copy in enumerate(copies):
        copy.wait()
        mask_tile(r, chosen, core, live_ref, buf, out_ref)


def block_scratch(rows):
    return [pltpu.VMEM((rows, BLOCK), BF16), pltpu.SemaphoreType.DMA((rows // TILE,))]


def prep(order, tile_live, x_values, step):
    rows = x_values.shape[0]
    return call(
        functools.partial(prep_body, step),
        sds((rows, BLOCK), BF16),
        smem(2) + hbm(1),
        "prep",
        nbytes=4 * rows * BLOCK,
        scratch_shapes=block_scratch(rows),
    )(order, tile_live, x_values)


def prep_general(x_values, tile_live, chosen, core, own):
    rows = x_values.shape[0]
    tiles = BLOCK // TILE
    x = lax.dynamic_slice_in_dim(x_values, chosen * BLOCK, BLOCK, 1)
    live = lax.dynamic_slice_in_dim(tile_live, chosen * tiles, tiles, 1).astype(BF16)
    x = x.reshape(rows // TILE, TILE, tiles, TILE) * live[:, None, :, None]
    x = x.reshape(rows, HALF // own, 2, own)
    mine = lax.dynamic_index_in_dim(x, core, 2, keepdims=False)
    other = lax.dynamic_index_in_dim(x, 1 - core, 2, keepdims=False)
    return jnp.concatenate([mine.reshape(rows, HALF), other.reshape(rows, HALF)], axis=1)


def half_sums(res_t, spread_ref, x_ref, first, g_ref):
    rows = x_ref.shape[0]
    grad = jnp.dot(res_t, x_ref[:, first : first + HALF], preferred_element_type=F32)
    row = lax.broadcasted_iota(jnp.int32, (8, TILE), 0)
    for k in range(NB):
        lanes = slice(first + k * TILE, first + (k + 1) * TILE)
        acc = jnp.zeros((8, TILE), F32)
        for r in range(rows // TILE):
            here = slice(r * TILE, (r + 1) * TILE)
            x = x_ref[here, lanes].astype(F32)
            term = x * x * spread_ref[here, :]
            acc = acc + jnp.sum(term.reshape(TILE // 8, 8, TILE), axis=0)
        total = jnp.sum(acc, axis=0, keepdims=True)
        g_ref[k, 0:C, :] = grad[:, k * TILE : (k + 1) * TILE]
        g_ref[k, C:ROWS, :] = jnp.where(row == 0, total, 0.0)


def soft_rows(score, labels, here, res_ref, spread_ref):
    top = jnp.max(score, axis=0, keepdims=True)
    expo = jnp.exp(score - top)
    prob = expo / jnp.sum(expo, axis=0, keepdims=True)
    classes = lax.broadcasted_iota(jnp.int32, (C, TILE), 0)
    residual = prob - jnp.where(labels == classes, 1.0, 0.0)
    spread = (1.0 - jnp.sum(prob * prob, axis=0, keepdims=True)).astype(BF16).astype(F32)
    res_ref[:, here] = residual.astype(BF16)
    spread_ref[here, :] = jnp.broadcast_to(spread, (TILE, TILE)).T


def tiles_of(rows):
    return [(r, slice(r * TILE, (r + 1) * TILE)) for r in range(rows // TILE)]


def first_body(
    order_hbm, live_hbm, margins_hbm, lab_hbm, coef_hbm, x_hbm,
    x_ref, score_ref, res_ref, spread_ref, g_ref, first_ref, other_ref, first_send, other_send, *rest,
):
    same_refs = rest[: STEPS - 1]
    order, live, margins, labels, coef, small, buf, sems = rest[STEPS - 1 :]
    loads = [
        pltpu.make_async_copy(src, dst, small.at[i])
        for i, (src, dst) in enumerate(
            ((order_hbm, order), (live_hbm, live), (margins_hbm, margins), (lab_hbm, labels), (coef_hbm, coef))
        )
    ]
    for load in loads:
        load.start()
    loads[0].wait()
    chosen, core = order[0, 0], lax.axis_index("ex") % 2
    copies = load_block(chosen, x_hbm, buf, sems)
    for load in loads[1:]:
        load.wait()
    for r, here in tiles_of(margins.shape[0]):
        score = margins[here, :].astype(F32).T
        score_ref[:, here] = score
        soft_rows(score, labels[r : r + 1, :], here, res_ref, spread_ref)
    for block, keep, send in ((chosen, first_ref, first_send), (1 - chosen, other_ref, other_send)):
        rows = coef[block].T
        keep[...] = rows
        send[...] = rows.astype(BF16)
    for step, same_ref in enumerate(same_refs):
        same_ref[...] = jnp.full((8, TILE), (order[0, step + 1] == chosen).astype(F32))
    for r, copy in enumerate(copies):
        copy.wait()
        mask_tile(r, chosen, core, live, buf, x_ref)
    half_sums(res_ref[...], spread_ref, x_ref, HALF, g_ref)


def first_general_body(margins_ref, lab_ref, x_ref, score_ref, res_ref, spread_ref, g_ref):
    for r, here in tiles_of(margins_ref.shape[0]):
        score = margins_ref[here, :].astype(F32).T
        score_ref[:, here] = score
        soft_rows(score, lab_ref[r : r + 1, :], here, res_ref, spread_ref)
    half_sums(res_ref[...], spread_ref, x_ref, HALF, g_ref)


def next_body(before_ref, a_ref, ra_ref, b_ref, rb_ref, lab_ref, x_ref, score_ref, res_ref, spread_ref, g_ref):
    rows = before_ref.shape[1]
    for r, here in tiles_of(rows):
        score = before_ref[:, here] + change_tile(here, rows, a_ref, ra_ref, b_ref, rb_ref)
        score_ref[:, here] = score
        soft_rows(score, lab_ref[r : r + 1, :], here, res_ref, spread_ref)
    half_sums(res_ref[...], spread_ref, x_ref, HALF, g_ref)


def last_body(before_ref, a_ref, ra_ref, b_ref, rb_ref, out_ref):
    rows = before_ref.shape[1]
    for _, here in tiles_of(rows):
        score = before_ref[:, here] + change_tile(here, rows, a_ref, ra_ref, b_ref, rb_ref)
        out_ref[here, :] = score.T


def change_tile(here, rows, a_ref, ra_ref, b_ref, rb_ref):
    if here.stop <= rows // 2:
        return a_ref[:, here].astype(F32) + ra_ref[:, here].astype(F32)
    at = slice(here.start - rows // 2, here.stop - rows // 2)
    return b_ref[:, at].astype(F32) + rb_ref[:, at].astype(F32)


def own_body(res_ref, spread_ref, x_ref, g_ref):
    half_sums(res_ref[...], spread_ref, x_ref, 0, g_ref)


def encode(k, grad, curv, out_ref):
    out_ref[k, 0:C, :] = grad.astype(BF16)
    high = curv.astype(BF16).astype(F32)
    low = curv - high
    row = lax.broadcasted_iota(jnp.int32, (8, TILE), 0)
    tail = jnp.where(row == 0, high, jnp.where(row == 1, low, 0.0))
    out_ref[k, C:ROWS, :] = tail.astype(BF16)


def pair_body(own_ref, got_ref, p_ref, q_ref):
    for k in range(NB):
        total = own_ref[k] + got_ref[k]
        encode(k % PB, total[0:C], total[C : C + 1], p_ref if k < PB else q_ref)


def decode_sum(k, mine_ref, got_ref):
    total = mine_ref[k].astype(F32) + got_ref[k].astype(F32)
    return total[0:C], total[C : C + 1] + total[C + 1 : C + 2]


def hop_body(mine_ref, got_ref, out_ref):
    for k in range(PB):
        encode(k, *decode_sum(k, mine_ref, got_ref), out_ref)


def place_body(far_ref, near_ref, coef_ref, out_ref):
    place = lax.axis_index("ex") // 2
    out_ref[place] = coef_ref[...]
    out_ref[jnp.bitwise_xor(place, 2)] = far_ref[...].astype(F32)
    out_ref[jnp.bitwise_xor(place, 1)] = near_ref[0].astype(F32)
    out_ref[jnp.bitwise_xor(place, 3)] = near_ref[1].astype(F32)


def step_coef(count, k, mine_ref, got_ref, old):
    grad, curv = decode_sum(k, mine_ref, got_ref)
    inverse = 1.0 / (curv / count + ridge)
    shifted = old - grad * (inverse / count)
    limit = lasso * inverse
    return shifted - jnp.clip(shifted, -limit, limit)


def prox_first_body(count, p_ref, gp_ref, q_ref, gq_ref, old_ref, new_ref, delta_ref):
    for k in range(NB):
        old = old_ref[k]
        chunk = (p_ref, gp_ref) if k < PB else (q_ref, gq_ref)
        new = step_coef(count, k % PB, *chunk, old)
        new_ref[k] = new
        delta_ref[:, k * TILE : (k + 1) * TILE] = (new - old).astype(BF16)


def prox_body(count, same_ref, p_ref, gp_ref, q_ref, gq_ref, old0_ref, old1_ref, new0_ref, new1_ref, delta_ref):
    same = jnp.broadcast_to(same_ref[0:1, :], (C, TILE)) > 0.5
    for k in range(NB):
        old0, old1 = old0_ref[k], old1_ref[k]
        old = jnp.where(same, old0, old1)
        chunk = (p_ref, gp_ref) if k < PB else (q_ref, gq_ref)
        new = step_coef(count, k % PB, *chunk, old)
        new0_ref[k] = jnp.where(same, new, old0)
        new1_ref[k] = jnp.where(same, old1, new)
        delta_ref[:, k * TILE : (k + 1) * TILE] = (new - old).astype(BF16)


def coef_body(order_ref, first_ref, other_ref, out_ref):
    place = lax.axis_index("ex") // 2
    block = order_ref[0, 0]
    out_ref[block] = first_ref[place].T
    out_ref[1 - block] = other_ref[place].T


def contrib(x_ref, first, delta_ref):
    return lax.dot_general(
        x_ref[:, first : first + HALF], delta_ref[...],
        (((1,), (1,)), ((), ())), preferred_element_type=F32,
    )


def mine_body(x_ref, delta_ref, part_ref):
    part_ref[...] = contrib(x_ref, 0, delta_ref)


def change_body(carried, x_ref, part_ref, delta_ref, *refs):
    errors, (a_ref, b_ref, *keep) = refs[:carried], refs[carried:]
    part = part_ref[...] + contrib(x_ref, HALF, delta_ref)
    rows = x_ref.shape[0]
    for _, here in tiles_of(rows):
        low = here.stop <= rows // 2
        at = here if low else slice(here.start - rows // 2, here.stop - rows // 2)
        full = part[here, :].T
        for e_ref in errors[0::2] if low else errors[1::2]:
            full = full + e_ref[:, at]
        sent = full.astype(BF16)
        (a_ref if low else b_ref)[:, at] = sent
        if keep:
            keep[0 if low else 1][:, at] = full - sent.astype(F32)


def meet_body(share, mine_ref, got_ref, out_ref, *error_refs):
    total = mine_ref[...].astype(F32) + got_ref[...].astype(F32)
    sent = total.astype(BF16)
    out_ref[...] = sent
    for error_ref in error_refs:
        error_ref[...] = share * (total - sent.astype(F32))


def bits(n):
    return [1 << i for i in range(n.bit_length() - 1)]


def swap(x, move):
    n_feat, n_ex = lax.axis_size("feat"), lax.axis_size("ex")
    pairs = []
    for f in range(n_feat):
        for e in range(n_ex):
            to_f, to_e = move(f, e)
            pairs.append((f * n_ex + e, to_f * n_ex + to_e))
    return lax.ppermute(x, ("feat", "ex"), pairs)


def swap_core(x):
    return swap(x, lambda f, e: (f, e ^ 1))


def sum_over_feat(a, b, last):
    order = bits(lax.axis_size("feat"))
    errors, pair = [], 1
    for n in range(len(order)):
        got_a = swap(a, lambda f, e, n=n: (f ^ order[n], e))
        got_b = swap(b, lambda f, e, n=n: (f ^ order[-1 - n], e))
        if n == len(order) - 1:
            return (a, got_a, b, got_b), errors
        pair *= 2
        shapes = (sds(a.shape, BF16),) + (() if last else (sds(a.shape, F32),))
        meet = functools.partial(meet_body, 1.0 / pair)
        a, *ea = call(meet, shapes, vmem(2), "meet_a")(a, got_a)
        b, *eb = call(meet, shapes, vmem(2), "meet_b")(b, got_b)
        errors += ea + eb


def gather_blocks(coef, order, z_bits):
    n_z = 1 << len(z_bits)
    far = jnp.swapaxes(coef, 1, 2)[:, None]
    for bit in z_bits:
        far = jnp.concatenate([far, swap(far, lambda f, e, bit=bit: (f, e ^ bit))], axis=1)
    place = lax.axis_index("ex") // 2
    far = jnp.take(far, jnp.bitwise_xor(jnp.arange(n_z), place), axis=1)
    old = far.transpose(0, 2, 1, 3).reshape(2, C, NB, TILE).transpose(0, 2, 1, 3)
    block = order[0, 0]
    return [lax.dynamic_index_in_dim(old, i, 0, keepdims=False) for i in (block, 1 - block)]


def own_blocks(olds, order, own):
    place = lax.axis_index("ex") // 2
    rows = []
    for old in olds:
        old = old.transpose(1, 0, 2).reshape(C, HALF)
        rows.append(lax.dynamic_slice_in_dim(old, place * own, own, 1))
    first = order[0, 0] == 0
    both = [jnp.where(first, rows[0], rows[1]), jnp.where(first, rows[1], rows[0])]
    return jnp.swapaxes(jnp.stack(both), 1, 2)


def local(x_values, tile_live, labels, margins, coef, order):
    rows = x_values.shape[0]
    n_ex = lax.axis_size("ex")
    count = float(rows * n_ex)
    own = coef.shape[1]
    core = lax.axis_index("ex") % 2
    aligned = own == TILE and n_ex == 2 * NB
    labels = labels.reshape(rows // TILE, TILE)
    order = order.reshape(1, STEPS)
    z_bits = [2 * b for b in bits(n_ex // 2)]

    x_shape = sds((rows, BLOCK), BF16)
    soft_shapes = (
        sds((C, rows), F32), sds((C, rows), BF16), sds((rows, TILE), F32), sds((NB, ROWS, TILE), F32),
    )
    g_shape = soft_shapes[-1]
    old_shape, delta_shape = sds((NB, C, TILE), F32), sds((C, HALF), BF16)
    part_shape, half = sds((rows, C), F32), (C, rows // 2)
    own_shape, send_shape, same_shape = sds((C, TILE), F32), sds((C, TILE), BF16), sds((8, TILE), F32)
    flops, nbytes = 2 * rows * HALF * C, 1 << 20

    message = sds((PB, ROWS, TILE), BF16)

    if aligned:
        x, score, res_t, spread, g_other, *rest = call(
            first_body,
            (x_shape,) + soft_shapes + (own_shape,) * 2 + (send_shape,) * 2 + (same_shape,) * (STEPS - 1),
            hbm(6), "soft_first", flops, nbytes,
            scratch_shapes=[
                pltpu.SMEM(order.shape, jnp.int32),
                pltpu.SMEM(tile_live.shape, jnp.int32),
                pltpu.VMEM(margins.shape, BF16),
                pltpu.VMEM(labels.shape, jnp.int32),
                pltpu.VMEM(coef.shape, F32),
                pltpu.SemaphoreType.DMA((5,)),
            ] + block_scratch(rows),
        )(order, tile_live, margins, labels, coef, x_values)
        blocks, sends, same = rest[:2], rest[2:4], rest[4:]
    else:
        x = prep_general(x_values, tile_live, order[0, 0], core, own)
        score, res_t, spread, g_other = call(
            first_general_body, soft_shapes, vmem(3), "soft_first", flops, nbytes
        )(margins, labels, x)
        blocks = gather_blocks(coef, order, z_bits)
        same = [
            jnp.full((8, TILE), (order[0, step] == order[0, 0]).astype(F32)) for step in range(1, STEPS)
        ]

    errors = []
    for step in range(STEPS):
        if step > 0:
            x = following
            score, res_t, spread, g_other = call(
                next_body, soft_shapes, vmem(7), "soft_next", flops, nbytes
            )(score, *halves, labels, x)
        got = swap_core(g_other)
        g_own = call(own_body, g_shape, vmem(3), "own", flops, nbytes)(res_t, spread, x)
        p, q = call(pair_body, (message, message), vmem(2), "pair")(g_own, got)
        carry = aligned and step < 2
        if carry:
            p, q, send = lax.optimization_barrier((p, q, sends[step]))
        for n, bit in enumerate(z_bits):
            got_p = swap(p, lambda f, e, bit=bit: (f, e ^ bit))
            got_q = swap(q, lambda f, e, bit=bit: (f, e ^ bit))
            if n < len(z_bits) - 1:
                if carry:
                    far = swap(send, lambda f, e: (f, e ^ z_bits[1]))
                p = call(hop_body, message, vmem(2), "hop_p")(p, got_p)
                q = call(hop_body, message, vmem(2), "hop_q")(q, got_q)
        if carry:
            near = swap(jnp.stack([send, far]), lambda f, e: (f, e ^ z_bits[0]))
            old = call(place_body, old_shape, vmem(3), "place")(far, near, blocks[step])
        elif step < 2:
            old = blocks[step]
        sums = (p, got_p, q, got_q)
        if step < STEPS - 1 and aligned:
            following = prep(order, tile_live, x_values, step + 1)
            *sums, following = lax.optimization_barrier((*sums, following))
        elif step < STEPS - 1:
            following = prep_general(x_values, tile_live, order[0, step + 1], core, own)
        if step == 0:
            first, delta = call(
                functools.partial(prox_first_body, count), (old_shape, delta_shape), vmem(5), "prox"
            )(*sums, old)
        else:
            first, other, delta = call(
                functools.partial(prox_body, count), (old_shape, old_shape, delta_shape), vmem(7), "prox"
            )(same[step - 1], *sums, first, old if step == 1 else other)
        got = swap_core(delta)
        part = call(mine_body, part_shape, vmem(2), "mine", flops, nbytes)(x, delta)
        last = step == STEPS - 1
        shapes = (sds(half, BF16),) * 2 + (() if last else (sds(half, F32),) * 2)
        a, b, *kept = call(
            functools.partial(change_body, len(errors)), shapes, vmem(3 + len(errors)), "change", flops, nbytes,
        )(x, part, got, *errors)
        halves, errors = sum_over_feat(a, b, last)
        errors = kept + errors
    score = call(last_body, jax.ShapeDtypeStruct((rows, C), F32), vmem(5), "last")(score, *halves)
    if aligned:
        coef = call(coef_body, sds(coef.shape, F32), smem(1) + vmem(2), "coef_out")(order, first, other)
    else:
        coef = own_blocks((first, other), order, own)
    return score, coef


def solution(mesh):
    return jax.shard_map(
        local,
        mesh=mesh,
        in_specs=(
            P("ex", "feat"),
            P("ex", "feat"),
            P("ex"),
            P("ex", None),
            P(None, ("feat", "ex"), None),
            P(None, "feat"),
        ),
        out_specs=(P("ex", None), P(None, ("feat", "ex"), None)),
        check_vma=False,
    )
```

```python
import functools

import jax
import jax.numpy as jnp
from jax import lax
from jax.experimental import pallas as pl
from jax.experimental.pallas import tpu as pltpu
from jax.sharding import PartitionSpec as P

C = 128
BLOCK = 1024
STEPS = 3
HALF = BLOCK // 2
TILE = 128
NB = HALF // TILE
PB = NB // 2
ROWS = C + 8

ridge = 0.002
lasso = 0.005

F32 = jnp.float32
BF16 = jnp.bfloat16


def vmem(n):
    return [pl.BlockSpec(memory_space=pltpu.VMEM)] * n


def smem(n):
    return [pl.BlockSpec(memory_space=pltpu.SMEM)] * n


def hbm(n):
    return [pl.BlockSpec(memory_space=pltpu.HBM)] * n


def call(body, outs, in_specs, name, flops=0, nbytes=0, **kw):
    f = pl.pallas_call(
        body,
        out_shape=outs,
        in_specs=in_specs,
        out_specs=jax.tree.map(lambda _: pl.BlockSpec(memory_space=pltpu.VMEM), outs),
        name=name,
        cost_estimate=pl.CostEstimate(flops=flops, bytes_accessed=nbytes, transcendentals=0),
        compiler_params=pltpu.CompilerParams(vmem_limit_bytes=16 << 20),
        **kw,
    )

    def run(*args):
        return f(
            *(
                x
                if spec.memory_space == pltpu.SMEM
                else pltpu.with_memory_space_constraint(x, spec.memory_space)
                for spec, x in zip(in_specs, args, strict=True)
            )
        )

    return run


def sds(shape, dtype):
    return pltpu.VMEM(shape, dtype)


def load_block(chosen, x_ref, buf, sems):
    copies = [
        pltpu.make_async_copy(
            x_ref.at[pl.ds(r * TILE, TILE), pl.ds(pl.multiple_of(chosen * BLOCK, BLOCK), BLOCK)],
            buf.at[pl.ds(r * TILE, TILE)],
            sems.at[r],
        )
        for r in range(buf.shape[0] // TILE)
    ]
    for copy in copies:
        copy.start()
    return copies


def mask_tile(r, chosen, core, live_ref, buf, out_ref):
    tiles = BLOCK // TILE
    here = pl.ds(r * TILE, TILE)
    for k in range(tiles):
        col = 2 * (k % NB) + (core if k < NB else 1 - core)
        live = live_ref[r, chosen * tiles + col].astype(F32)
        tile = buf[here, pl.ds(pl.multiple_of(col * TILE, TILE), TILE)]
        out_ref[here, k * TILE : (k + 1) * TILE] = (tile.astype(F32) * live).astype(BF16)


def prep_body(step, order_ref, live_ref, x_ref, out_ref, buf, sems):
    chosen, core = order_ref[0, step], lax.axis_index("ex") % 2
    copies = load_block(chosen, x_ref, buf, sems)
    for r, copy in enumerate(copies):
        copy.wait()
        mask_tile(r, chosen, core, live_ref, buf, out_ref)


def block_scratch(rows):
    return [pltpu.VMEM((rows, BLOCK), BF16), pltpu.SemaphoreType.DMA((rows // TILE,))]


def prep(order, tile_live, x_values, step):
    rows = x_values.shape[0]
    return call(
        functools.partial(prep_body, step),
        sds((rows, BLOCK), BF16),
        smem(2) + hbm(1),
        "prep",
        nbytes=4 * rows * BLOCK,
        scratch_shapes=block_scratch(rows),
    )(order, tile_live, x_values)


def prep_general(x_values, tile_live, chosen, core, own):
    rows = x_values.shape[0]
    tiles = BLOCK // TILE
    x = lax.dynamic_slice_in_dim(x_values, chosen * BLOCK, BLOCK, 1)
    live = lax.dynamic_slice_in_dim(tile_live, chosen * tiles, tiles, 1).astype(BF16)
    x = x.reshape(rows // TILE, TILE, tiles, TILE) * live[:, None, :, None]
    x = x.reshape(rows, HALF // own, 2, own)
    mine = lax.dynamic_index_in_dim(x, core, 2, keepdims=False)
    other = lax.dynamic_index_in_dim(x, 1 - core, 2, keepdims=False)
    return jnp.concatenate([mine.reshape(rows, HALF), other.reshape(rows, HALF)], axis=1)


def half_sums(res_t, spread_ref, x_ref, start, first, g_ref, so_far=None):
    rows = spread_ref.shape[0]
    grad = jnp.dot(res_t, x_ref[start : start + rows, first : first + HALF], preferred_element_type=F32)
    row = lax.broadcasted_iota(jnp.int32, (8, TILE), 0)
    for k in range(NB):
        lanes = slice(first + k * TILE, first + (k + 1) * TILE)
        acc = jnp.zeros((8, TILE), F32)
        for r, here in tiles_of(rows):
            x = x_ref[start + r * TILE : start + (r + 1) * TILE, lanes].astype(F32)
            term = x * x * spread_ref[here, :]
            acc = acc + jnp.sum(term.reshape(TILE // 8, 8, TILE), axis=0)
        total = jnp.where(row == 0, jnp.sum(acc, axis=0, keepdims=True), 0.0)
        here = grad[:, k * TILE : (k + 1) * TILE]
        if so_far is not None:
            here, total = here + so_far[k, 0:C, :], total + so_far[k, C:ROWS, :]
        g_ref[k, 0:C, :] = here
        g_ref[k, C:ROWS, :] = total


def soft_rows(score, labels, here, res_ref, spread_ref):
    top = jnp.max(score, axis=0, keepdims=True)
    expo = jnp.exp(score - top)
    prob = expo / jnp.sum(expo, axis=0, keepdims=True)
    classes = lax.broadcasted_iota(jnp.int32, (C, TILE), 0)
    residual = prob - jnp.where(labels == classes, 1.0, 0.0)
    spread = (1.0 - jnp.sum(prob * prob, axis=0, keepdims=True)).astype(BF16).astype(F32)
    res_ref[:, here] = residual.astype(BF16)
    spread_ref[here, :] = jnp.broadcast_to(spread, (TILE, TILE)).T


def tiles_of(rows):
    return [(r, slice(r * TILE, (r + 1) * TILE)) for r in range(rows // TILE)]


def keep_score(score, r, low_ref, high_ref):
    per = low_ref.shape[1] // TILE
    (low_ref if r < per else high_ref)[:, r % per * TILE : (r % per + 1) * TILE] = score


def first_body(
    order_hbm, live_hbm, margins_hbm, lab_hbm, coef_hbm, x_hbm,
    x_ref, low_ref, high_ref, res_ref, spread_ref, g_ref, first_ref, other_ref, first_send, other_send, *rest,
):
    same_refs = rest[: STEPS - 1]
    order, live, margins, labels, coef, small, buf, sems = rest[STEPS - 1 :]
    loads = [
        pltpu.make_async_copy(src, dst, small.at[i])
        for i, (src, dst) in enumerate(
            ((order_hbm, order), (live_hbm, live), (margins_hbm, margins), (lab_hbm, labels), (coef_hbm, coef))
        )
    ]
    for load in loads:
        load.start()
    loads[0].wait()
    chosen, core = order[0, 0], lax.axis_index("ex") % 2
    copies = load_block(chosen, x_hbm, buf, sems)
    for load in loads[1:]:
        load.wait()
    for r, here in tiles_of(margins.shape[0]):
        score = margins[here, :].astype(F32).T
        keep_score(score, r, low_ref, high_ref)
        soft_rows(score, labels[r : r + 1, :], here, res_ref, spread_ref)
    for block, keep, send in ((chosen, first_ref, first_send), (1 - chosen, other_ref, other_send)):
        rows = coef[block].T
        keep[...] = rows
        send[...] = rows.astype(BF16)
    for step, same_ref in enumerate(same_refs):
        same_ref[...] = jnp.full((8, TILE), (order[0, step + 1] == chosen).astype(F32))
    for r, copy in enumerate(copies):
        copy.wait()
        mask_tile(r, chosen, core, live, buf, x_ref)
    half_sums(res_ref[...], spread_ref, x_ref, 0, HALF, g_ref)


def first_general_body(margins_ref, lab_ref, x_ref, low_ref, high_ref, res_ref, spread_ref, g_ref):
    for r, here in tiles_of(margins_ref.shape[0]):
        score = margins_ref[here, :].astype(F32).T
        keep_score(score, r, low_ref, high_ref)
        soft_rows(score, lab_ref[r : r + 1, :], here, res_ref, spread_ref)
    half_sums(res_ref[...], spread_ref, x_ref, 0, HALF, g_ref)


def next_rows(start, before_ref, part_ref, got_ref, lab_ref, score_ref, res_ref, spread_ref):
    for r, here in tiles_of(before_ref.shape[1]):
        score = before_ref[:, here] + (part_ref[:, here].astype(F32) + got_ref[:, here].astype(F32))
        score_ref[:, here] = score
        row = start // TILE + r
        soft_rows(score, lab_ref[row : row + 1, :], here, res_ref, spread_ref)


def next_low_body(before_ref, part_ref, got_ref, lab_ref, x_ref, score_ref, res_ref, spread_ref, g_ref, own_ref):
    next_rows(0, before_ref, part_ref, got_ref, lab_ref, score_ref, res_ref, spread_ref)
    half_sums(res_ref[...], spread_ref, x_ref, 0, HALF, g_ref)
    half_sums(res_ref[...], spread_ref, x_ref, 0, 0, own_ref)


def next_high_body(before_ref, part_ref, got_ref, lab_ref, x_ref, so_far, score_ref, res_ref, spread_ref, g_ref):
    start = before_ref.shape[1]
    next_rows(start, before_ref, part_ref, got_ref, lab_ref, score_ref, res_ref, spread_ref)
    half_sums(res_ref[...], spread_ref, x_ref, start, HALF, g_ref, so_far)


def last_low_body(before_ref, part_ref, got_ref, out_ref):
    for _, here in tiles_of(before_ref.shape[1]):
        score = before_ref[:, here] + (part_ref[:, here].astype(F32) + got_ref[:, here].astype(F32))
        out_ref[here, :] = score.T


def last_high_body(low_ref, before_ref, part_ref, got_ref, out_hbm, buf, sems):
    rows = before_ref.shape[1]
    copies = [
        pltpu.make_async_copy(ref, out_hbm.at[pl.ds(i * rows, rows)], sems.at[i])
        for i, ref in enumerate((low_ref, buf))
    ]
    copies[0].start()
    last_low_body(before_ref, part_ref, got_ref, buf)
    copies[1].start()
    for copy in copies:
        copy.wait()


def own_body(res_ref, spread_ref, x_ref, g_ref):
    half_sums(res_ref[...], spread_ref, x_ref, 0, 0, g_ref)


def own_high_body(res_ref, spread_ref, x_ref, so_far, g_ref):
    half_sums(res_ref[...], spread_ref, x_ref, spread_ref.shape[0], 0, g_ref, so_far)


def encode(k, grad, curv, out_ref):
    out_ref[k, 0:C, :] = grad.astype(BF16)
    high = curv.astype(BF16).astype(F32)
    low = curv - high
    row = lax.broadcasted_iota(jnp.int32, (8, TILE), 0)
    tail = jnp.where(row == 0, high, jnp.where(row == 1, low, 0.0))
    out_ref[k, C:ROWS, :] = tail.astype(BF16)


def pair_body(own_ref, got_ref, p_ref, q_ref):
    for k in range(NB):
        total = own_ref[k] + got_ref[k]
        encode(k if k < PB else k - PB, total[0:C], total[C : C + 1], p_ref if k < PB else q_ref)


def decode_sum(k, mine_ref, got_ref):
    total = mine_ref[k].astype(F32) + got_ref[k].astype(F32)
    return total[0:C], total[C : C + 1] + total[C + 1 : C + 2]


def hop_body(mine_ref, got_ref, out_ref):
    for k in range(out_ref.shape[0]):
        encode(k, *decode_sum(k, mine_ref, got_ref), out_ref)


def place_body(far_ref, near_ref, coef_ref, out_ref):
    place = lax.axis_index("ex") // 2
    out_ref[place] = coef_ref[...]
    out_ref[jnp.bitwise_xor(place, 2)] = far_ref[...].astype(F32)
    out_ref[jnp.bitwise_xor(place, 1)] = near_ref[0].astype(F32)
    out_ref[jnp.bitwise_xor(place, 3)] = near_ref[1].astype(F32)


def step_coef(count, k, mine_ref, got_ref, old):
    grad, curv = decode_sum(k, mine_ref, got_ref)
    inverse = 1.0 / (curv / count + ridge)
    shifted = old - grad * (inverse / count)
    limit = lasso * inverse
    return shifted - jnp.clip(shifted, -limit, limit)


def prox_first_body(count, p_ref, gp_ref, q_ref, gq_ref, old_ref, new_ref, delta_ref):
    for k in range(NB):
        old = old_ref[k]
        chunk = (p_ref, gp_ref) if k < PB else (q_ref, gq_ref)
        new = step_coef(count, k if k < PB else k - PB, *chunk, old)
        new_ref[k] = new
        delta_ref[:, k * TILE : (k + 1) * TILE] = (new - old).astype(BF16)


def prox_body(count, same_ref, p_ref, gp_ref, q_ref, gq_ref, old0_ref, old1_ref, new0_ref, new1_ref, delta_ref):
    same = jnp.broadcast_to(same_ref[0:1, :], (C, TILE)) > 0.5
    for k in range(NB):
        old0, old1 = old0_ref[k], old1_ref[k]
        old = jnp.where(same, old0, old1)
        chunk = (p_ref, gp_ref) if k < PB else (q_ref, gq_ref)
        new = step_coef(count, k if k < PB else k - PB, *chunk, old)
        new0_ref[k] = jnp.where(same, new, old0)
        new1_ref[k] = jnp.where(same, old1, new)
        delta_ref[:, k * TILE : (k + 1) * TILE] = (new - old).astype(BF16)


def coef_body(order_ref, first_ref, other_ref, out_ref):
    place = lax.axis_index("ex") // 2
    block = order_ref[0, 0]
    out_ref[block] = first_ref[place].T
    out_ref[1 - block] = other_ref[place].T


def contrib(x_ref, first, delta_ref):
    return lax.dot_general(
        x_ref[:, first : first + HALF], delta_ref[...],
        (((1,), (1,)), ((), ())), preferred_element_type=F32,
    )


def mine_body(x_ref, delta_ref, part_ref):
    part_ref[...] = contrib(x_ref, 0, delta_ref)


def change_body(carried, x_ref, part_ref, delta_ref, *refs):
    errors, (a_ref, b_ref, *keep) = refs[:carried], refs[carried:]
    part = part_ref[...] + contrib(x_ref, HALF, delta_ref)
    rows = x_ref.shape[0]
    for _, here in tiles_of(rows):
        low = here.stop <= rows // 2
        at = here if low else slice(here.start - rows // 2, here.stop - rows // 2)
        full = part[here, :].T
        for e_ref in errors[0::2] if low else errors[1::2]:
            full = full + e_ref[:, at]
        sent = full.astype(BF16)
        (a_ref if low else b_ref)[:, at] = sent
        if keep:
            keep[0 if low else 1][:, at] = full - sent.astype(F32)


def meet_body(share, mine_ref, got_ref, out_ref, *error_refs):
    total = mine_ref[...].astype(F32) + got_ref[...].astype(F32)
    sent = total.astype(BF16)
    out_ref[...] = sent
    for error_ref in error_refs:
        error_ref[...] = share * (total - sent.astype(F32))


def bits(n):
    return [1 << i for i in range(n.bit_length() - 1)]


def swap(x, move):
    n_feat, n_ex = lax.axis_size("feat"), lax.axis_size("ex")
    pairs = []
    for f in range(n_feat):
        for e in range(n_ex):
            to_f, to_e = move(f, e)
            pairs.append((f * n_ex + e, to_f * n_ex + to_e))
    return lax.ppermute(x, ("feat", "ex"), pairs)


def swap_core(x):
    return swap(x, lambda f, e: (f, e ^ 1))


def sum_over_feat(a, b, last):
    order = bits(lax.axis_size("feat"))
    errors, pair = [], 1
    for n in range(len(order)):
        got_a = swap(a, lambda f, e, n=n: (f ^ order[n], e))
        got_b = swap(b, lambda f, e, n=n: (f ^ order[-1 - n], e))
        if n == len(order) - 1:
            return (a, got_a, b, got_b), errors
        pair *= 2
        shapes = (sds(a.shape, BF16),) + (() if last else (sds(a.shape, F32),))
        meet = functools.partial(meet_body, 1.0 / pair)
        a, *ea = call(meet, shapes, vmem(2), "meet_a")(a, got_a)
        b, *eb = call(meet, shapes, vmem(2), "meet_b")(b, got_b)
        errors += ea + eb


def gather_blocks(coef, order, z_bits):
    n_z = 1 << len(z_bits)
    far = jnp.swapaxes(coef, 1, 2)[:, None]
    for bit in z_bits:
        far = jnp.concatenate([far, swap(far, lambda f, e, bit=bit: (f, e ^ bit))], axis=1)
    place = lax.axis_index("ex") // 2
    far = jnp.take(far, jnp.bitwise_xor(jnp.arange(n_z), place), axis=1)
    old = far.transpose(0, 2, 1, 3).reshape(2, C, NB, TILE).transpose(0, 2, 1, 3)
    block = order[0, 0]
    return [lax.dynamic_index_in_dim(old, i, 0, keepdims=False) for i in (block, 1 - block)]


def own_blocks(olds, order, own):
    place = lax.axis_index("ex") // 2
    rows = []
    for old in olds:
        old = old.transpose(1, 0, 2).reshape(C, HALF)
        rows.append(lax.dynamic_slice_in_dim(old, place * own, own, 1))
    first = order[0, 0] == 0
    both = [jnp.where(first, rows[0], rows[1]), jnp.where(first, rows[1], rows[0])]
    return jnp.swapaxes(jnp.stack(both), 1, 2)


def local(x_values, tile_live, labels, margins, coef, order):
    rows = x_values.shape[0]
    n_ex = lax.axis_size("ex")
    count = float(rows * n_ex)
    own = coef.shape[1]
    core = lax.axis_index("ex") % 2
    aligned = own == TILE and n_ex == 2 * NB
    labels = labels.reshape(rows // TILE, TILE)
    order = order.reshape(1, STEPS)
    z_bits = [2 * b for b in bits(n_ex // 2)]

    x_shape = sds((rows, BLOCK), BF16)
    soft_shapes = (
        sds((C, rows // 2), F32), sds((C, rows // 2), F32),
        sds((C, rows), BF16), sds((rows, TILE), F32), sds((NB, ROWS, TILE), F32),
    )
    g_shape = soft_shapes[-1]
    next_shapes = (soft_shapes[0], sds((C, rows // 2), BF16), sds((rows // 2, TILE), F32), g_shape)
    old_shape, delta_shape = sds((NB, C, TILE), F32), sds((C, HALF), BF16)
    part_shape, half = sds((rows, C), F32), (C, rows // 2)
    own_shape, send_shape, same_shape = sds((C, TILE), F32), sds((C, TILE), BF16), sds((8, TILE), F32)
    flops, nbytes = 2 * rows * HALF * C, 1 << 20

    p_shape, q_shape = sds((PB, ROWS, TILE), BF16), sds((NB - PB, ROWS, TILE), BF16)

    if aligned:
        x, low, high, res_t, spread, g_other, *rest = call(
            first_body,
            (x_shape,) + soft_shapes + (own_shape,) * 2 + (send_shape,) * 2 + (same_shape,) * (STEPS - 1),
            hbm(6), "soft_first", flops, nbytes,
            scratch_shapes=[
                pltpu.SMEM(order.shape, jnp.int32),
                pltpu.SMEM(tile_live.shape, jnp.int32),
                pltpu.VMEM(margins.shape, BF16),
                pltpu.VMEM(labels.shape, jnp.int32),
                pltpu.VMEM(coef.shape, F32),
                pltpu.SemaphoreType.DMA((5,)),
            ] + block_scratch(rows),
        )(order, tile_live, margins, labels, coef, x_values)
        blocks, sends, same = rest[:2], rest[2:4], rest[4:]
    else:
        x = prep_general(x_values, tile_live, order[0, 0], core, own)
        low, high, res_t, spread, g_other = call(
            first_general_body, soft_shapes, vmem(3), "soft_first", flops, nbytes
        )(margins, labels, x)
        blocks = gather_blocks(coef, order, z_bits)
        same = [
            jnp.full((8, TILE), (order[0, step] == order[0, 0]).astype(F32)) for step in range(1, STEPS)
        ]

    errors = []
    for step in range(STEPS):
        if step > 0:
            x = following
            a, got_a, b, got_b = halves
            low, _, _, g_other, g_own = call(
                next_low_body, next_shapes + (g_shape,), vmem(5), "soft_low", flops, nbytes
            )(low, a, got_a, labels, x)
            high, res_t, spread, g_other = call(
                next_high_body, next_shapes, vmem(6), "soft_high", flops // 2, nbytes
            )(high, b, got_b, labels, x, g_other)
            got = swap_core(g_other)
            g_own = call(own_high_body, g_shape, vmem(4), "own", flops // 2, nbytes)(res_t, spread, x, g_own)
        else:
            got = swap_core(g_other)
            g_own = call(own_body, g_shape, vmem(3), "own", flops, nbytes)(res_t, spread, x)
        p, q = call(pair_body, (p_shape, q_shape), vmem(2), "pair")(g_own, got)
        carry = aligned and step < 2
        if carry:
            p, q, send = lax.optimization_barrier((p, q, sends[step]))
        for n, bit in enumerate(z_bits):
            got_p = swap(p, lambda f, e, bit=bit: (f, e ^ bit))
            got_q = swap(q, lambda f, e, bit=bit: (f, e ^ bit))
            if n < len(z_bits) - 1:
                if carry:
                    far = swap(send, lambda f, e: (f, e ^ z_bits[1]))
                p = call(hop_body, p_shape, vmem(2), "hop_p")(p, got_p)
                q = call(hop_body, q_shape, vmem(2), "hop_q")(q, got_q)
        if carry:
            near = swap(jnp.stack([send, far]), lambda f, e: (f, e ^ z_bits[0]))
            old = call(place_body, old_shape, vmem(3), "place")(far, near, blocks[step])
        elif step < 2:
            old = blocks[step]
        sums = (p, got_p, q, got_q)
        if step < STEPS - 1 and aligned:
            following = prep(order, tile_live, x_values, step + 1)
            *sums, following = lax.optimization_barrier((*sums, following))
        elif step < STEPS - 1:
            following = prep_general(x_values, tile_live, order[0, step + 1], core, own)
        if step == 0:
            first, delta = call(
                functools.partial(prox_first_body, count), (old_shape, delta_shape), vmem(5), "prox"
            )(*sums, old)
        else:
            first, other, delta = call(
                functools.partial(prox_body, count), (old_shape, old_shape, delta_shape), vmem(7), "prox"
            )(same[step - 1], *sums, first, old if step == 1 else other)
        got = swap_core(delta)
        part = call(mine_body, part_shape, vmem(2), "mine", flops, nbytes)(x, delta)
        last = step == STEPS - 1
        shapes = (sds(half, BF16),) * 2 + (() if last else (sds(half, F32),) * 2)
        a, b, *kept = call(
            functools.partial(change_body, len(errors)), shapes, vmem(3 + len(errors)), "change", flops, nbytes,
        )(x, part, got, *errors)
        halves, errors = sum_over_feat(a, b, last)
        errors = kept + errors
    a, got_a, b, got_b = halves
    half = sds((rows // 2, C), F32)
    low = call(last_low_body, half, vmem(3), "last_low", flops // 4, nbytes)(low, a, got_a)
    score = pl.pallas_call(
        last_high_body,
        out_shape=jax.ShapeDtypeStruct((rows, C), F32),
        in_specs=vmem(4),
        out_specs=pl.BlockSpec(memory_space=pltpu.HBM),
        scratch_shapes=[pltpu.VMEM(half.shape, F32), pltpu.SemaphoreType.DMA((2,))],
        name="last_high",
        compiler_params=pltpu.CompilerParams(vmem_limit_bytes=16 << 20),
    )(*(pltpu.with_memory_space_constraint(v, pltpu.VMEM) for v in (low, high, b, got_b)))
    if aligned:
        coef = call(coef_body, sds(coef.shape, F32), smem(1) + vmem(2), "coef_out")(order, first, other)
    else:
        coef = own_blocks((first, other), order, own)
    return score, coef


def solution(mesh):
    return jax.shard_map(
        local,
        mesh=mesh,
        in_specs=(
            P("ex", "feat"),
            P("ex", "feat"),
            P("ex"),
            P("ex", None),
            P(None, ("feat", "ex"), None),
            P(None, "feat"),
        ),
        out_specs=(P("ex", None), P(None, ("feat", "ex"), None)),
        check_vma=False,
    )
```

```python
import functools

import jax
import jax.numpy as jnp
from jax import lax
from jax.experimental import pallas as pl
from jax.experimental.pallas import tpu as pltpu
from jax.sharding import PartitionSpec as P

C = 128
BLOCK = 1024
STEPS = 3
HALF = BLOCK // 2
TILE = 128
NB = HALF // TILE
PB = NB // 2
TAIL = 8

ridge = 0.002
lasso = 0.005

F32 = jnp.float32
BF16 = jnp.bfloat16


def vmem(n):
    return [pl.BlockSpec(memory_space=pltpu.VMEM)] * n


def smem(n):
    return [pl.BlockSpec(memory_space=pltpu.SMEM)] * n


def hbm(n):
    return [pl.BlockSpec(memory_space=pltpu.HBM)] * n


def call(body, outs, in_specs, name, flops=0, nbytes=0, **kw):
    f = pl.pallas_call(
        body,
        out_shape=outs,
        in_specs=in_specs,
        out_specs=jax.tree.map(lambda _: pl.BlockSpec(memory_space=pltpu.VMEM), outs),
        name=name,
        cost_estimate=pl.CostEstimate(flops=flops, bytes_accessed=nbytes, transcendentals=0),
        compiler_params=pltpu.CompilerParams(vmem_limit_bytes=16 << 20),
        **kw,
    )

    def run(*args):
        return f(
            *(
                x
                if spec.memory_space == pltpu.SMEM
                else pltpu.with_memory_space_constraint(x, spec.memory_space)
                for spec, x in zip(in_specs, args, strict=True)
            )
        )

    return run


def sds(shape, dtype):
    return pltpu.VMEM(shape, dtype)


def load_block(chosen, x_ref, buf, sems):
    copies = [
        pltpu.make_async_copy(
            x_ref.at[pl.ds(r * TILE, TILE), pl.ds(pl.multiple_of(chosen * BLOCK, BLOCK), BLOCK)],
            buf.at[pl.ds(r * TILE, TILE)],
            sems.at[r],
        )
        for r in range(buf.shape[0] // TILE)
    ]
    for copy in copies:
        copy.start()
    return copies


def mask_tile(r, chosen, core, live_ref, buf, out_ref):
    tiles = BLOCK // TILE
    here = pl.ds(r * TILE, TILE)
    for k in range(tiles):
        col = 2 * (k % NB) + (core if k < NB else 1 - core)
        live = live_ref[r, chosen * tiles + col].astype(F32)
        tile = buf[here, pl.ds(pl.multiple_of(col * TILE, TILE), TILE)]
        out_ref[here, k * TILE : (k + 1) * TILE] = (tile.astype(F32) * live).astype(BF16)


def prep_body(step, order_ref, live_ref, x_ref, out_ref, buf, sems):
    chosen, core = order_ref[0, step], lax.axis_index("ex") % 2
    copies = load_block(chosen, x_ref, buf, sems)
    for r, copy in enumerate(copies):
        copy.wait()
        mask_tile(r, chosen, core, live_ref, buf, out_ref)


def block_scratch(rows):
    return [pltpu.VMEM((rows, BLOCK), BF16), pltpu.SemaphoreType.DMA((rows // TILE,))]


def prep(order, tile_live, x_values, step):
    rows = x_values.shape[0]
    return call(
        functools.partial(prep_body, step),
        sds((rows, BLOCK), BF16),
        smem(2) + hbm(1),
        "prep",
        nbytes=4 * rows * BLOCK,
        scratch_shapes=block_scratch(rows),
    )(order, tile_live, x_values)


def prep_general(x_values, tile_live, chosen, core, own):
    rows = x_values.shape[0]
    tiles = BLOCK // TILE
    x = lax.dynamic_slice_in_dim(x_values, chosen * BLOCK, BLOCK, 1)
    live = lax.dynamic_slice_in_dim(tile_live, chosen * tiles, tiles, 1).astype(BF16)
    x = x.reshape(rows // TILE, TILE, tiles, TILE) * live[:, None, :, None]
    x = x.reshape(rows, HALF // own, 2, own)
    mine = lax.dynamic_index_in_dim(x, core, 2, keepdims=False)
    other = lax.dynamic_index_in_dim(x, 1 - core, 2, keepdims=False)
    return jnp.concatenate([mine.reshape(rows, HALF), other.reshape(rows, HALF)], axis=1)


def stack_rows(rows):
    if len(rows) < TAIL:
        rows = rows + [jnp.zeros((TAIL - len(rows), TILE), F32)]
    return jnp.concatenate(rows, axis=0)


def split_rows(curvs):
    rows = []
    for curv in curvs:
        high = curv.astype(BF16).astype(F32)
        rows += [high, curv - high]
    return stack_rows(rows).astype(BF16)


def block(k):
    return slice(k * C, (k + 1) * C)


def half_sums(res_t, spread_ref, x_ref, start, first, g_ref, so_far=None):
    rows = spread_ref.shape[0]
    grad = jnp.dot(res_t, x_ref[start : start + rows, first : first + HALF], preferred_element_type=F32)
    curvs = []
    for k in range(NB):
        lanes = slice(first + k * TILE, first + (k + 1) * TILE)
        acc = jnp.zeros((8, TILE), F32)
        for r, here in tiles_of(rows):
            x = x_ref[start + r * TILE : start + (r + 1) * TILE, lanes].astype(F32)
            term = x * x * spread_ref[here, :]
            acc = acc + jnp.sum(term.reshape(TILE // 8, 8, TILE), axis=0)
        curv = jnp.sum(acc, axis=0, keepdims=True)
        part = grad[:, k * TILE : (k + 1) * TILE]
        if so_far is not None:
            part, curv = part + so_far[block(k), :], curv + so_far[NB * C + k : NB * C + k + 1, :]
        g_ref[block(k), :] = part.astype(g_ref.dtype)
        curvs.append(curv)
    g_ref[NB * C : NB * C + TAIL, :] = split_rows(curvs) if g_ref.dtype == BF16 else stack_rows(curvs)


def soft_rows(score, labels, here, res_ref, spread_ref):
    top = jnp.max(score, axis=0, keepdims=True)
    expo = jnp.exp(score - top)
    prob = expo / jnp.sum(expo, axis=0, keepdims=True)
    classes = lax.broadcasted_iota(jnp.int32, (C, TILE), 0)
    residual = prob - jnp.where(labels == classes, 1.0, 0.0)
    spread = (1.0 - jnp.sum(prob * prob, axis=0, keepdims=True)).astype(BF16).astype(F32)
    res_ref[:, here] = residual.astype(BF16)
    spread_ref[here, :] = jnp.broadcast_to(spread, (TILE, TILE)).T


def tiles_of(rows):
    return [(r, slice(r * TILE, (r + 1) * TILE)) for r in range(rows // TILE)]


def keep_score(score, r, low_ref, high_ref):
    per = low_ref.shape[1] // TILE
    (low_ref if r < per else high_ref)[:, r % per * TILE : (r % per + 1) * TILE] = score


def first_body(
    order_hbm, live_hbm, margins_hbm, lab_hbm, coef_hbm, x_hbm,
    x_ref, low_ref, high_ref, res_ref, spread_ref, g_ref, first_ref, other_ref, first_send, other_send, *rest,
):
    same_refs = rest[: STEPS - 1]
    order, live, margins, labels, coef, small, buf, sems = rest[STEPS - 1 :]
    loads = [
        pltpu.make_async_copy(src, dst, small.at[i])
        for i, (src, dst) in enumerate(
            ((order_hbm, order), (live_hbm, live), (margins_hbm, margins), (lab_hbm, labels), (coef_hbm, coef))
        )
    ]
    for load in loads:
        load.start()
    loads[0].wait()
    chosen, core = order[0, 0], lax.axis_index("ex") % 2
    copies = load_block(chosen, x_hbm, buf, sems)
    for load in loads[1:]:
        load.wait()
    for r, here in tiles_of(margins.shape[0]):
        score = margins[here, :].astype(F32).T
        keep_score(score, r, low_ref, high_ref)
        soft_rows(score, labels[r : r + 1, :], here, res_ref, spread_ref)
    for block, keep, send in ((chosen, first_ref, first_send), (1 - chosen, other_ref, other_send)):
        rows = coef[block].T
        keep[...] = rows
        send[...] = rows.astype(BF16)
    for step, same_ref in enumerate(same_refs):
        same_ref[...] = jnp.full((8, TILE), (order[0, step + 1] == chosen).astype(F32))
    for r, copy in enumerate(copies):
        copy.wait()
        mask_tile(r, chosen, core, live, buf, x_ref)
    half_sums(res_ref[...], spread_ref, x_ref, 0, HALF, g_ref)


def first_general_body(margins_ref, lab_ref, x_ref, low_ref, high_ref, res_ref, spread_ref, g_ref):
    for r, here in tiles_of(margins_ref.shape[0]):
        score = margins_ref[here, :].astype(F32).T
        keep_score(score, r, low_ref, high_ref)
        soft_rows(score, lab_ref[r : r + 1, :], here, res_ref, spread_ref)
    half_sums(res_ref[...], spread_ref, x_ref, 0, HALF, g_ref)


def next_rows(start, before_ref, part_ref, got_ref, lab_ref, score_ref, res_ref, spread_ref):
    for r, here in tiles_of(before_ref.shape[1]):
        score = before_ref[:, here] + (part_ref[:, here].astype(F32) + got_ref[:, here].astype(F32))
        score_ref[:, here] = score
        row = start // TILE + r
        soft_rows(score, lab_ref[row : row + 1, :], here, res_ref, spread_ref)


def next_low_body(before_ref, part_ref, got_ref, lab_ref, x_ref, score_ref, g_ref, own_ref, res_ref, spread_ref):
    next_rows(0, before_ref, part_ref, got_ref, lab_ref, score_ref, res_ref, spread_ref)
    half_sums(res_ref[...], spread_ref, x_ref, 0, HALF, g_ref)
    half_sums(res_ref[...], spread_ref, x_ref, 0, 0, own_ref)


def next_high_body(before_ref, part_ref, got_ref, lab_ref, x_ref, so_far, score_ref, res_ref, spread_ref, g_ref):
    start = before_ref.shape[1]
    next_rows(start, before_ref, part_ref, got_ref, lab_ref, score_ref, res_ref, spread_ref)
    half_sums(res_ref[...], spread_ref, x_ref, start, HALF, g_ref, so_far)


def last_low_body(before_ref, part_ref, got_ref, out_ref):
    for _, here in tiles_of(before_ref.shape[1]):
        score = before_ref[:, here] + (part_ref[:, here].astype(F32) + got_ref[:, here].astype(F32))
        out_ref[here, :] = score.T


def last_high_body(low_ref, before_ref, part_ref, got_ref, out_hbm, buf, sems):
    rows = before_ref.shape[1]
    copies = [
        pltpu.make_async_copy(ref, out_hbm.at[pl.ds(i * rows, rows)], sems.at[i])
        for i, ref in enumerate((low_ref, buf))
    ]
    copies[0].start()
    last_low_body(before_ref, part_ref, got_ref, buf)
    copies[1].start()
    for copy in copies:
        copy.wait()


def own_body(res_ref, spread_ref, x_ref, g_ref):
    half_sums(res_ref[...], spread_ref, x_ref, 0, 0, g_ref)


def own_high_body(res_ref, spread_ref, x_ref, so_far, g_ref):
    half_sums(res_ref[...], spread_ref, x_ref, spread_ref.shape[0], 0, g_ref, so_far)


def pair_body(own_ref, got_ref, p_ref, q_ref):
    tail = got_ref[NB * C : NB * C + TAIL, :].astype(F32)
    curvs = []
    for k in range(NB):
        total = own_ref[block(k), :] + got_ref[block(k), :].astype(F32)
        ref, j = (p_ref, k) if k < PB else (q_ref, k - PB)
        ref[block(j), :] = total.astype(BF16)
        curvs.append(own_ref[NB * C + k : NB * C + k + 1, :] + tail[2 * k : 2 * k + 1] + tail[2 * k + 1 : 2 * k + 2])
    p_ref[PB * C : PB * C + TAIL, :] = split_rows(curvs[:PB])
    q_ref[(NB - PB) * C : (NB - PB) * C + TAIL, :] = split_rows(curvs[PB:])


def sum_of(mine_ref, got_ref, rows):
    return mine_ref[rows, :].astype(F32) + got_ref[rows, :].astype(F32)


def curvs_of(mine_ref, got_ref):
    n = mine_ref.shape[0] // C
    tail = sum_of(mine_ref, got_ref, slice(n * C, n * C + TAIL))
    return [tail[2 * j : 2 * j + 1] + tail[2 * j + 1 : 2 * j + 2] for j in range(n)]


def hop_body(mine_ref, got_ref, out_ref):
    curvs = curvs_of(mine_ref, got_ref)
    for j in range(len(curvs)):
        out_ref[block(j), :] = sum_of(mine_ref, got_ref, block(j)).astype(BF16)
    out_ref[len(curvs) * C : len(curvs) * C + TAIL, :] = split_rows(curvs)


def place_body(far_ref, near_ref, coef_ref, out_ref):
    place = lax.axis_index("ex") // 2
    out_ref[place] = coef_ref[...]
    out_ref[jnp.bitwise_xor(place, 2)] = far_ref[...].astype(F32)
    out_ref[jnp.bitwise_xor(place, 1)] = near_ref[0].astype(F32)
    out_ref[jnp.bitwise_xor(place, 3)] = near_ref[1].astype(F32)


def totals(p_ref, gp_ref, q_ref, gq_ref):
    both = []
    for pair in ((p_ref, gp_ref), (q_ref, gq_ref)):
        both += [(sum_of(*pair, block(j)), curv) for j, curv in enumerate(curvs_of(*pair))]
    return both


def step_coef(count, grad, curv, old):
    inverse = 1.0 / (curv / count + ridge)
    shifted = old - grad * (inverse / count)
    limit = lasso * inverse
    return shifted - jnp.clip(shifted, -limit, limit)


def prox_first_body(count, p_ref, gp_ref, q_ref, gq_ref, old_ref, new_ref, delta_ref):
    for k, (grad, curv) in enumerate(totals(p_ref, gp_ref, q_ref, gq_ref)):
        old = old_ref[k]
        new = step_coef(count, grad, curv, old)
        new_ref[k] = new
        delta_ref[:, k * TILE : (k + 1) * TILE] = (new - old).astype(BF16)


def prox_body(count, same_ref, p_ref, gp_ref, q_ref, gq_ref, old0_ref, old1_ref, new0_ref, new1_ref, delta_ref):
    same = jnp.broadcast_to(same_ref[0:1, :], (C, TILE)) > 0.5
    for k, (grad, curv) in enumerate(totals(p_ref, gp_ref, q_ref, gq_ref)):
        old0, old1 = old0_ref[k], old1_ref[k]
        old = jnp.where(same, old0, old1)
        new = step_coef(count, grad, curv, old)
        new0_ref[k] = jnp.where(same, new, old0)
        new1_ref[k] = jnp.where(same, old1, new)
        delta_ref[:, k * TILE : (k + 1) * TILE] = (new - old).astype(BF16)


def coef_body(order_ref, first_ref, other_ref, out_ref):
    place = lax.axis_index("ex") // 2
    block = order_ref[0, 0]
    out_ref[block] = first_ref[place].T
    out_ref[1 - block] = other_ref[place].T


def contrib(x_ref, first, delta_ref):
    return lax.dot_general(
        x_ref[:, first : first + HALF], delta_ref[...],
        (((1,), (1,)), ((), ())), preferred_element_type=F32,
    )


def mine_body(x_ref, delta_ref, part_ref):
    part_ref[...] = contrib(x_ref, 0, delta_ref)


def change_body(carried, x_ref, part_ref, delta_ref, *refs):
    errors, (a_ref, b_ref, *keep) = refs[:carried], refs[carried:]
    part = part_ref[...] + contrib(x_ref, HALF, delta_ref)
    rows = x_ref.shape[0]
    for _, here in tiles_of(rows):
        low = here.stop <= rows // 2
        at = here if low else slice(here.start - rows // 2, here.stop - rows // 2)
        full = part[here, :].T
        for e_ref in errors[0::2] if low else errors[1::2]:
            full = full + e_ref[:, at]
        sent = full.astype(BF16)
        (a_ref if low else b_ref)[:, at] = sent
        if keep:
            keep[0 if low else 1][:, at] = full - sent.astype(F32)


def meet_body(share, mine_ref, got_ref, out_ref, *error_refs):
    total = mine_ref[...].astype(F32) + got_ref[...].astype(F32)
    sent = total.astype(BF16)
    out_ref[...] = sent
    for error_ref in error_refs:
        error_ref[...] = share * (total - sent.astype(F32))


def bits(n):
    return [1 << i for i in range(n.bit_length() - 1)]


def swap(x, move):
    n_feat, n_ex = lax.axis_size("feat"), lax.axis_size("ex")
    pairs = []
    for f in range(n_feat):
        for e in range(n_ex):
            to_f, to_e = move(f, e)
            pairs.append((f * n_ex + e, to_f * n_ex + to_e))
    return lax.ppermute(x, ("feat", "ex"), pairs)


def swap_core(x):
    return swap(x, lambda f, e: (f, e ^ 1))


def sum_over_feat(a, b, last):
    order = bits(lax.axis_size("feat"))
    errors, pair = [], 1
    for n in range(len(order)):
        got_a = swap(a, lambda f, e, n=n: (f ^ order[n], e))
        got_b = swap(b, lambda f, e, n=n: (f ^ order[-1 - n], e))
        if n == len(order) - 1:
            return (a, got_a, b, got_b), errors
        pair *= 2
        shapes = (sds(a.shape, BF16),) + (() if last else (sds(a.shape, F32),))
        meet = functools.partial(meet_body, 1.0 / pair)
        a, *ea = call(meet, shapes, vmem(2), "meet_a")(a, got_a)
        b, *eb = call(meet, shapes, vmem(2), "meet_b")(b, got_b)
        errors += ea + eb


def gather_blocks(coef, order, z_bits):
    n_z = 1 << len(z_bits)
    far = jnp.swapaxes(coef, 1, 2)[:, None]
    for bit in z_bits:
        far = jnp.concatenate([far, swap(far, lambda f, e, bit=bit: (f, e ^ bit))], axis=1)
    place = lax.axis_index("ex") // 2
    far = jnp.take(far, jnp.bitwise_xor(jnp.arange(n_z), place), axis=1)
    old = far.transpose(0, 2, 1, 3).reshape(2, C, NB, TILE).transpose(0, 2, 1, 3)
    block = order[0, 0]
    return [lax.dynamic_index_in_dim(old, i, 0, keepdims=False) for i in (block, 1 - block)]


def own_blocks(olds, order, own):
    place = lax.axis_index("ex") // 2
    rows = []
    for old in olds:
        old = old.transpose(1, 0, 2).reshape(C, HALF)
        rows.append(lax.dynamic_slice_in_dim(old, place * own, own, 1))
    first = order[0, 0] == 0
    both = [jnp.where(first, rows[0], rows[1]), jnp.where(first, rows[1], rows[0])]
    return jnp.swapaxes(jnp.stack(both), 1, 2)


def local(x_values, tile_live, labels, margins, coef, order):
    rows = x_values.shape[0]
    n_ex = lax.axis_size("ex")
    count = float(rows * n_ex)
    own = coef.shape[1]
    core = lax.axis_index("ex") % 2
    aligned = own == TILE and n_ex == 2 * NB
    labels = labels.reshape(rows // TILE, TILE)
    order = order.reshape(1, STEPS)
    z_bits = [2 * b for b in bits(n_ex // 2)]

    x_shape = sds((rows, BLOCK), BF16)
    soft_shapes = (
        sds((C, rows // 2), F32), sds((C, rows // 2), F32),
        sds((C, rows), BF16), sds((rows, TILE), F32), sds((NB * C + TAIL, TILE), BF16),
    )
    g_shape = sds((NB * C + TAIL, TILE), F32)
    score_shape, g_sent_shape = soft_shapes[0], soft_shapes[-1]
    rows_shapes = (sds((C, rows // 2), BF16), sds((rows // 2, TILE), F32))
    old_shape, delta_shape = sds((NB, C, TILE), F32), sds((C, HALF), BF16)
    part_shape, half = sds((rows, C), F32), (C, rows // 2)
    own_shape, send_shape, same_shape = sds((C, TILE), F32), sds((C, TILE), BF16), sds((8, TILE), F32)
    flops, nbytes = 2 * rows * HALF * C, 1 << 20

    p_shape, q_shape = sds((PB * C + TAIL, TILE), BF16), sds(((NB - PB) * C + TAIL, TILE), BF16)

    if aligned:
        x, low, high, res_t, spread, g_other, *rest = call(
            first_body,
            (x_shape,) + soft_shapes + (own_shape,) * 2 + (send_shape,) * 2 + (same_shape,) * (STEPS - 1),
            hbm(6), "soft_first", flops, nbytes,
            scratch_shapes=[
                pltpu.SMEM(order.shape, jnp.int32),
                pltpu.SMEM(tile_live.shape, jnp.int32),
                pltpu.VMEM(margins.shape, BF16),
                pltpu.VMEM(labels.shape, jnp.int32),
                pltpu.VMEM(coef.shape, F32),
                pltpu.SemaphoreType.DMA((5,)),
            ] + block_scratch(rows),
        )(order, tile_live, margins, labels, coef, x_values)
        blocks, sends, same = rest[:2], rest[2:4], rest[4:]
    else:
        x = prep_general(x_values, tile_live, order[0, 0], core, own)
        low, high, res_t, spread, g_other = call(
            first_general_body, soft_shapes, vmem(3), "soft_first", flops, nbytes
        )(margins, labels, x)
        blocks = gather_blocks(coef, order, z_bits)
        same = [
            jnp.full((8, TILE), (order[0, step] == order[0, 0]).astype(F32)) for step in range(1, STEPS)
        ]

    errors = []
    for step in range(STEPS):
        if step > 0:
            x = following
            a, got_a, b, got_b = halves
            low, g_other, g_own = call(
                next_low_body, (score_shape, g_shape, g_shape), vmem(5), "soft_low", flops, nbytes,
                scratch_shapes=list(rows_shapes),
            )(low, a, got_a, labels, x)
            high, res_t, spread, g_other = call(
                next_high_body, (score_shape, *rows_shapes, g_sent_shape), vmem(6), "soft_high", flops // 2, nbytes
            )(high, b, got_b, labels, x, g_other)
            got = swap_core(g_other)
            g_own = call(own_high_body, g_shape, vmem(4), "own", flops // 2, nbytes)(res_t, spread, x, g_own)
        else:
            got = swap_core(g_other)
            g_own = call(own_body, g_shape, vmem(3), "own", flops, nbytes)(res_t, spread, x)
        p, q = call(pair_body, (p_shape, q_shape), vmem(2), "pair")(g_own, got)
        carry = aligned and step < 2
        if carry:
            p, q, send = lax.optimization_barrier((p, q, sends[step]))
        for n, bit in enumerate(z_bits):
            got_p = swap(p, lambda f, e, bit=bit: (f, e ^ bit))
            got_q = swap(q, lambda f, e, bit=bit: (f, e ^ bit))
            if n < len(z_bits) - 1:
                if carry:
                    far = swap(send, lambda f, e: (f, e ^ z_bits[1]))
                p = call(hop_body, p_shape, vmem(2), "hop_p")(p, got_p)
                q = call(hop_body, q_shape, vmem(2), "hop_q")(q, got_q)
        if carry:
            near = swap(jnp.stack([send, far]), lambda f, e: (f, e ^ z_bits[0]))
            old = call(place_body, old_shape, vmem(3), "place")(far, near, blocks[step])
        elif step < 2:
            old = blocks[step]
        sums = (p, got_p, q, got_q)
        if step < STEPS - 1 and aligned:
            following = prep(order, tile_live, x_values, step + 1)
            *sums, following = lax.optimization_barrier((*sums, following))
        elif step < STEPS - 1:
            following = prep_general(x_values, tile_live, order[0, step + 1], core, own)
        if step == 0:
            first, delta = call(
                functools.partial(prox_first_body, count), (old_shape, delta_shape), vmem(5), "prox"
            )(*sums, old)
        else:
            first, other, delta = call(
                functools.partial(prox_body, count), (old_shape, old_shape, delta_shape), vmem(7), "prox"
            )(same[step - 1], *sums, first, old if step == 1 else other)
        got = swap_core(delta)
        part = call(mine_body, part_shape, vmem(2), "mine", flops, nbytes)(x, delta)
        last = step == STEPS - 1
        shapes = (sds(half, BF16),) * 2 + (() if last else (sds(half, F32),) * 2)
        a, b, *kept = call(
            functools.partial(change_body, len(errors)), shapes, vmem(3 + len(errors)), "change", flops, nbytes,
        )(x, part, got, *errors)
        halves, errors = sum_over_feat(a, b, last)
        errors = kept + errors
    a, got_a, b, got_b = halves
    half = sds((rows // 2, C), F32)
    low = call(last_low_body, half, vmem(3), "last_low", flops // 4, nbytes)(low, a, got_a)
    score = pl.pallas_call(
        last_high_body,
        out_shape=jax.ShapeDtypeStruct((rows, C), F32),
        in_specs=vmem(4),
        out_specs=pl.BlockSpec(memory_space=pltpu.HBM),
        scratch_shapes=[pltpu.VMEM(half.shape, F32), pltpu.SemaphoreType.DMA((2,))],
        name="last_high",
        compiler_params=pltpu.CompilerParams(vmem_limit_bytes=16 << 20),
    )(*(pltpu.with_memory_space_constraint(v, pltpu.VMEM) for v in (low, high, b, got_b)))
    if aligned:
        coef = call(coef_body, sds(coef.shape, F32), smem(1) + vmem(2), "coef_out")(order, first, other)
    else:
        coef = own_blocks((first, other), order, own)
    return score, coef


def solution(mesh):
    return jax.shard_map(
        local,
        mesh=mesh,
        in_specs=(
            P("ex", "feat"),
            P("ex", "feat"),
            P("ex"),
            P("ex", None),
            P(None, ("feat", "ex"), None),
            P(None, "feat"),
        ),
        out_specs=(P("ex", None), P(None, ("feat", "ex"), None)),
        check_vma=False,
    )
```

```python
import functools

import jax
import jax.numpy as jnp
from jax import lax
from jax.experimental import pallas as pl
from jax.experimental.pallas import tpu as pltpu
from jax.sharding import PartitionSpec as P

C = 128
BLOCK = 1024
STEPS = 3
HALF = BLOCK // 2
TILE = 128
NB = HALF // TILE
PB = NB // 2
TAIL = 8

ridge = 0.002
lasso = 0.005

F32 = jnp.float32
BF16 = jnp.bfloat16


def vmem(n):
    return [pl.BlockSpec(memory_space=pltpu.VMEM)] * n


def smem(n):
    return [pl.BlockSpec(memory_space=pltpu.SMEM)] * n


def hbm(n):
    return [pl.BlockSpec(memory_space=pltpu.HBM)] * n


def call(body, outs, in_specs, name, flops=0, nbytes=0, **kw):
    f = pl.pallas_call(
        body,
        out_shape=outs,
        in_specs=in_specs,
        out_specs=jax.tree.map(lambda _: pl.BlockSpec(memory_space=pltpu.VMEM), outs),
        name=name,
        cost_estimate=pl.CostEstimate(flops=flops, bytes_accessed=nbytes, transcendentals=0),
        compiler_params=pltpu.CompilerParams(vmem_limit_bytes=16 << 20),
        **kw,
    )

    def run(*args):
        return f(
            *(
                x
                if spec.memory_space == pltpu.SMEM
                else pltpu.with_memory_space_constraint(x, spec.memory_space)
                for spec, x in zip(in_specs, args, strict=True)
            )
        )

    return run


def sds(shape, dtype):
    return pltpu.VMEM(shape, dtype)


def load_block(chosen, x_ref, buf, sems):
    copies = [
        pltpu.make_async_copy(
            x_ref.at[pl.ds(r * TILE, TILE), pl.ds(pl.multiple_of(chosen * BLOCK, BLOCK), BLOCK)],
            buf.at[pl.ds(r * TILE, TILE)],
            sems.at[r],
        )
        for r in range(buf.shape[0] // TILE)
    ]
    for copy in copies:
        copy.start()
    return copies


def mask_tile(r, chosen, core, live_ref, buf, out_ref):
    tiles = BLOCK // TILE
    here = pl.ds(r * TILE, TILE)
    for k in range(tiles):
        col = 2 * (k % NB) + (core if k < NB else 1 - core)
        live = live_ref[r, chosen * tiles + col].astype(F32)
        tile = buf[here, pl.ds(pl.multiple_of(col * TILE, TILE), TILE)]
        out_ref[here, k * TILE : (k + 1) * TILE] = (tile.astype(F32) * live).astype(BF16)


def prep_body(step, order_ref, live_ref, x_ref, out_ref, buf, sems):
    chosen, core = order_ref[0, step], lax.axis_index("ex") % 2
    copies = load_block(chosen, x_ref, buf, sems)
    for r, copy in enumerate(copies):
        copy.wait()
        mask_tile(r, chosen, core, live_ref, buf, out_ref)


def block_scratch(rows):
    return [pltpu.VMEM((rows, BLOCK), BF16), pltpu.SemaphoreType.DMA((rows // TILE,))]


def prep(order, tile_live, x_values, step):
    rows = x_values.shape[0]
    return call(
        functools.partial(prep_body, step),
        sds((rows, BLOCK), BF16),
        smem(2) + hbm(1),
        "prep",
        nbytes=4 * rows * BLOCK,
        scratch_shapes=block_scratch(rows),
    )(order, tile_live, x_values)


def prep_general(x_values, tile_live, chosen, core, own):
    rows = x_values.shape[0]
    tiles = BLOCK // TILE
    x = lax.dynamic_slice_in_dim(x_values, chosen * BLOCK, BLOCK, 1)
    live = lax.dynamic_slice_in_dim(tile_live, chosen * tiles, tiles, 1).astype(BF16)
    x = x.reshape(rows // TILE, TILE, tiles, TILE) * live[:, None, :, None]
    x = x.reshape(rows, HALF // own, 2, own)
    mine = lax.dynamic_index_in_dim(x, core, 2, keepdims=False)
    other = lax.dynamic_index_in_dim(x, 1 - core, 2, keepdims=False)
    return jnp.concatenate([mine.reshape(rows, HALF), other.reshape(rows, HALF)], axis=1)


def stack_rows(rows):
    if len(rows) < TAIL:
        rows = rows + [jnp.zeros((TAIL - len(rows), TILE), F32)]
    return jnp.concatenate(rows, axis=0)


def split_rows(curvs):
    rows = []
    for curv in curvs:
        high = curv.astype(BF16).astype(F32)
        rows += [high, curv - high]
    return stack_rows(rows).astype(BF16)


def block(k):
    return slice(k * C, (k + 1) * C)


def half_sums(res_t, spread_ref, x_ref, start, first, g_ref, so_far=None):
    rows = spread_ref.shape[0]
    grad = jnp.dot(res_t, x_ref[start : start + rows, first : first + HALF], preferred_element_type=F32)
    curvs = []
    for k in range(NB):
        lanes = slice(first + k * TILE, first + (k + 1) * TILE)
        acc = jnp.zeros((8, TILE), F32)
        for r, here in tiles_of(rows):
            x = x_ref[start + r * TILE : start + (r + 1) * TILE, lanes].astype(F32)
            term = x * x * spread_ref[here, :]
            acc = acc + jnp.sum(term.reshape(TILE // 8, 8, TILE), axis=0)
        curv = jnp.sum(acc, axis=0, keepdims=True)
        part = grad[:, k * TILE : (k + 1) * TILE]
        if so_far is not None:
            part, curv = part + so_far[block(k), :], curv + so_far[NB * C + k : NB * C + k + 1, :]
        g_ref[block(k), :] = part.astype(g_ref.dtype)
        curvs.append(curv)
    g_ref[NB * C : NB * C + TAIL, :] = split_rows(curvs) if g_ref.dtype == BF16 else stack_rows(curvs)


def soft_rows(score, labels, here, res_ref, spread_ref):
    top = jnp.max(score, axis=0, keepdims=True)
    expo = jnp.exp(score - top)
    prob = expo / jnp.sum(expo, axis=0, keepdims=True)
    classes = lax.broadcasted_iota(jnp.int32, (C, TILE), 0)
    residual = prob - jnp.where(labels == classes, 1.0, 0.0)
    spread = (1.0 - jnp.sum(prob * prob, axis=0, keepdims=True)).astype(BF16).astype(F32)
    res_ref[:, here] = residual.astype(BF16)
    spread_ref[here, :] = jnp.broadcast_to(spread, (TILE, TILE)).T


def tiles_of(rows):
    return [(r, slice(r * TILE, (r + 1) * TILE)) for r in range(rows // TILE)]


def keep_score(score, r, low_ref, high_ref):
    per = low_ref.shape[1] // TILE
    (low_ref if r < per else high_ref)[:, r % per * TILE : (r % per + 1) * TILE] = score


def first_body(
    order_hbm, live_hbm, margins_hbm, lab_hbm, coef_hbm, x_hbm,
    x_ref, low_ref, high_ref, res_ref, spread_ref, g_ref, first_ref, other_ref, first_send, other_send, *rest,
):
    same_refs = rest[: STEPS - 1]
    order, live, margins, labels, coef, small, buf, sems = rest[STEPS - 1 :]
    loads = [
        pltpu.make_async_copy(src, dst, small.at[i])
        for i, (src, dst) in enumerate(
            ((order_hbm, order), (live_hbm, live), (margins_hbm, margins), (lab_hbm, labels), (coef_hbm, coef))
        )
    ]
    for load in loads:
        load.start()
    loads[0].wait()
    chosen, core = order[0, 0], lax.axis_index("ex") % 2
    copies = load_block(chosen, x_hbm, buf, sems)
    for load in loads[1:]:
        load.wait()
    for r, here in tiles_of(margins.shape[0]):
        score = margins[here, :].astype(F32).T
        keep_score(score, r, low_ref, high_ref)
        soft_rows(score, labels[r : r + 1, :], here, res_ref, spread_ref)
    for block, keep, send in ((chosen, first_ref, first_send), (1 - chosen, other_ref, other_send)):
        rows = coef[block].T
        keep[...] = rows
        send[...] = rows.astype(BF16)
    for step, same_ref in enumerate(same_refs):
        same_ref[...] = jnp.full((8, TILE), (order[0, step + 1] == chosen).astype(F32))
    for r, copy in enumerate(copies):
        copy.wait()
        mask_tile(r, chosen, core, live, buf, x_ref)
    half_sums(res_ref[...], spread_ref, x_ref, 0, HALF, g_ref)


def first_general_body(margins_ref, lab_ref, x_ref, low_ref, high_ref, res_ref, spread_ref, g_ref):
    for r, here in tiles_of(margins_ref.shape[0]):
        score = margins_ref[here, :].astype(F32).T
        keep_score(score, r, low_ref, high_ref)
        soft_rows(score, lab_ref[r : r + 1, :], here, res_ref, spread_ref)
    half_sums(res_ref[...], spread_ref, x_ref, 0, HALF, g_ref)


def next_rows(start, before_ref, part_ref, got_ref, lab_ref, score_ref, res_ref, spread_ref):
    for r, here in tiles_of(before_ref.shape[1]):
        score = before_ref[:, here] + (part_ref[:, here].astype(F32) + got_ref[:, here].astype(F32))
        score_ref[:, here] = score
        row = start // TILE + r
        soft_rows(score, lab_ref[row : row + 1, :], here, res_ref, spread_ref)


def next_low_body(before_ref, part_ref, got_ref, lab_ref, x_ref, score_ref, g_ref, own_ref, res_ref, spread_ref):
    next_rows(0, before_ref, part_ref, got_ref, lab_ref, score_ref, res_ref, spread_ref)
    half_sums(res_ref[...], spread_ref, x_ref, 0, HALF, g_ref)
    half_sums(res_ref[...], spread_ref, x_ref, 0, 0, own_ref)


def next_high_body(before_ref, part_ref, got_ref, lab_ref, x_ref, so_far, score_ref, res_ref, spread_ref, g_ref):
    start = before_ref.shape[1]
    next_rows(start, before_ref, part_ref, got_ref, lab_ref, score_ref, res_ref, spread_ref)
    half_sums(res_ref[...], spread_ref, x_ref, start, HALF, g_ref, so_far)


def last_low_body(before_ref, part_ref, got_ref, out_ref):
    for _, here in tiles_of(before_ref.shape[1]):
        score = before_ref[:, here] + (part_ref[:, here].astype(F32) + got_ref[:, here].astype(F32))
        out_ref[here, :] = score.T


def last_high_body(low_ref, before_ref, part_ref, got_ref, out_hbm, buf, sems):
    rows = before_ref.shape[1]
    copies = [
        pltpu.make_async_copy(ref, out_hbm.at[pl.ds(i * rows, rows)], sems.at[i])
        for i, ref in enumerate((low_ref, buf))
    ]
    copies[0].start()
    last_low_body(before_ref, part_ref, got_ref, buf)
    copies[1].start()
    for copy in copies:
        copy.wait()


def own_body(res_ref, spread_ref, x_ref, g_ref):
    half_sums(res_ref[...], spread_ref, x_ref, 0, 0, g_ref)


def own_high_body(res_ref, spread_ref, x_ref, so_far, g_ref):
    half_sums(res_ref[...], spread_ref, x_ref, spread_ref.shape[0], 0, g_ref, so_far)


def pair_body(own_ref, got_ref, p_ref, q_ref):
    tail = got_ref[NB * C : NB * C + TAIL, :].astype(F32)
    curvs = []
    for k in range(NB):
        total = own_ref[block(k), :] + got_ref[block(k), :].astype(F32)
        ref, j = (p_ref, k) if k < PB else (q_ref, k - PB)
        ref[block(j), :] = total.astype(BF16)
        curvs.append(own_ref[NB * C + k : NB * C + k + 1, :] + tail[2 * k : 2 * k + 1] + tail[2 * k + 1 : 2 * k + 2])
    p_ref[PB * C : PB * C + TAIL, :] = split_rows(curvs[:PB])
    q_ref[(NB - PB) * C : (NB - PB) * C + TAIL, :] = split_rows(curvs[PB:])


def sum_of(mine_ref, got_ref, rows):
    return mine_ref[rows, :].astype(F32) + got_ref[rows, :].astype(F32)


def curvs_of(mine_ref, got_ref):
    n = mine_ref.shape[0] // C
    tail = sum_of(mine_ref, got_ref, slice(n * C, n * C + TAIL))
    return [tail[2 * j : 2 * j + 1] + tail[2 * j + 1 : 2 * j + 2] for j in range(n)]


def hop_body(mine_ref, got_ref, out_ref):
    curvs = curvs_of(mine_ref, got_ref)
    for j in range(len(curvs)):
        out_ref[block(j), :] = sum_of(mine_ref, got_ref, block(j)).astype(BF16)
    out_ref[len(curvs) * C : len(curvs) * C + TAIL, :] = split_rows(curvs)


def place_body(far_ref, near_ref, coef_ref, out_ref):
    place = lax.axis_index("ex") // 2
    out_ref[place] = coef_ref[...]
    out_ref[jnp.bitwise_xor(place, 2)] = far_ref[...].astype(F32)
    out_ref[jnp.bitwise_xor(place, 1)] = near_ref[0].astype(F32)
    out_ref[jnp.bitwise_xor(place, 3)] = near_ref[1].astype(F32)


def totals(p_ref, gp_ref, q_ref, gq_ref):
    both = []
    for pair in ((p_ref, gp_ref), (q_ref, gq_ref)):
        both += [(sum_of(*pair, block(j)), curv) for j, curv in enumerate(curvs_of(*pair))]
    return both


def step_coef(count, grad, curv, old):
    inverse = 1.0 / (curv / count + ridge)
    shifted = old - grad * (inverse / count)
    limit = lasso * inverse
    return shifted - jnp.clip(shifted, -limit, limit)


def prox_first_body(count, p_ref, gp_ref, q_ref, gq_ref, old_ref, new_ref, delta_ref):
    for k, (grad, curv) in enumerate(totals(p_ref, gp_ref, q_ref, gq_ref)):
        old = old_ref[k]
        new = step_coef(count, grad, curv, old)
        new_ref[k] = new
        delta_ref[:, k * TILE : (k + 1) * TILE] = (new - old).astype(BF16)


def prox_body(count, same_ref, p_ref, gp_ref, q_ref, gq_ref, old0_ref, old1_ref, new0_ref, new1_ref, delta_ref):
    same = jnp.broadcast_to(same_ref[0:1, :], (C, TILE)) > 0.5
    for k, (grad, curv) in enumerate(totals(p_ref, gp_ref, q_ref, gq_ref)):
        old0, old1 = old0_ref[k], old1_ref[k]
        old = jnp.where(same, old0, old1)
        new = step_coef(count, grad, curv, old)
        new0_ref[k] = jnp.where(same, new, old0)
        new1_ref[k] = jnp.where(same, old1, new)
        delta_ref[:, k * TILE : (k + 1) * TILE] = (new - old).astype(BF16)


def coef_body(order_ref, first_ref, other_ref, out_ref):
    place = lax.axis_index("ex") // 2
    block = order_ref[0, 0]
    out_ref[block] = first_ref[place].T
    out_ref[1 - block] = other_ref[place].T


def contrib(x_ref, first, delta_ref):
    return lax.dot_general(
        x_ref[:, first : first + HALF], delta_ref[...],
        (((1,), (1,)), ((), ())), preferred_element_type=F32,
    )


def mine_body(x_ref, delta_ref, part_ref):
    part_ref[...] = contrib(x_ref, 0, delta_ref)


def change_body(carried, start, x_ref, part_ref, delta_ref, *refs):
    errors, (out_ref, *keep) = refs[:carried], refs[carried:]
    rows = out_ref.shape[1]
    part = part_ref[start : start + rows, :] + lax.dot_general(
        x_ref[start : start + rows, HALF:], delta_ref[...],
        (((1,), (1,)), ((), ())), preferred_element_type=F32,
    )
    for _, here in tiles_of(rows):
        full = part[here, :].T
        for e_ref in errors:
            full = full + e_ref[:, here]
        sent = full.astype(BF16)
        out_ref[:, here] = sent
        for e_ref in keep:
            e_ref[:, here] = full - sent.astype(F32)


def meet_body(share, mine_ref, got_ref, out_ref, *error_refs):
    total = mine_ref[...].astype(F32) + got_ref[...].astype(F32)
    sent = total.astype(BF16)
    out_ref[...] = sent
    for error_ref in error_refs:
        error_ref[...] = share * (total - sent.astype(F32))


def bits(n):
    return [1 << i for i in range(n.bit_length() - 1)]


def swap(x, move):
    n_feat, n_ex = lax.axis_size("feat"), lax.axis_size("ex")
    pairs = []
    for f in range(n_feat):
        for e in range(n_ex):
            to_f, to_e = move(f, e)
            pairs.append((f * n_ex + e, to_f * n_ex + to_e))
    return lax.ppermute(x, ("feat", "ex"), pairs)


def swap_core(x):
    return swap(x, lambda f, e: (f, e ^ 1))


def sum_over_feat(a, b, last):
    order = bits(lax.axis_size("feat"))
    errors, pair = [], 1
    for n in range(len(order)):
        got_a = swap(a, lambda f, e, n=n: (f ^ order[n], e))
        got_b = swap(b, lambda f, e, n=n: (f ^ order[-1 - n], e))
        if n == len(order) - 1:
            return (a, got_a, b, got_b), errors
        pair *= 2
        shapes = (sds(a.shape, BF16),) + (() if last else (sds(a.shape, F32),))
        meet = functools.partial(meet_body, 1.0 / pair)
        a, *ea = call(meet, shapes, vmem(2), "meet_a")(a, got_a)
        b, *eb = call(meet, shapes, vmem(2), "meet_b")(b, got_b)
        errors += ea + eb


def gather_blocks(coef, order, z_bits):
    n_z = 1 << len(z_bits)
    far = jnp.swapaxes(coef, 1, 2)[:, None]
    for bit in z_bits:
        far = jnp.concatenate([far, swap(far, lambda f, e, bit=bit: (f, e ^ bit))], axis=1)
    place = lax.axis_index("ex") // 2
    far = jnp.take(far, jnp.bitwise_xor(jnp.arange(n_z), place), axis=1)
    old = far.transpose(0, 2, 1, 3).reshape(2, C, NB, TILE).transpose(0, 2, 1, 3)
    block = order[0, 0]
    return [lax.dynamic_index_in_dim(old, i, 0, keepdims=False) for i in (block, 1 - block)]


def own_blocks(olds, order, own):
    place = lax.axis_index("ex") // 2
    rows = []
    for old in olds:
        old = old.transpose(1, 0, 2).reshape(C, HALF)
        rows.append(lax.dynamic_slice_in_dim(old, place * own, own, 1))
    first = order[0, 0] == 0
    both = [jnp.where(first, rows[0], rows[1]), jnp.where(first, rows[1], rows[0])]
    return jnp.swapaxes(jnp.stack(both), 1, 2)


def local(x_values, tile_live, labels, margins, coef, order):
    rows = x_values.shape[0]
    n_ex = lax.axis_size("ex")
    count = float(rows * n_ex)
    own = coef.shape[1]
    core = lax.axis_index("ex") % 2
    aligned = own == TILE and n_ex == 2 * NB
    labels = labels.reshape(rows // TILE, TILE)
    order = order.reshape(1, STEPS)
    z_bits = [2 * b for b in bits(n_ex // 2)]

    x_shape = sds((rows, BLOCK), BF16)
    soft_shapes = (
        sds((C, rows // 2), F32), sds((C, rows // 2), F32),
        sds((C, rows), BF16), sds((rows, TILE), F32), sds((NB * C + TAIL, TILE), BF16),
    )
    g_shape = sds((NB * C + TAIL, TILE), F32)
    score_shape, g_sent_shape = soft_shapes[0], soft_shapes[-1]
    rows_shapes = (sds((C, rows // 2), BF16), sds((rows // 2, TILE), F32))
    old_shape, delta_shape = sds((NB, C, TILE), F32), sds((C, HALF), BF16)
    part_shape, half = sds((rows, C), F32), (C, rows // 2)
    own_shape, send_shape, same_shape = sds((C, TILE), F32), sds((C, TILE), BF16), sds((8, TILE), F32)
    flops, nbytes = 2 * rows * HALF * C, 1 << 20

    p_shape, q_shape = sds((PB * C + TAIL, TILE), BF16), sds(((NB - PB) * C + TAIL, TILE), BF16)

    if aligned:
        x, low, high, res_t, spread, g_other, *rest = call(
            first_body,
            (x_shape,) + soft_shapes + (own_shape,) * 2 + (send_shape,) * 2 + (same_shape,) * (STEPS - 1),
            hbm(6), "soft_first", flops, nbytes,
            scratch_shapes=[
                pltpu.SMEM(order.shape, jnp.int32),
                pltpu.SMEM(tile_live.shape, jnp.int32),
                pltpu.VMEM(margins.shape, BF16),
                pltpu.VMEM(labels.shape, jnp.int32),
                pltpu.VMEM(coef.shape, F32),
                pltpu.SemaphoreType.DMA((5,)),
            ] + block_scratch(rows),
        )(order, tile_live, margins, labels, coef, x_values)
        blocks, sends, same = rest[:2], rest[2:4], rest[4:]
    else:
        x = prep_general(x_values, tile_live, order[0, 0], core, own)
        low, high, res_t, spread, g_other = call(
            first_general_body, soft_shapes, vmem(3), "soft_first", flops, nbytes
        )(margins, labels, x)
        blocks = gather_blocks(coef, order, z_bits)
        same = [
            jnp.full((8, TILE), (order[0, step] == order[0, 0]).astype(F32)) for step in range(1, STEPS)
        ]

    errors = []
    for step in range(STEPS):
        if step > 0:
            x = following
            a, got_a, b, got_b = halves
            low, g_other, g_own = call(
                next_low_body, (score_shape, g_shape, g_shape), vmem(5), "soft_low", flops, nbytes,
                scratch_shapes=list(rows_shapes),
            )(low, a, got_a, labels, x)
            high, res_t, spread, g_other = call(
                next_high_body, (score_shape, *rows_shapes, g_sent_shape), vmem(6), "soft_high", flops // 2, nbytes
            )(high, b, got_b, labels, x, g_other)
            got = swap_core(g_other)
            g_own = call(own_high_body, g_shape, vmem(4), "own", flops // 2, nbytes)(res_t, spread, x, g_own)
        else:
            got = swap_core(g_other)
            g_own = call(own_body, g_shape, vmem(3), "own", flops, nbytes)(res_t, spread, x)
        p, q = call(pair_body, (p_shape, q_shape), vmem(2), "pair")(g_own, got)
        carry = aligned and step < 2
        if carry:
            p, q, send = lax.optimization_barrier((p, q, sends[step]))
        for n, bit in enumerate(z_bits):
            got_p = swap(p, lambda f, e, bit=bit: (f, e ^ bit))
            got_q = swap(q, lambda f, e, bit=bit: (f, e ^ bit))
            if n < len(z_bits) - 1:
                if carry:
                    far = swap(send, lambda f, e: (f, e ^ z_bits[1]))
                p = call(hop_body, p_shape, vmem(2), "hop_p")(p, got_p)
                q = call(hop_body, q_shape, vmem(2), "hop_q")(q, got_q)
        if carry:
            near = swap(jnp.stack([send, far]), lambda f, e: (f, e ^ z_bits[0]))
            old = call(place_body, old_shape, vmem(3), "place")(far, near, blocks[step])
        elif step < 2:
            old = blocks[step]
        sums = (p, got_p, q, got_q)
        if step < STEPS - 1 and aligned:
            following = prep(order, tile_live, x_values, step + 1)
            *sums, following = lax.optimization_barrier((*sums, following))
        elif step < STEPS - 1:
            following = prep_general(x_values, tile_live, order[0, step + 1], core, own)
        if step == 0:
            first, delta = call(
                functools.partial(prox_first_body, count), (old_shape, delta_shape), vmem(5), "prox"
            )(*sums, old)
        else:
            first, other, delta = call(
                functools.partial(prox_body, count), (old_shape, old_shape, delta_shape), vmem(7), "prox"
            )(same[step - 1], *sums, first, old if step == 1 else other)
        got = swap_core(delta)
        part = call(mine_body, part_shape, vmem(2), "mine", flops, nbytes)(x, delta)
        last = step == STEPS - 1
        shapes = (sds(half, BF16),) + (() if last else (sds(half, F32),))
        sent, kept = [], []
        for at in range(2):
            mine = errors[at::2]
            change, *error = call(
                functools.partial(change_body, len(mine), at * (rows // 2)), shapes, vmem(3 + len(mine)),
                "change", flops // 2, nbytes,
            )(x, part, got, *mine)
            sent.append(change)
            kept += error
        a, b = sent
        halves, errors = sum_over_feat(a, b, last)
        errors = kept + errors
    a, got_a, b, got_b = halves
    half = sds((rows // 2, C), F32)
    low = call(last_low_body, half, vmem(3), "last_low", flops // 4, nbytes)(low, a, got_a)
    score = pl.pallas_call(
        last_high_body,
        out_shape=jax.ShapeDtypeStruct((rows, C), F32),
        in_specs=vmem(4),
        out_specs=pl.BlockSpec(memory_space=pltpu.HBM),
        scratch_shapes=[pltpu.VMEM(half.shape, F32), pltpu.SemaphoreType.DMA((2,))],
        name="last_high",
        compiler_params=pltpu.CompilerParams(vmem_limit_bytes=16 << 20),
    )(*(pltpu.with_memory_space_constraint(v, pltpu.VMEM) for v in (low, high, b, got_b)))
    if aligned:
        coef = call(coef_body, sds(coef.shape, F32), smem(1) + vmem(2), "coef_out")(order, first, other)
    else:
        coef = own_blocks((first, other), order, own)
    return score, coef


def solution(mesh):
    return jax.shard_map(
        local,
        mesh=mesh,
        in_specs=(
            P("ex", "feat"),
            P("ex", "feat"),
            P("ex"),
            P("ex", None),
            P(None, ("feat", "ex"), None),
            P(None, "feat"),
        ),
        out_specs=(P("ex", None), P(None, ("feat", "ex"), None)),
        check_vma=False,
    )
```

```python
import functools

import jax
import jax.numpy as jnp
from jax import lax
from jax.experimental import pallas as pl
from jax.experimental.pallas import tpu as pltpu
from jax.sharding import PartitionSpec as P

C = 128
BLOCK = 1024
STEPS = 3
HALF = BLOCK // 2
TILE = 128
NB = HALF // TILE
PB = NB // 2
TAIL = 8

ridge = 0.002
lasso = 0.005

F32 = jnp.float32
BF16 = jnp.bfloat16


def vmem(n):
    return [pl.BlockSpec(memory_space=pltpu.VMEM)] * n


def smem(n):
    return [pl.BlockSpec(memory_space=pltpu.SMEM)] * n


def hbm(n):
    return [pl.BlockSpec(memory_space=pltpu.HBM)] * n


def call(body, outs, in_specs, name, flops=0, nbytes=0, **kw):
    f = pl.pallas_call(
        body,
        out_shape=outs,
        in_specs=in_specs,
        out_specs=jax.tree.map(lambda _: pl.BlockSpec(memory_space=pltpu.VMEM), outs),
        name=name,
        cost_estimate=pl.CostEstimate(flops=flops, bytes_accessed=nbytes, transcendentals=0),
        compiler_params=pltpu.CompilerParams(vmem_limit_bytes=16 << 20),
        **kw,
    )

    def run(*args):
        return f(
            *(
                x
                if spec.memory_space == pltpu.SMEM
                else pltpu.with_memory_space_constraint(x, spec.memory_space)
                for spec, x in zip(in_specs, args, strict=True)
            )
        )

    return run


def sds(shape, dtype):
    return pltpu.VMEM(shape, dtype)


def load_block(chosen, x_ref, buf, sems):
    copies = [
        pltpu.make_async_copy(
            x_ref.at[pl.ds(r * TILE, TILE), pl.ds(pl.multiple_of(chosen * BLOCK, BLOCK), BLOCK)],
            buf.at[pl.ds(r * TILE, TILE)],
            sems.at[r],
        )
        for r in range(buf.shape[0] // TILE)
    ]
    for copy in copies:
        copy.start()
    return copies


def mask_tile(r, chosen, core, live_ref, buf, out_ref, begin=0):
    tiles = BLOCK // TILE
    here = pl.ds(r * TILE, TILE)
    for k in range(tiles):
        col = 2 * (k % NB) + (core if k < NB else 1 - core)
        live = live_ref[r, chosen * tiles + col].astype(F32)
        tile = buf[here, pl.ds(pl.multiple_of(begin + col * TILE, TILE), TILE)]
        out_ref[here, k * TILE : (k + 1) * TILE] = (tile.astype(F32) * live).astype(BF16)


def prep_body(step, order_ref, live_ref, x_ref, out_ref, buf, sems):
    chosen, core = order_ref[0, step], lax.axis_index("ex") % 2
    copies = load_block(chosen, x_ref, buf, sems)
    for r, copy in enumerate(copies):
        copy.wait()
        mask_tile(r, chosen, core, live_ref, buf, out_ref)


def block_scratch(rows):
    return [pltpu.VMEM((rows, BLOCK), BF16), pltpu.SemaphoreType.DMA((rows // TILE,))]


def prep(order, tile_live, x_values, step):
    rows = x_values.shape[0]
    return call(
        functools.partial(prep_body, step),
        sds((rows, BLOCK), BF16),
        smem(2) + hbm(1),
        "prep",
        nbytes=4 * rows * BLOCK,
        scratch_shapes=block_scratch(rows),
    )(order, tile_live, x_values)


def prep_general(x_values, tile_live, chosen, core, own):
    rows = x_values.shape[0]
    tiles = BLOCK // TILE
    x = lax.dynamic_slice_in_dim(x_values, chosen * BLOCK, BLOCK, 1)
    live = lax.dynamic_slice_in_dim(tile_live, chosen * tiles, tiles, 1).astype(BF16)
    x = x.reshape(rows // TILE, TILE, tiles, TILE) * live[:, None, :, None]
    x = x.reshape(rows, HALF // own, 2, own)
    mine = lax.dynamic_index_in_dim(x, core, 2, keepdims=False)
    other = lax.dynamic_index_in_dim(x, 1 - core, 2, keepdims=False)
    return jnp.concatenate([mine.reshape(rows, HALF), other.reshape(rows, HALF)], axis=1)


def stack_rows(rows):
    if len(rows) < TAIL:
        rows = rows + [jnp.zeros((TAIL - len(rows), TILE), F32)]
    return jnp.concatenate(rows, axis=0)


def split_rows(curvs):
    rows = []
    for curv in curvs:
        high = curv.astype(BF16).astype(F32)
        rows += [high, curv - high]
    return stack_rows(rows).astype(BF16)


def block(k):
    return slice(k * C, (k + 1) * C)


def half_sums(res_t, spread_ref, x_ref, start, first, g_ref, so_far=None):
    rows = spread_ref.shape[0]
    grad = jnp.dot(res_t, x_ref[start : start + rows, first : first + HALF], preferred_element_type=F32)
    curvs = []
    for k in range(NB):
        lanes = slice(first + k * TILE, first + (k + 1) * TILE)
        acc = jnp.zeros((8, TILE), F32)
        for r, here in tiles_of(rows):
            x = x_ref[start + r * TILE : start + (r + 1) * TILE, lanes].astype(F32)
            term = x * x * spread_ref[here, :]
            acc = acc + jnp.sum(term.reshape(TILE // 8, 8, TILE), axis=0)
        curv = jnp.sum(acc, axis=0, keepdims=True)
        part = grad[:, k * TILE : (k + 1) * TILE]
        if so_far is not None:
            part, curv = part + so_far[block(k), :], curv + so_far[NB * C + k : NB * C + k + 1, :]
        g_ref[block(k), :] = part.astype(g_ref.dtype)
        curvs.append(curv)
    g_ref[NB * C : NB * C + TAIL, :] = split_rows(curvs) if g_ref.dtype == BF16 else stack_rows(curvs)


def soft_rows(score, labels, here, res_ref, spread_ref):
    top = jnp.max(score, axis=0, keepdims=True)
    expo = jnp.exp(score - top)
    prob = expo / jnp.sum(expo, axis=0, keepdims=True)
    classes = lax.broadcasted_iota(jnp.int32, (C, TILE), 0)
    residual = prob - jnp.where(labels == classes, 1.0, 0.0)
    spread = (1.0 - jnp.sum(prob * prob, axis=0, keepdims=True)).astype(BF16).astype(F32)
    res_ref[:, here] = residual.astype(BF16)
    spread_ref[here, :] = jnp.broadcast_to(spread, (TILE, TILE)).T


def tiles_of(rows):
    return [(r, slice(r * TILE, (r + 1) * TILE)) for r in range(rows // TILE)]


def keep_score(score, r, low_ref, high_ref):
    per = low_ref.shape[1] // TILE
    (low_ref if r < per else high_ref)[:, r % per * TILE : (r % per + 1) * TILE] = score


def first_body(
    order_hbm, live_hbm, margins_hbm, lab_hbm, coef_hbm, x_hbm,
    x_ref, low_ref, high_ref, res_ref, spread_ref, g_ref, first_ref, other_ref, first_send, other_send, *rest,
):
    same_refs = rest[: STEPS - 1]
    order, live, margins, labels, coef, small, buf, sems = rest[STEPS - 1 :]
    loads = [
        pltpu.make_async_copy(src, dst, small.at[i])
        for i, (src, dst) in enumerate(
            ((order_hbm, order), (live_hbm, live), (margins_hbm, margins), (lab_hbm, labels), (coef_hbm, coef))
        )
    ]
    for load in loads:
        load.start()
    copies = [
        pltpu.make_async_copy(
            x_hbm.at[pl.ds(r * TILE, TILE)], buf.at[pl.ds(r * TILE, TILE)], sems.at[r]
        )
        for r in range(buf.shape[0] // TILE)
    ]
    for copy in copies:
        copy.start()
    for load in loads:
        load.wait()
    chosen, core = order[0, 0], lax.axis_index("ex") % 2
    for r, here in tiles_of(margins.shape[0]):
        score = margins[here, :].astype(F32).T
        keep_score(score, r, low_ref, high_ref)
        soft_rows(score, labels[r : r + 1, :], here, res_ref, spread_ref)
    for block, keep, send in ((chosen, first_ref, first_send), (1 - chosen, other_ref, other_send)):
        rows = coef[block].T
        keep[...] = rows
        send[...] = rows.astype(BF16)
    for step, same_ref in enumerate(same_refs):
        same_ref[...] = jnp.full((8, TILE), (order[0, step + 1] == chosen).astype(F32))
    for r, copy in enumerate(copies):
        copy.wait()
        mask_tile(r, chosen, core, live, buf, x_ref, chosen * BLOCK)
    half_sums(res_ref[...], spread_ref, x_ref, 0, HALF, g_ref)


def first_general_body(margins_ref, lab_ref, x_ref, low_ref, high_ref, res_ref, spread_ref, g_ref):
    for r, here in tiles_of(margins_ref.shape[0]):
        score = margins_ref[here, :].astype(F32).T
        keep_score(score, r, low_ref, high_ref)
        soft_rows(score, lab_ref[r : r + 1, :], here, res_ref, spread_ref)
    half_sums(res_ref[...], spread_ref, x_ref, 0, HALF, g_ref)


def next_rows(start, before_ref, part_ref, got_ref, lab_ref, score_ref, res_ref, spread_ref):
    for r, here in tiles_of(before_ref.shape[1]):
        score = before_ref[:, here] + (part_ref[:, here].astype(F32) + got_ref[:, here].astype(F32))
        score_ref[:, here] = score
        row = start // TILE + r
        soft_rows(score, lab_ref[row : row + 1, :], here, res_ref, spread_ref)


def next_low_body(before_ref, part_ref, got_ref, lab_ref, x_ref, score_ref, g_ref, own_ref, res_ref, spread_ref):
    next_rows(0, before_ref, part_ref, got_ref, lab_ref, score_ref, res_ref, spread_ref)
    half_sums(res_ref[...], spread_ref, x_ref, 0, HALF, g_ref)
    half_sums(res_ref[...], spread_ref, x_ref, 0, 0, own_ref)


def next_high_body(before_ref, part_ref, got_ref, lab_ref, x_ref, so_far, score_ref, res_ref, spread_ref, g_ref):
    start = before_ref.shape[1]
    next_rows(start, before_ref, part_ref, got_ref, lab_ref, score_ref, res_ref, spread_ref)
    half_sums(res_ref[...], spread_ref, x_ref, start, HALF, g_ref, so_far)


def last_low_body(before_ref, part_ref, got_ref, out_ref):
    for _, here in tiles_of(before_ref.shape[1]):
        score = before_ref[:, here] + (part_ref[:, here].astype(F32) + got_ref[:, here].astype(F32))
        out_ref[here, :] = score.T


def last_high_body(low_ref, before_ref, part_ref, got_ref, out_hbm, buf, sems):
    rows = before_ref.shape[1]
    copies = [
        pltpu.make_async_copy(ref, out_hbm.at[pl.ds(i * rows, rows)], sems.at[i])
        for i, ref in enumerate((low_ref, buf))
    ]
    copies[0].start()
    last_low_body(before_ref, part_ref, got_ref, buf)
    copies[1].start()
    for copy in copies:
        copy.wait()


def own_body(res_ref, spread_ref, x_ref, g_ref):
    half_sums(res_ref[...], spread_ref, x_ref, 0, 0, g_ref)


def own_high_body(res_ref, spread_ref, x_ref, so_far, g_ref):
    half_sums(res_ref[...], spread_ref, x_ref, spread_ref.shape[0], 0, g_ref, so_far)


def pair_body(own_ref, got_ref, p_ref, q_ref):
    tail = got_ref[NB * C : NB * C + TAIL, :].astype(F32)
    curvs = []
    for k in range(NB):
        total = own_ref[block(k), :] + got_ref[block(k), :].astype(F32)
        ref, j = (p_ref, k) if k < PB else (q_ref, k - PB)
        ref[block(j), :] = total.astype(BF16)
        curvs.append(own_ref[NB * C + k : NB * C + k + 1, :] + tail[2 * k : 2 * k + 1] + tail[2 * k + 1 : 2 * k + 2])
    p_ref[PB * C : PB * C + TAIL, :] = split_rows(curvs[:PB])
    q_ref[(NB - PB) * C : (NB - PB) * C + TAIL, :] = split_rows(curvs[PB:])


def sum_of(mine_ref, got_ref, rows):
    return mine_ref[rows, :].astype(F32) + got_ref[rows, :].astype(F32)


def curvs_of(mine_ref, got_ref):
    n = mine_ref.shape[0] // C
    tail = sum_of(mine_ref, got_ref, slice(n * C, n * C + TAIL))
    return [tail[2 * j : 2 * j + 1] + tail[2 * j + 1 : 2 * j + 2] for j in range(n)]


def hop_body(mine_ref, got_ref, out_ref):
    curvs = curvs_of(mine_ref, got_ref)
    for j in range(len(curvs)):
        out_ref[block(j), :] = sum_of(mine_ref, got_ref, block(j)).astype(BF16)
    out_ref[len(curvs) * C : len(curvs) * C + TAIL, :] = split_rows(curvs)


def place_body(far_ref, near_ref, coef_ref, out_ref):
    place = lax.axis_index("ex") // 2
    out_ref[place] = coef_ref[...]
    out_ref[jnp.bitwise_xor(place, 2)] = far_ref[...].astype(F32)
    out_ref[jnp.bitwise_xor(place, 1)] = near_ref[0].astype(F32)
    out_ref[jnp.bitwise_xor(place, 3)] = near_ref[1].astype(F32)


def totals(p_ref, gp_ref, q_ref, gq_ref):
    both = []
    for pair in ((p_ref, gp_ref), (q_ref, gq_ref)):
        both += [(sum_of(*pair, block(j)), curv) for j, curv in enumerate(curvs_of(*pair))]
    return both


def step_coef(count, grad, curv, old):
    inverse = 1.0 / (curv / count + ridge)
    shifted = old - grad * (inverse / count)
    limit = lasso * inverse
    return shifted - jnp.clip(shifted, -limit, limit)


def prox_first_body(count, p_ref, gp_ref, q_ref, gq_ref, old_ref, new_ref, delta_ref):
    for k, (grad, curv) in enumerate(totals(p_ref, gp_ref, q_ref, gq_ref)):
        old = old_ref[k]
        new = step_coef(count, grad, curv, old)
        new_ref[k] = new
        delta_ref[:, k * TILE : (k + 1) * TILE] = (new - old).astype(BF16)


def prox_body(count, same_ref, p_ref, gp_ref, q_ref, gq_ref, old0_ref, old1_ref, new0_ref, new1_ref, delta_ref):
    same = jnp.broadcast_to(same_ref[0:1, :], (C, TILE)) > 0.5
    for k, (grad, curv) in enumerate(totals(p_ref, gp_ref, q_ref, gq_ref)):
        old0, old1 = old0_ref[k], old1_ref[k]
        old = jnp.where(same, old0, old1)
        new = step_coef(count, grad, curv, old)
        new0_ref[k] = jnp.where(same, new, old0)
        new1_ref[k] = jnp.where(same, old1, new)
        delta_ref[:, k * TILE : (k + 1) * TILE] = (new - old).astype(BF16)


def coef_body(order_ref, first_ref, other_ref, out_ref):
    place = lax.axis_index("ex") // 2
    block = order_ref[0, 0]
    out_ref[block] = first_ref[place].T
    out_ref[1 - block] = other_ref[place].T


def contrib(x_ref, first, delta_ref):
    return lax.dot_general(
        x_ref[:, first : first + HALF], delta_ref[...],
        (((1,), (1,)), ((), ())), preferred_element_type=F32,
    )


def mine_body(x_ref, delta_ref, part_ref):
    part_ref[...] = contrib(x_ref, 0, delta_ref)


def change_body(carried, start, x_ref, part_ref, delta_ref, *refs):
    errors, (out_ref, *keep) = refs[:carried], refs[carried:]
    rows = out_ref.shape[1]
    part = part_ref[start : start + rows, :] + lax.dot_general(
        x_ref[start : start + rows, HALF:], delta_ref[...],
        (((1,), (1,)), ((), ())), preferred_element_type=F32,
    )
    for _, here in tiles_of(rows):
        full = part[here, :].T
        for e_ref in errors:
            full = full + e_ref[:, here]
        sent = full.astype(BF16)
        out_ref[:, here] = sent
        for e_ref in keep:
            e_ref[:, here] = full - sent.astype(F32)


def meet_body(share, mine_ref, got_ref, out_ref, *error_refs):
    total = mine_ref[...].astype(F32) + got_ref[...].astype(F32)
    sent = total.astype(BF16)
    out_ref[...] = sent
    for error_ref in error_refs:
        error_ref[...] = share * (total - sent.astype(F32))


def bits(n):
    return [1 << i for i in range(n.bit_length() - 1)]


def swap(x, move):
    n_feat, n_ex = lax.axis_size("feat"), lax.axis_size("ex")
    pairs = []
    for f in range(n_feat):
        for e in range(n_ex):
            to_f, to_e = move(f, e)
            pairs.append((f * n_ex + e, to_f * n_ex + to_e))
    return lax.ppermute(x, ("feat", "ex"), pairs)


def swap_core(x):
    return swap(x, lambda f, e: (f, e ^ 1))


def sum_over_feat(a, b, last):
    order = bits(lax.axis_size("feat"))
    errors, pair = [], 1
    for n in range(len(order)):
        got_a = swap(a, lambda f, e, n=n: (f ^ order[n], e))
        got_b = swap(b, lambda f, e, n=n: (f ^ order[-1 - n], e))
        if n == len(order) - 1:
            return (a, got_a, b, got_b), errors
        pair *= 2
        shapes = (sds(a.shape, BF16),) + (() if last else (sds(a.shape, F32),))
        meet = functools.partial(meet_body, 1.0 / pair)
        a, *ea = call(meet, shapes, vmem(2), "meet_a")(a, got_a)
        b, *eb = call(meet, shapes, vmem(2), "meet_b")(b, got_b)
        errors += ea + eb


def gather_blocks(coef, order, z_bits):
    n_z = 1 << len(z_bits)
    far = jnp.swapaxes(coef, 1, 2)[:, None]
    for bit in z_bits:
        far = jnp.concatenate([far, swap(far, lambda f, e, bit=bit: (f, e ^ bit))], axis=1)
    place = lax.axis_index("ex") // 2
    far = jnp.take(far, jnp.bitwise_xor(jnp.arange(n_z), place), axis=1)
    old = far.transpose(0, 2, 1, 3).reshape(2, C, NB, TILE).transpose(0, 2, 1, 3)
    block = order[0, 0]
    return [lax.dynamic_index_in_dim(old, i, 0, keepdims=False) for i in (block, 1 - block)]


def own_blocks(olds, order, own):
    place = lax.axis_index("ex") // 2
    rows = []
    for old in olds:
        old = old.transpose(1, 0, 2).reshape(C, HALF)
        rows.append(lax.dynamic_slice_in_dim(old, place * own, own, 1))
    first = order[0, 0] == 0
    both = [jnp.where(first, rows[0], rows[1]), jnp.where(first, rows[1], rows[0])]
    return jnp.swapaxes(jnp.stack(both), 1, 2)


def local(x_values, tile_live, labels, margins, coef, order):
    rows = x_values.shape[0]
    n_ex = lax.axis_size("ex")
    count = float(rows * n_ex)
    own = coef.shape[1]
    core = lax.axis_index("ex") % 2
    aligned = own == TILE and n_ex == 2 * NB
    labels = labels.reshape(rows // TILE, TILE)
    order = order.reshape(1, STEPS)
    z_bits = [2 * b for b in bits(n_ex // 2)]

    x_shape = sds((rows, BLOCK), BF16)
    soft_shapes = (
        sds((C, rows // 2), F32), sds((C, rows // 2), F32),
        sds((C, rows), BF16), sds((rows, TILE), F32), sds((NB * C + TAIL, TILE), BF16),
    )
    g_shape = sds((NB * C + TAIL, TILE), F32)
    score_shape, g_sent_shape = soft_shapes[0], soft_shapes[-1]
    rows_shapes = (sds((C, rows // 2), BF16), sds((rows // 2, TILE), F32))
    old_shape, delta_shape = sds((NB, C, TILE), F32), sds((C, HALF), BF16)
    part_shape, half = sds((rows, C), F32), (C, rows // 2)
    own_shape, send_shape, same_shape = sds((C, TILE), F32), sds((C, TILE), BF16), sds((8, TILE), F32)
    flops, nbytes = 2 * rows * HALF * C, 1 << 20

    p_shape, q_shape = sds((PB * C + TAIL, TILE), BF16), sds(((NB - PB) * C + TAIL, TILE), BF16)

    if aligned:
        x, low, high, res_t, spread, g_other, *rest = call(
            first_body,
            (x_shape,) + soft_shapes + (own_shape,) * 2 + (send_shape,) * 2 + (same_shape,) * (STEPS - 1),
            hbm(6), "soft_first", flops, nbytes,
            scratch_shapes=[
                pltpu.SMEM(order.shape, jnp.int32),
                pltpu.SMEM(tile_live.shape, jnp.int32),
                pltpu.VMEM(margins.shape, BF16),
                pltpu.VMEM(labels.shape, jnp.int32),
                pltpu.VMEM(coef.shape, F32),
                pltpu.SemaphoreType.DMA((5,)),
                pltpu.VMEM(x_values.shape, BF16),
                pltpu.SemaphoreType.DMA((rows // TILE,)),
            ],
        )(order, tile_live, margins, labels, coef, x_values)
        blocks, sends, same = rest[:2], rest[2:4], rest[4:]
    else:
        x = prep_general(x_values, tile_live, order[0, 0], core, own)
        low, high, res_t, spread, g_other = call(
            first_general_body, soft_shapes, vmem(3), "soft_first", flops, nbytes
        )(margins, labels, x)
        blocks = gather_blocks(coef, order, z_bits)
        same = [
            jnp.full((8, TILE), (order[0, step] == order[0, 0]).astype(F32)) for step in range(1, STEPS)
        ]

    errors = []
    for step in range(STEPS):
        if step > 0:
            x = following
            a, got_a, b, got_b = halves
            low, g_other, g_own = call(
                next_low_body, (score_shape, g_shape, g_shape), vmem(5), "soft_low", flops, nbytes,
                scratch_shapes=list(rows_shapes),
            )(low, a, got_a, labels, x)
            high, res_t, spread, g_other = call(
                next_high_body, (score_shape, *rows_shapes, g_sent_shape), vmem(6), "soft_high", flops // 2, nbytes
            )(high, b, got_b, labels, x, g_other)
            got = swap_core(g_other)
            g_own = call(own_high_body, g_shape, vmem(4), "own", flops // 2, nbytes)(res_t, spread, x, g_own)
        else:
            got = swap_core(g_other)
            g_own = call(own_body, g_shape, vmem(3), "own", flops, nbytes)(res_t, spread, x)
        p, q = call(pair_body, (p_shape, q_shape), vmem(2), "pair")(g_own, got)
        carry = aligned and step < 2
        if carry:
            p, q, send = lax.optimization_barrier((p, q, sends[step]))
        for n, bit in enumerate(z_bits):
            got_p = swap(p, lambda f, e, bit=bit: (f, e ^ bit))
            got_q = swap(q, lambda f, e, bit=bit: (f, e ^ bit))
            if n < len(z_bits) - 1:
                if carry:
                    far = swap(send, lambda f, e: (f, e ^ z_bits[1]))
                p = call(hop_body, p_shape, vmem(2), "hop_p")(p, got_p)
                q = call(hop_body, q_shape, vmem(2), "hop_q")(q, got_q)
        if carry:
            near = swap(jnp.stack([send, far]), lambda f, e: (f, e ^ z_bits[0]))
            old = call(place_body, old_shape, vmem(3), "place")(far, near, blocks[step])
        elif step < 2:
            old = blocks[step]
        sums = (p, got_p, q, got_q)
        if step < STEPS - 1 and aligned:
            following = prep(order, tile_live, x_values, step + 1)
            *sums, following = lax.optimization_barrier((*sums, following))
        elif step < STEPS - 1:
            following = prep_general(x_values, tile_live, order[0, step + 1], core, own)
        if step == 0:
            first, delta = call(
                functools.partial(prox_first_body, count), (old_shape, delta_shape), vmem(5), "prox"
            )(*sums, old)
        else:
            first, other, delta = call(
                functools.partial(prox_body, count), (old_shape, old_shape, delta_shape), vmem(7), "prox"
            )(same[step - 1], *sums, first, old if step == 1 else other)
        got = swap_core(delta)
        part = call(mine_body, part_shape, vmem(2), "mine", flops, nbytes)(x, delta)
        last = step == STEPS - 1
        shapes = (sds(half, BF16),) + (() if last else (sds(half, F32),))
        sent, kept = [], []
        for at in range(2):
            mine = errors[at::2]
            change, *error = call(
                functools.partial(change_body, len(mine), at * (rows // 2)), shapes, vmem(3 + len(mine)),
                "change", flops // 2, nbytes,
            )(x, part, got, *mine)
            sent.append(change)
            kept += error
        a, b = sent
        halves, errors = sum_over_feat(a, b, last)
        errors = kept + errors
    a, got_a, b, got_b = halves
    half = sds((rows // 2, C), F32)
    low = call(last_low_body, half, vmem(3), "last_low", flops // 4, nbytes)(low, a, got_a)
    score = pl.pallas_call(
        last_high_body,
        out_shape=jax.ShapeDtypeStruct((rows, C), F32),
        in_specs=vmem(4),
        out_specs=pl.BlockSpec(memory_space=pltpu.HBM),
        scratch_shapes=[pltpu.VMEM(half.shape, F32), pltpu.SemaphoreType.DMA((2,))],
        name="last_high",
        compiler_params=pltpu.CompilerParams(vmem_limit_bytes=16 << 20),
    )(*(pltpu.with_memory_space_constraint(v, pltpu.VMEM) for v in (low, high, b, got_b)))
    if aligned:
        coef = call(coef_body, sds(coef.shape, F32), smem(1) + vmem(2), "coef_out")(order, first, other)
    else:
        coef = own_blocks((first, other), order, own)
    return score, coef


def solution(mesh):
    return jax.shard_map(
        local,
        mesh=mesh,
        in_specs=(
            P("ex", "feat"),
            P("ex", "feat"),
            P("ex"),
            P("ex", None),
            P(None, ("feat", "ex"), None),
            P(None, "feat"),
        ),
        out_specs=(P("ex", None), P(None, ("feat", "ex"), None)),
        check_vma=False,
    )
```
